32 devices in a mesh: dp: 4 (over z), fsdp: 8 (over y, x, core).
Axes of the slice: x: 2, y: 2, z: 4, core: 2. Of those that a mesh axis runs over, the one named last changes fastest.
Arguments:
- dec_in: bfloat16 [64, 176, 768], P(('dp', 'fsdp')), may hold values from -6 to 6
- enc_out: bfloat16 [64, 512, 768], P(('dp', 'fsdp')), may hold values from -6 to 6
- seg_dec: int32 [64, 176], P(('dp', 'fsdp')), may hold values from 0 to 4, as said below
- seg_enc: int32 [64, 512], P(('dp', 'fsdp')), may hold values from 0 to 4, as said below
- out_grad: bfloat16 [64, 176, 768], P(('dp', 'fsdp')), may hold values from -6 to 6
- gain_self: bfloat16 [768], P('fsdp'), may hold values from 0.099609375 to 1.8984375
- wq_self: bfloat16 [768, 768], P('fsdp'), may hold values from -0.21875 to 0.21875
- wk_self: bfloat16 [768, 768], P('fsdp'), may hold values from -0.21875 to 0.21875
- wv_self: bfloat16 [768, 768], P('fsdp'), may hold values from -0.21875 to 0.21875
- wo_self: bfloat16 [768, 768], P('fsdp'), may hold values from -1.5 to 1.5
- gain_cross: bfloat16 [768], P('fsdp'), may hold values from 0.099609375 to 1.8984375
- wq_cross: bfloat16 [768, 768], P('fsdp'), may hold values from -0.21875 to 0.21875
- wk_cross: bfloat16 [768, 768], P('fsdp'), may hold values from -0.21875 to 0.21875
- wv_cross: bfloat16 [768, 768], P('fsdp'), may hold values from -0.21875 to 0.21875
- wo_cross: bfloat16 [768, 768], P('fsdp'), may hold values from -2.5 to 2.5
- gain_ffn: bfloat16 [768], P('fsdp'), may hold values from 0.099609375 to 1.8984375
- w_gate: bfloat16 [768, 2048], P('fsdp'), may hold values from -0.21875 to 0.21875
- w_up: bfloat16 [768, 2048], P('fsdp'), may hold values from -0.21875 to 0.21875
- w_down: bfloat16 [2048, 768], P('fsdp'), may hold values from -0.125 to 0.125
Outputs:
- dec_out: bfloat16 [64, 176, 768], P(('dp', 'fsdp'))
- grad_dec: float32 [64, 176, 768], P(('dp', 'fsdp'))
- grad_enc: float32 [64, 512, 768], P(('dp', 'fsdp'))
- grad_gain_self: float32 [768], P('fsdp')
- grad_wq_self: float32 [768, 768], P('fsdp')
- grad_wk_self: float32 [768, 768], P('fsdp')
- grad_wv_self: float32 [768, 768], P('fsdp')
- grad_wo_self: float32 [768, 768], P('fsdp')
- grad_gain_cross: float32 [768], P('fsdp')
- grad_wq_cross: float32 [768, 768], P('fsdp')
- grad_wk_cross: float32 [768, 768], P('fsdp')
- grad_wv_cross: float32 [768, 768], P('fsdp')
- grad_wo_cross: float32 [768, 768], P('fsdp')
- grad_gain_ffn: float32 [768], P('fsdp')
- grad_w_gate: float32 [768, 2048], P('fsdp')
- grad_w_up: float32 [768, 2048], P('fsdp')
- grad_w_down: float32 [2048, 768], P('fsdp')
The draws below stay inside these ranges and needn't reach their ends.
Inputs may be any that keep to these rules, and one draw needn't show every extreme that they name: `seg_dec`: each row holds segments 1, 2, 3, 4 in this order, each present in both its decoder and its encoder tokens, then 1 to 176 // 16 (decoder) or 512 // 16 (encoder) padding tokens of segment 0 at its end. `seg_enc`: as for seg_dec, with the same segments present.
All inputs are finite; a program needn't handle non-finite values.
Results may differ from the reference program's by a relative error of at most 0.023.
Values may be sent and summed in bfloat16 or wider, within the bound.
A program may use at most 192 MiB of HBM per device.

```python
import jax
import jax.numpy as jnp
from jax import lax

D = 768
HD = 64
FF = 2048
INNER = 768
LD = 176
LE = 512
ROWS = 64


def segment_layout(key, length):
    quarter = length // 4
    reach_max = quarter // 4
    jitter = jax.random.randint(key, (ROWS, 3), -reach_max, reach_max + 1)
    cut_points = jnp.arange(1, 4, dtype=jnp.int32)[None, :] * quarter + jitter
    pad_count = jax.random.randint(jax.random.fold_in(key, 7), (ROWS, 1), 1, reach_max + 1)
    position = jnp.arange(length, dtype=jnp.int32)
    segment = 1 + jnp.sum((position[None, :, None] >= cut_points[:, None, :]).astype(jnp.int32), axis=-1)
    return jnp.where(position[None, :] >= length - pad_count, 0, segment).astype(jnp.int32)


def draw_seg_dec(key, part):
    return segment_layout(jax.random.fold_in(key, 11), LD)


def draw_seg_enc(key, part):
    return segment_layout(jax.random.fold_in(key, 23), LE)


def strengthened(drawn, key, source, target, shards_of, factor):
    def block_of(axis_at):
        return (jnp.arange(drawn.shape[axis_at]) // (drawn.shape[axis_at] // shards_of)).reshape((-1,) + (1,) * (drawn.ndim - 1 - axis_at))

    one_side = jax.random.permutation(key, shards_of)[block_of(target)]
    other_side = (block_of(target) + shards_of // 2) % shards_of
    return jnp.where((block_of(source) == one_side) | (block_of(source) == other_side), factor * drawn, drawn)


def block_levels(own_key, extent, cuts, least, top_value):
    def one(dim, blocks):
        draws = jax.random.uniform(jax.random.fold_in(jax.random.fold_in(own_key, 6), dim), (blocks,), jnp.float32, least / len(cuts), top_value / len(cuts))
        return jnp.repeat(jnp.exp(draws), extent[dim] // blocks).reshape((-1,) + (1,) * (len(extent) - dim - 1))

    level = one(*cuts[0])
    for cut in cuts[1:]:
        level = level * one(*cut)
    return level


def normal_values(stream_key, dims, scale, bound, split=(), kind=jnp.bfloat16):
    entries = jax.random.normal(stream_key, dims, jnp.float32) * scale
    if len(split) > 0:
        entries = block_levels(stream_key, dims, split, -0.22, 0.18) * entries
    return jnp.clip(entries, min=-bound, max=bound).astype(kind)


def gaussian_with(stream_key, dims, deviation, reach, shards, heavy, kind=jnp.bfloat16):
    values = deviation * jax.random.normal(stream_key, dims, jnp.float32)
    if shards:
        values = values * block_levels(stream_key, dims, shards, -0.22, 0.18)
    return jnp.clip(strengthened(values, jax.random.fold_in(stream_key, 3), *heavy), -reach, reach).astype(kind)


def setup_inputs(seed: int = 0) -> dict:
    key_of = jax.random.split(jax.random.key(seed), 20)
    dec_in = normal_values(key_of[0], (ROWS, LD, D), 1.0, 6.0, ((0, 32),))
    enc_out = normal_values(key_of[1], (ROWS, LE, D), 1.0, 6.0, ((0, 32),))
    seg_dec = draw_seg_dec(jax.random.fold_in(key_of[19], 71), 0)
    seg_enc = draw_seg_enc(jax.random.fold_in(key_of[19], 71), 0)
    out_grad = gaussian_with(key_of[4], (ROWS, LD, D), 1.0, 6.0, ((0, 32),), (0, 2, 32, 2.75))
    gain_self = jnp.clip(1.0 + 0.18 * jax.random.normal(key_of[5], (D,), jnp.float32), 0.099609375, 1.8984375).astype(jnp.bfloat16)
    wq_self = normal_values(key_of[6], (D, INNER), D ** -0.5, 0.21875, ((0, 8),))
    wk_self = normal_values(key_of[7], (D, INNER), D ** -0.5, 0.21875, ((0, 8),))
    wv_self = normal_values(key_of[8], (D, INNER), D ** -0.5, 0.21875, ((0, 8),))
    wo_self = normal_values(key_of[9], (INNER, D), (INNER * 4 // LD) ** -0.5, 1.5, ((0, 8),))
    gain_cross = jnp.clip(1.0 + 0.18 * jax.random.normal(key_of[10], (D,), jnp.float32), 0.099609375, 1.8984375).astype(jnp.bfloat16)
    wq_cross = normal_values(key_of[11], (D, INNER), D ** -0.5, 0.21875, ((0, 8),))
    wk_cross = normal_values(key_of[12], (D, INNER), D ** -0.5, 0.21875, ((0, 8),))
    wv_cross = normal_values(key_of[13], (D, INNER), D ** -0.5, 0.21875, ((0, 8),))
    wo_cross = normal_values(key_of[14], (INNER, D), (INNER * 4 // LE) ** -0.5, 2.5, ((0, 8),))
    gain_ffn = jnp.clip(1.0 + 0.18 * jax.random.normal(key_of[15], (D,), jnp.float32), 0.099609375, 1.8984375).astype(jnp.bfloat16)
    w_gate = normal_values(key_of[16], (D, FF), D ** -0.5, 0.21875, ((0, 8),))
    w_up = normal_values(key_of[17], (D, FF), D ** -0.5, 0.21875, ((0, 8),))
    w_down = normal_values(key_of[18], (FF, D), FF ** -0.5, 0.125, ((0, 8),))
    return dict(dec_in=dec_in, enc_out=enc_out, seg_dec=seg_dec, seg_enc=seg_enc, out_grad=out_grad, gain_self=gain_self, wq_self=wq_self, wk_self=wk_self, wv_self=wv_self, wo_self=wo_self, gain_cross=gain_cross, wq_cross=wq_cross, wk_cross=wk_cross, wv_cross=wv_cross, wo_cross=wo_cross, gain_ffn=gain_ffn, w_gate=w_gate, w_up=w_up, w_down=w_down)


@jax.custom_vjp
def low(v):
    return lax.optimization_barrier(v.astype(jnp.bfloat16)).astype(jnp.float32)

@jax.custom_vjp
def low_back(v):
    return v

def low_keep(v):
    return (low(v), None)

def low_pass(kept, grad):
    return (grad,)

def back_keep(v):
    return (v, None)

def back_low(kept, grad):
    return (low(grad),)
low.defvjp(low_keep, low_pass)
low_back.defvjp(back_keep, back_low)
EPSILON = 1e-06
MASKED = -1000000000.0

def matmul(left, right):
    return jnp.dot(left, right, precision=lax.Precision.HIGHEST)

def rms_norm(values_in, gain_vec):
    return values_in * lax.rsqrt(lax.optimization_barrier(jnp.mean(values_in * values_in, axis=-1, keepdims=True)) + EPSILON) * gain_vec

def attend(queries, keys_all, values, allowed):
    q_heads = queries.reshape(queries.shape[0], -1, HD)
    k_heads = keys_all.reshape(keys_all.shape[0], -1, HD)
    v_heads = values.reshape(values.shape[0], -1, HD)
    scores = jnp.einsum('qhd,khd->hqk', q_heads, k_heads, precision=lax.Precision.HIGHEST) * HD ** (-0.5)
    scores = jnp.where(allowed[None], low_back(scores), MASKED)
    probability = low(jax.nn.softmax(scores, axis=-1))
    mixture = jnp.einsum('hqk,khd->qhd', probability, v_heads, precision=lax.Precision.HIGHEST)
    return low(low_back(mixture.reshape(queries.shape[0], -1)))

def decoder_layer(weights, dec_value, enc_value, seg_row_dec, seg_row_enc):
    gain_a, wq_a, wk_a, wv_a, wo_a, gain_c, wq_c, wk_c, wv_c, wo_c, gain_f, gate_w, up_w, down_w = weights
    position = jnp.arange(dec_value.shape[0])
    self_ok = (seg_row_dec[:, None] == seg_row_dec[None, :]) & (position[:, None] >= position[None, :])
    cross_ok = seg_row_dec[:, None] == seg_row_enc[None, :]
    normed = low(rms_norm(dec_value, gain_a))
    queries = low(low_back(matmul(normed, wq_a)))
    keys_all = low(low_back(matmul(normed, wk_a)))
    values = low(low_back(matmul(normed, wv_a)))
    after_self = dec_value + low_back(matmul(attend(queries, keys_all, values, self_ok), wo_a))
    normed = low(rms_norm(after_self, gain_c))
    queries = low(low_back(matmul(normed, wq_c)))
    keys_all = low(low_back(matmul(enc_value, wk_c)))
    values = low(low_back(matmul(enc_value, wv_c)))
    after_cross = after_self + low_back(matmul(attend(queries, keys_all, values, cross_ok), wo_c))
    normed = low(rms_norm(after_cross, gain_f))
    gate_pre = low_back(matmul(normed, gate_w))
    up_pre = low_back(matmul(normed, up_w))
    hidden = low(jax.nn.gelu(gate_pre, approximate=True) * up_pre)
    return after_cross + low_back(matmul(hidden, down_w))

def reference(dec_in, enc_out, seg_dec, seg_enc, out_grad, gain_self, wq_self, wk_self, wv_self, wo_self, gain_cross, wq_cross, wk_cross, wv_cross, wo_cross, gain_ffn, w_gate, w_up, w_down):
    params = tuple((weight.astype(jnp.float32) for weight in (gain_self, wq_self, wk_self, wv_self, wo_self, gain_cross, wq_cross, wk_cross, wv_cross, wo_cross, gain_ffn, w_gate, w_up, w_down)))

    def row_terms(dec_row, enc_row, seg_row_dec, seg_row_enc, cot_row):

        def forward(weights, dec_value, enc_value):
            return decoder_layer(weights, dec_value, enc_value, seg_row_dec, seg_row_enc)
        result, pullback = jax.vjp(forward, params, dec_row.astype(jnp.float32), enc_row.astype(jnp.float32))
        weight_grads, grad_row_dec, grad_row_enc = pullback(cot_row.astype(jnp.float32))
        return (result.astype(jnp.bfloat16), grad_row_dec, grad_row_enc, weight_grads)

    def scan_step(running, batch_rows):
        result, grad_row_dec, grad_row_enc, weight_grads = jax.vmap(row_terms)(*batch_rows)
        running = tuple((accumulated + lax.optimization_barrier(jnp.sum(contribution, axis=0)) for accumulated, contribution in zip(running, weight_grads)))
        return (running, (result, grad_row_dec, grad_row_enc))
    group_rows = 8
    grouped = tuple((source.reshape((-1, group_rows) + source.shape[1:]) for source in (dec_in, enc_out, seg_dec, seg_enc, out_grad)))
    initial = tuple((jnp.zeros(weight.shape, jnp.float32) for weight in params))
    summed, (outputs, grads_dec, grads_enc) = lax.scan(scan_step, initial, grouped)
    dec_out = outputs.reshape(dec_in.shape)
    grad_dec = grads_dec.reshape(dec_in.shape)
    grad_enc = grads_enc.reshape(enc_out.shape)
    return (dec_out, grad_dec, grad_enc, summed[0], summed[1], summed[2], summed[3], summed[4], summed[5], summed[6], summed[7], summed[8], summed[9], summed[10], summed[11], summed[12], summed[13])
```

```python
import jax
import jax.numpy as jnp
from jax import lax
from jax.sharding import PartitionSpec as P

HD = 64


EPSILON = 1e-06
MASKED = -1000000000.0


def rms_forward(values_in, gain_vec):
    return (
        values_in
        * lax.rsqrt(jnp.mean(values_in * values_in, axis=-1, keepdims=True) + EPSILON)
        * gain_vec
    )


def rms_backward(values_in, gain_low, grad_out):
    _, pullback = jax.vjp(rms_forward, values_in, gain_low.astype(jnp.float32))
    return pullback(grad_out)


def project(acts, weight):
    return jnp.einsum("rld,dn->rln", acts, weight, preferred_element_type=jnp.float32)


def weight_grad(acts, grad_out):
    return jnp.einsum("rld,rln->dn", acts, grad_out, preferred_element_type=jnp.float32)


def input_grad(grad_out, weight):
    return jnp.einsum("rln,dn->rld", grad_out, weight, preferred_element_type=jnp.float32)


def split_heads(tensor):
    return tensor.reshape(tensor.shape[0], tensor.shape[1], -1, HD)


def merge_heads(tensor):
    return tensor.reshape(tensor.shape[0], tensor.shape[1], -1)


def masked_scores(queries, keys_all, allowed):
    raw_scores = jnp.einsum(
        "rqhd,rkhd->rhqk",
        split_heads(queries),
        split_heads(keys_all),
        preferred_element_type=jnp.float32,
    ) * HD ** (-0.5)
    return jnp.where(allowed[:, None], raw_scores, MASKED)


def attend_forward(queries, keys_all, values, allowed):
    scores = masked_scores(queries, keys_all, allowed)
    maxima = jnp.max(scores, axis=-1, keepdims=True)
    log_total = maxima + jnp.log(jnp.sum(jnp.exp(scores - maxima), axis=-1, keepdims=True))
    weights_low = jnp.exp(scores - log_total).astype(jnp.bfloat16)
    mixture = jnp.einsum(
        "rhqk,rkhd->rqhd", weights_low, split_heads(values), preferred_element_type=jnp.float32
    )
    return (merge_heads(mixture).astype(jnp.bfloat16), log_total)


def attend_backward(queries, keys_all, values, allowed, log_total, grad_mix):
    scores = masked_scores(queries, keys_all, allowed)
    weights_full = jnp.exp(scores - log_total)
    grad_heads = split_heads(grad_mix)
    grad_values = jnp.einsum(
        "rhqk,rqhd->rkhd",
        weights_full.astype(jnp.bfloat16),
        grad_heads,
        preferred_element_type=jnp.float32,
    )
    grad_weights = jnp.einsum(
        "rqhd,rkhd->rhqk", grad_heads, split_heads(values), preferred_element_type=jnp.float32
    )
    grad_scores = (
        weights_full * (grad_weights - jnp.sum(weights_full * grad_weights, axis=-1, keepdims=True))
    ).astype(jnp.bfloat16)
    grad_queries = jnp.einsum(
        "rhqk,rkhd->rqhd", grad_scores, split_heads(keys_all), preferred_element_type=jnp.float32
    ) * HD ** (-0.5)
    grad_keys = jnp.einsum(
        "rhqk,rqhd->rkhd", grad_scores, split_heads(queries), preferred_element_type=jnp.float32
    ) * HD ** (-0.5)
    return (
        merge_heads(grad_queries).astype(jnp.bfloat16),
        merge_heads(grad_keys).astype(jnp.bfloat16),
        merge_heads(grad_values).astype(jnp.bfloat16),
    )


def gather_group(shards):
    joined = jnp.concatenate(shards, axis=0)
    whole = lax.all_gather(joined, "fsdp", axis=0, tiled=False)
    parts = []
    start = 0
    for shard in shards:
        part = whole[:, start : start + shard.shape[0]]
        parts.append(part.reshape((-1,) + shard.shape[1:]))
        start += shard.shape[0]
    return parts


def reduce_group(gradients, shards):
    count = lax.axis_size("fsdp")
    joined = jnp.concatenate(
        [
            gradient.astype(jnp.bfloat16).reshape((count, -1) + gradient.shape[1:])
            for gradient in gradients
        ],
        axis=1,
    )
    owned = lax.psum_scatter(joined, "fsdp", scatter_dimension=0, tiled=False)
    quarter = lax.psum_scatter(owned, "dp", scatter_dimension=0, tiled=True)
    summed = lax.all_gather(quarter, "dp", axis=0, tiled=True)
    parts = []
    start = 0
    for shard in shards:
        part = summed[start : start + shard.shape[0]]
        parts.append(part.astype(jnp.float32))
        start += shard.shape[0]
    return parts


def micro_step(
    dec_rows, enc_rows, seg_rows_dec, seg_rows_enc, grad_rows, get_self, get_cross, get_ffn
):
    position = jnp.arange(seg_rows_dec.shape[1])
    causal = position[:, None] >= position[None, :]
    self_ok = (seg_rows_dec[:, :, None] == seg_rows_dec[:, None, :]) & causal[None]
    cross_ok = seg_rows_dec[:, :, None] == seg_rows_enc[:, None, :]
    gain_a, wq_a, wk_a, wv_a, wo_a = get_self()
    dec_float = dec_rows.astype(jnp.float32)
    normed_a = rms_forward(dec_float, gain_a.astype(jnp.float32)).astype(jnp.bfloat16)
    query_a = project(normed_a, wq_a).astype(jnp.bfloat16)
    keys_a = project(normed_a, wk_a).astype(jnp.bfloat16)
    values_a = project(normed_a, wv_a).astype(jnp.bfloat16)
    mix_a, total_a = attend_forward(query_a, keys_a, values_a, self_ok)
    after_self = dec_float + project(mix_a, wo_a)
    gain_c, wq_c, wk_c, wv_c, wo_c = get_cross()
    normed_c = rms_forward(after_self, gain_c.astype(jnp.float32)).astype(jnp.bfloat16)
    query_c = project(normed_c, wq_c).astype(jnp.bfloat16)
    keys_c = project(enc_rows, wk_c).astype(jnp.bfloat16)
    values_c = project(enc_rows, wv_c).astype(jnp.bfloat16)
    mix_c, total_c = attend_forward(query_c, keys_c, values_c, cross_ok)
    after_cross = after_self + project(mix_c, wo_c)
    gain_f, gate_w, up_w, down_w = get_ffn()
    normed_f = rms_forward(after_cross, gain_f.astype(jnp.float32)).astype(jnp.bfloat16)
    gate_pre = project(normed_f, gate_w)
    up_pre = project(normed_f, up_w)
    hidden_low = (jax.nn.gelu(gate_pre, approximate=True) * up_pre).astype(jnp.bfloat16)
    dec_result = (after_cross + project(hidden_low, down_w)).astype(jnp.bfloat16)
    gain_f, gate_w, up_w, down_w = get_ffn()
    grad_res = grad_rows.astype(jnp.float32)
    grad_branch = grad_res.astype(jnp.bfloat16)
    grad_down = weight_grad(hidden_low, grad_branch)
    grad_hidden = input_grad(grad_branch, down_w)
    _, gelu_pull = jax.vjp(
        lambda gate_in, up_in: jax.nn.gelu(gate_in, approximate=True) * up_in, gate_pre, up_pre
    )
    grad_gate_pre, grad_up_pre = gelu_pull(grad_hidden)
    grad_gate_low = grad_gate_pre.astype(jnp.bfloat16)
    grad_up_low = grad_up_pre.astype(jnp.bfloat16)
    grad_gate = weight_grad(normed_f, grad_gate_low)
    grad_up = weight_grad(normed_f, grad_up_low)
    grad_normed = input_grad(grad_gate_low, gate_w) + input_grad(grad_up_low, up_w)
    grad_input, grad_gain_f = rms_backward(after_cross, gain_f, grad_normed)
    grad_res = grad_res + grad_input
    gain_c, wq_c, wk_c, wv_c, wo_c = get_cross()
    grad_branch = grad_res.astype(jnp.bfloat16)
    grad_wo_c = weight_grad(mix_c, grad_branch)
    grad_mix = input_grad(grad_branch, wo_c).astype(jnp.bfloat16)
    grad_query, grad_keys, grad_values = attend_backward(
        query_c, keys_c, values_c, cross_ok, total_c, grad_mix
    )
    grad_wq_c = weight_grad(normed_c, grad_query)
    grad_wk_c = weight_grad(enc_rows, grad_keys)
    grad_wv_c = weight_grad(enc_rows, grad_values)
    grad_enc_rows = input_grad(grad_keys, wk_c) + input_grad(grad_values, wv_c)
    grad_normed = input_grad(grad_query, wq_c)
    grad_input, grad_gain_c = rms_backward(after_self, gain_c, grad_normed)
    grad_res = grad_res + grad_input
    gain_a, wq_a, wk_a, wv_a, wo_a = get_self()
    grad_branch = grad_res.astype(jnp.bfloat16)
    grad_wo_a = weight_grad(mix_a, grad_branch)
    grad_mix = input_grad(grad_branch, wo_a).astype(jnp.bfloat16)
    grad_query, grad_keys, grad_values = attend_backward(
        query_a, keys_a, values_a, self_ok, total_a, grad_mix
    )
    grad_wq_a = weight_grad(normed_a, grad_query)
    grad_wk_a = weight_grad(normed_a, grad_keys)
    grad_wv_a = weight_grad(normed_a, grad_values)
    grad_normed = (
        input_grad(grad_query, wq_a) + input_grad(grad_keys, wk_a) + input_grad(grad_values, wv_a)
    )
    grad_input, grad_gain_a = rms_backward(dec_float, gain_a, grad_normed)
    grad_dec_rows = grad_res + grad_input
    full_grads = (
        grad_gain_a,
        grad_wq_a,
        grad_wk_a,
        grad_wv_a,
        grad_wo_a,
        grad_gain_c,
        grad_wq_c,
        grad_wk_c,
        grad_wv_c,
        grad_wo_c,
        grad_gain_f,
        grad_gate,
        grad_up,
        grad_down,
    )
    return (dec_result, grad_dec_rows, grad_enc_rows, full_grads)


def body(
    dec_in,
    enc_out,
    seg_dec,
    seg_enc,
    out_grad,
    gain_self,
    wq_self,
    wk_self,
    wv_self,
    wo_self,
    gain_cross,
    wq_cross,
    wk_cross,
    wv_cross,
    wo_cross,
    gain_ffn,
    w_gate,
    w_up,
    w_down,
):
    narrow = (wq_self, wk_self, wv_self, wo_self, wq_cross, wk_cross, wv_cross, wo_cross, w_down)
    gain_a, gain_c, gain_f = gather_group((gain_self, gain_cross, gain_ffn))
    full = gather_group(narrow)
    gate_full, up_full = gather_group((w_gate, w_up))
    get_self = lambda: (gain_a, *full[0:4])
    get_cross = lambda: (gain_c, *full[4:8])
    get_ffn = lambda: (gain_f, gate_full, up_full, full[8])
    result_rows, grad_rows_dec, grad_rows_enc, grads = micro_step(
        dec_in, enc_out, seg_dec, seg_enc, out_grad, get_self, get_cross, get_ffn
    )
    gains = reduce_group((grads[0], grads[5], grads[10]), (gain_self, gain_cross, gain_ffn))
    wide = reduce_group(grads[11:13], (w_gate, w_up))
    thin = reduce_group(grads[1:5] + grads[6:10] + grads[13:14], narrow)
    return (
        (result_rows, grad_rows_dec, grad_rows_enc, gains[0])
        + tuple(thin[0:4])
        + (gains[1],)
        + tuple(thin[4:8])
        + (gains[2], *wide, thin[8])
    )


def solution(mesh):
    placed = (
        P(("dp", "fsdp"), None, None),
        P(("dp", "fsdp"), None, None),
        P(("dp", "fsdp"), None),
        P(("dp", "fsdp"), None),
        P(("dp", "fsdp"), None, None),
        P("fsdp"),
        P("fsdp", None),
        P("fsdp", None),
        P("fsdp", None),
        P("fsdp", None),
        P("fsdp"),
        P("fsdp", None),
        P("fsdp", None),
        P("fsdp", None),
        P("fsdp", None),
        P("fsdp"),
        P("fsdp", None),
        P("fsdp", None),
        P("fsdp", None),
    )
    return jax.shard_map(
        body,
        mesh=mesh,
        in_specs=placed,
        out_specs=(
            P(("dp", "fsdp"), None, None),
            P(("dp", "fsdp"), None, None),
            P(("dp", "fsdp"), None, None),
            P("fsdp"),
            P("fsdp", None),
            P("fsdp", None),
            P("fsdp", None),
            P("fsdp", None),
            P("fsdp"),
            P("fsdp", None),
            P("fsdp", None),
            P("fsdp", None),
            P("fsdp", None),
            P("fsdp"),
            P("fsdp", None),
            P("fsdp", None),
            P("fsdp", None),
        ),
        check_vma=False,
    )
```

```python
import functools

import jax
import jax.numpy as jnp
from jax import lax
from jax.experimental import pallas as pl
from jax.experimental.pallas import tpu as pltpu
from jax.sharding import PartitionSpec as P

HD = 64
MODEL = 768


EPSILON = 1e-06
MASKED = -1000000000.0


def rms_forward(values_in, gain_vec):
    return (
        values_in
        * lax.rsqrt(jnp.mean(values_in * values_in, axis=-1, keepdims=True) + EPSILON)
        * gain_vec
    )


def rms_backward(values_in, gain_low, grad_out):
    _, pullback = jax.vjp(rms_forward, values_in, gain_low.astype(jnp.float32))
    return pullback(grad_out)


def project(acts, weight):
    return jnp.einsum("rld,dn->rln", acts, weight, preferred_element_type=jnp.float32)


def weight_grad(acts, grad_out):
    return jnp.einsum("rld,rln->dn", acts, grad_out, preferred_element_type=jnp.float32)


def input_grad(grad_out, weight):
    return jnp.einsum("rln,dn->rld", grad_out, weight, preferred_element_type=jnp.float32)


def split_heads(tensor):
    return tensor.reshape(tensor.shape[0], tensor.shape[1], -1, HD)


def merge_heads(tensor):
    return tensor.reshape(tensor.shape[0], tensor.shape[1], -1)


def attention_probs(queries, keys_all, allowed):
    scores = jnp.einsum(
        "rqhd,rkhd->rhqk",
        split_heads(queries),
        split_heads(keys_all),
        preferred_element_type=jnp.float32,
    )
    scores = jnp.where(allowed[:, None], scores, MASKED)
    return jax.nn.softmax(scores, axis=-1)


def attend_forward(queries, keys_all, values, allowed):
    probs = attention_probs(queries, keys_all, allowed).astype(jnp.bfloat16)
    mixture = jnp.einsum(
        "rhqk,rkhd->rqhd", probs, split_heads(values), preferred_element_type=jnp.float32
    )
    return merge_heads(mixture).astype(jnp.bfloat16)


def attend_backward(queries, keys_all, values, allowed, grad_mix):
    weights_full = attention_probs(queries, keys_all, allowed)
    grad_heads = split_heads(grad_mix)
    grad_values = jnp.einsum(
        "rhqk,rqhd->rkhd",
        weights_full.astype(jnp.bfloat16),
        grad_heads,
        preferred_element_type=jnp.float32,
    )
    grad_weights = jnp.einsum(
        "rqhd,rkhd->rhqk", grad_heads, split_heads(values), preferred_element_type=jnp.float32
    )
    grad_scores = (
        weights_full * (grad_weights - jnp.sum(weights_full * grad_weights, axis=-1, keepdims=True))
    ).astype(jnp.bfloat16)
    grad_queries = jnp.einsum(
        "rhqk,rkhd->rqhd", grad_scores, split_heads(keys_all), preferred_element_type=jnp.float32
    ) * HD ** (-0.5)
    grad_keys = jnp.einsum(
        "rhqk,rqhd->rkhd", grad_scores, split_heads(queries), preferred_element_type=jnp.float32
    )
    return (
        merge_heads(grad_queries).astype(jnp.bfloat16),
        merge_heads(grad_keys).astype(jnp.bfloat16),
        merge_heads(grad_values).astype(jnp.bfloat16),
    )


def gather_group(shards):
    joined = jnp.concatenate(shards, axis=0)
    whole = lax.all_gather(joined, "fsdp", axis=0, tiled=False)
    parts = []
    start = 0
    for shard in shards:
        part = whole[:, start : start + shard.shape[0]]
        parts.append(part.reshape((-1,) + shard.shape[1:]))
        start += shard.shape[0]
    return parts


def reduce_group(gradients, shards):
    count = lax.axis_size("fsdp")
    joined = jnp.concatenate(
        [
            gradient.astype(jnp.bfloat16).reshape((count, -1) + gradient.shape[1:])
            for gradient in gradients
        ],
        axis=1,
    )
    owned = lax.psum_scatter(joined, "fsdp", scatter_dimension=0, tiled=False)
    quarter = lax.psum_scatter(owned, "dp", scatter_dimension=0, tiled=True)
    summed = lax.all_gather(quarter, "dp", axis=0, tiled=True)
    parts = []
    start = 0
    for shard in shards:
        part = summed[start : start + shard.shape[0]]
        parts.append(part.astype(jnp.float32))
        start += shard.shape[0]
    return parts


def forward(dec_rows, enc_rows, self_ok, cross_ok, get_self, get_cross):
    gain_a, wq_a, wk_a, wv_a, wo_a = get_self()
    dec_float = dec_rows.astype(jnp.float32)
    normed_a = rms_forward(dec_float, gain_a.astype(jnp.float32)).astype(jnp.bfloat16)
    query_a = (project(normed_a, wq_a) * HD ** (-0.5)).astype(jnp.bfloat16)
    keys_a = project(normed_a, wk_a).astype(jnp.bfloat16)
    values_a = project(normed_a, wv_a).astype(jnp.bfloat16)
    mix_a = attend_forward(query_a, keys_a, values_a, self_ok)
    after_self = dec_float + project(mix_a, wo_a)
    gain_c, wq_c, wk_c, wv_c, wo_c = get_cross()
    normed_c = rms_forward(after_self, gain_c.astype(jnp.float32)).astype(jnp.bfloat16)
    query_c = (project(normed_c, wq_c) * HD ** (-0.5)).astype(jnp.bfloat16)
    keys_c = project(enc_rows, wk_c).astype(jnp.bfloat16)
    values_c = project(enc_rows, wv_c).astype(jnp.bfloat16)
    mix_c = attend_forward(query_c, keys_c, values_c, cross_ok)
    after_cross = after_self + project(mix_c, wo_c)
    return (
        (normed_a, query_a, keys_a, values_a, mix_a, normed_c, query_c, mix_c),
        (keys_c, values_c),
        (after_self, after_cross),
    )


def backward(dec_rows, enc_rows, self_ok, cross_ok, grad_rows, kept, get_self, get_cross, get_ffn):
    (normed_a, query_a, keys_a, values_a, mix_a, normed_c, query_c, mix_c) = kept[0]
    keys_c, values_c = kept[1]
    after_self, after_cross = kept[2]
    dec_float = dec_rows.astype(jnp.float32)
    gain_f, gate_w, up_w, down_w = get_ffn()
    normed_f = rms_forward(after_cross, gain_f.astype(jnp.float32)).astype(jnp.bfloat16)
    gate_pre = project(normed_f, gate_w)
    up_pre = project(normed_f, up_w)
    hidden_low = (jax.nn.gelu(gate_pre, approximate=True) * up_pre).astype(jnp.bfloat16)
    dec_result = (after_cross + project(hidden_low, down_w)).astype(jnp.bfloat16)
    grad_res = grad_rows.astype(jnp.float32)
    grad_branch = grad_res.astype(jnp.bfloat16)
    grad_down = weight_grad(hidden_low, grad_branch)
    grad_hidden = input_grad(grad_branch, down_w)
    _, gelu_pull = jax.vjp(
        lambda gate_in, up_in: jax.nn.gelu(gate_in, approximate=True) * up_in, gate_pre, up_pre
    )
    grad_gate_pre, grad_up_pre = gelu_pull(grad_hidden)
    grad_gate_low = grad_gate_pre.astype(jnp.bfloat16)
    grad_up_low = grad_up_pre.astype(jnp.bfloat16)
    grad_gate = weight_grad(normed_f, grad_gate_low)
    grad_up = weight_grad(normed_f, grad_up_low)
    grad_normed = input_grad(grad_gate_low, gate_w) + input_grad(grad_up_low, up_w)
    grad_input, grad_gain_f = rms_backward(after_cross, gain_f, grad_normed)
    grad_res = grad_res + grad_input
    gain_c, wq_c, wk_c, wv_c, wo_c = get_cross()
    grad_branch = grad_res.astype(jnp.bfloat16)
    grad_wo_c = weight_grad(mix_c, grad_branch)
    grad_mix = input_grad(grad_branch, wo_c).astype(jnp.bfloat16)
    grad_query, grad_keys, grad_values = attend_backward(
        query_c, keys_c, values_c, cross_ok, grad_mix
    )
    grad_wq_c = weight_grad(normed_c, grad_query)
    grad_wk_c = weight_grad(enc_rows, grad_keys)
    grad_wv_c = weight_grad(enc_rows, grad_values)
    grad_enc_rows = input_grad(grad_keys, wk_c) + input_grad(grad_values, wv_c)
    grad_normed = input_grad(grad_query, wq_c)
    grad_input, grad_gain_c = rms_backward(after_self, gain_c, grad_normed)
    grad_res = grad_res + grad_input
    gain_a, wq_a, wk_a, wv_a, wo_a = get_self()
    grad_branch = grad_res.astype(jnp.bfloat16)
    grad_wo_a = weight_grad(mix_a, grad_branch)
    grad_mix = input_grad(grad_branch, wo_a).astype(jnp.bfloat16)
    grad_query, grad_keys, grad_values = attend_backward(
        query_a, keys_a, values_a, self_ok, grad_mix
    )
    grad_wq_a = weight_grad(normed_a, grad_query)
    grad_wk_a = weight_grad(normed_a, grad_keys)
    grad_wv_a = weight_grad(normed_a, grad_values)
    grad_normed = (
        input_grad(grad_query, wq_a) + input_grad(grad_keys, wk_a) + input_grad(grad_values, wv_a)
    )
    grad_input, grad_gain_a = rms_backward(dec_float, gain_a, grad_normed)
    grad_dec_rows = grad_res + grad_input
    full_grads = (
        grad_gain_a,
        grad_wq_a,
        grad_wk_a,
        grad_wv_a,
        grad_wo_a,
        grad_gain_c,
        grad_wq_c,
        grad_wk_c,
        grad_wv_c,
        grad_wo_c,
        grad_gain_f,
        grad_gate,
        grad_up,
        grad_down,
    )
    return (dec_result, grad_dec_rows, grad_enc_rows, full_grads)


def dot_nn(left, right):
    return lax.dot_general(left, right, (((1,), (0,)), ((), ())), preferred_element_type=jnp.float32)


def dot_nt(left, right):
    return lax.dot_general(left, right, (((1,), (1,)), ((), ())), preferred_element_type=jnp.float32)


def dot_tn(left, right):
    return lax.dot_general(left, right, (((0,), (0,)), ((), ())), preferred_element_type=jnp.float32)


def flip(index, step):
    return index + step - 2 * step * ((index // step) % 2)


class Place:
    def __init__(self):
        self.dp = lax.axis_index("dp")
        self.fs = lax.axis_index("fsdp")
        self.core = self.fs % 2
        self.x = (self.fs // 2) % 2
        self.y = (self.fs // 4) % 2

    def to_core(self):
        return (self.dp, flip(self.fs, 1))

    def to_x(self):
        return (self.dp, flip(self.fs, 2))

    def to_y(self):
        return (self.dp, flip(self.fs, 4))

    def to_z(self, step):
        return (flip(self.dp, step), self.fs)


def remote(source, target, send_sem, recv_sem, device):
    return pltpu.make_async_remote_copy(
        src_ref=source,
        dst_ref=target,
        send_sem=send_sem,
        recv_sem=recv_sem,
        device_id=device,
        device_id_type=pl.DeviceIdType.MESH,
    )


def greet(devices):
    barrier = pltpu.get_barrier_semaphore()
    for device in devices:
        pl.semaphore_signal(
            barrier, inc=1, device_id=device, device_id_type=pl.DeviceIdType.MESH
        )
    pl.semaphore_wait(barrier, len(devices))


class Gather:
    def __init__(self, place, shards, wholes, chunks, sems):
        self.place = place
        self.shards = shards
        self.wholes = wholes
        self.chunks = chunks
        self.send_sems, self.recv_sems, self.own_sems = sems
        even = 1 - place.dp % 2
        fs = place.fs
        self.first = even * flip(fs, 2) + (1 - even) * flip(fs, 4)
        self.second = even * flip(fs, 4) + (1 - even) * flip(fs, 2)
        self.cross = flip(flip(fs, 2), 4)
        self.peers = [
            (place.dp, self.first),
            (place.dp, self.second),
            place.to_z(1),
            place.to_core(),
        ]

    def block(self, index, owner):
        which, start, rows = self.chunks[index]
        count = self.shards[which].shape[0]
        return self.wholes[which].at[pl.ds(owner * count + start, rows)]

    def copy(self, index, flow, owner, device, own=False):
        which, start, rows = self.chunks[index]
        source = self.shards[which].at[pl.ds(start, rows)] if own else self.block(index, owner)
        return remote(
            source,
            self.block(index, owner),
            self.send_sems.at[index, flow],
            self.recv_sems.at[index, flow],
            device,
        )

    def begin(self, index):
        fs = self.place.fs
        self.copy(index, 0, fs, self.peers[0], own=True).start()
        self.copy(index, 3, fs, self.peers[3], own=True).start()

    def keep(self, index):
        which, start, rows = self.chunks[index]
        return pltpu.make_async_copy(
            self.shards[which].at[pl.ds(start, rows)],
            self.block(index, self.place.fs),
            self.own_sems.at[index],
        )

    def relay_first(self, index):
        self.copy(index, 0, self.first, self.peers[0]).wait_recv()
        self.copy(index, 1, self.first, self.peers[1]).start()
        self.copy(index, 2, self.first, self.peers[2]).start()
        self.copy(index, 4, self.first, self.peers[3]).start()

    def relay_rest(self, index):
        self.copy(index, 1, self.cross, self.peers[1]).wait_recv()
        self.copy(index, 5, self.cross, self.peers[3]).start()
        self.copy(index, 2, self.second, self.peers[2]).wait_recv()
        self.copy(index, 6, self.second, self.peers[3]).start()

    def finish(self, index):
        self.keep(index).wait()
        for flow, owner in ((3, self.place.fs), (4, self.first), (5, self.cross), (6, self.second)):
            self.copy(index, flow, flip(owner, 1), self.peers[3]).wait_recv()

    def drain(self):
        fs = self.place.fs
        owners = (fs, self.first, self.first, fs, self.first, self.cross, self.second)
        targets = (0, 1, 2, 3, 3, 3, 3)
        for index in range(len(self.chunks)):
            for flow in range(7):
                self.copy(
                    index, flow, owners[flow], self.peers[targets[flow]], own=flow in (0, 3)
                ).wait_send()


def row_blocks(body, rows, step):
    def run(index, carry):
        body(pl.ds(pl.multiple_of(index * step, step), step))
        return carry

    lax.fori_loop(0, rows // step, run, 0)


def norm_rows(source, gain, target, rows, step=32):
    def body(block):
        values = source[block, :].astype(jnp.float32)
        scale = lax.rsqrt(jnp.mean(values * values, axis=-1, keepdims=True) + EPSILON)
        target[block, :] = (values * scale * gain).astype(target.dtype)

    row_blocks(body, rows, step)


def lane_halves():
    lane = lax.broadcasted_iota(jnp.int32, (1, 2 * HD), 1)
    low_half = (lane < HD).astype(jnp.float32)
    return low_half.astype(jnp.bfloat16), (1.0 - low_half).astype(jnp.bfloat16)


def make_masks(seg_dec, seg_enc, mask_self, mask_cross):
    rows, length = seg_dec.shape
    query = lax.broadcasted_iota(jnp.int32, (length, length), 0)
    key = lax.broadcasted_iota(jnp.int32, (length, length), 1)
    for row in range(rows):
        along = seg_dec[row : row + 1, :].astype(jnp.float32)
        down = jnp.sum(jnp.where(query == key, along, 0.0), axis=1, keepdims=True)
        same = jnp.where((down == along) & (key <= query), 1.0, 0.0)
        mask_self[row] = same
        enc = seg_enc[row : row + 1, :].astype(jnp.float32)
        mask_cross[row] = jnp.where(down == enc, 1.0, 0.0)


def softmax_rows(queries, keys, mask):
    scores = jnp.where(mask > 0.0, dot_nt(queries, keys), MASKED)
    powers = jnp.exp(scores - jnp.max(scores, axis=-1, keepdims=True))
    return powers * (1.0 / jnp.sum(powers, axis=-1, keepdims=True))


def attend_pairs(queries, keys, values, mask, target, len_q, len_k, first, last):
    pairs = queries.shape[1] // (2 * HD)

    def body(index, carry):
        row, pair = index // pairs, index % pairs
        cols = pl.ds(pl.multiple_of(pair * 2 * HD, 2 * HD), 2 * HD)
        at_q = pl.ds(pl.multiple_of(row * len_q, 16), len_q)
        at_k = pl.ds(pl.multiple_of(row * len_k, 16), len_k)
        both_q, both_k, both_v = queries[at_q, cols], keys[at_k, cols], values[at_k, cols]
        allowed = mask[row]
        total = None
        for half in lane_halves():
            probs = softmax_rows(both_q * half, both_k, allowed).astype(jnp.bfloat16)
            part = dot_nn(probs, both_v * half)
            total = part if total is None else total + part
        target[at_q, cols] = total.astype(jnp.bfloat16)
        return carry

    lax.fori_loop(first, last, body, 0)


def interleave(work, steps):
    now = 0.0
    done = 0

    def do_step():
        nonlocal now, done
        ready, action = steps[done]
        action()
        now = max(now, ready) + 0.2
        done += 1

    for needed, duration, action in work:
        while done <= needed:
            do_step()
        while done < len(steps) and steps[done][0] <= now:
            do_step()
        action()
        now += duration
    while done < len(steps):
        do_step()


FORWARD_ORDER = ("wq_a", "wk_a", "wv_a", "wo_a", "wk_c", "wv_c", "wq_c", "wo_c", "gate", "up", "down")
LINK_BYTES_PER_US = 45000.0
WINDOW = 3


def gain_row(gains, which, count):
    width = MODEL // count
    return jnp.concatenate(
        [gains[8 * owner + which : 8 * owner + which + 1, 0:width] for owner in range(count)], axis=1
    )


def forward_kernel(dims, *refs):
    shard_refs = refs[0:12]
    dec_hbm, enc_hbm, seg_dec, seg_enc = refs[12:16]
    whole_refs = refs[16:28]
    small_out, large_out, float_out = refs[28:31]
    (weights, small, large, floats, dec, enc, gains, mask_self, mask_cross) = refs[31:40]
    send_sems, recv_sems, own_sems, load_sems, store_sems = refs[40:45]
    rows, len_q, len_k, count = dims
    tokens, enc_tokens = rows * len_q, rows * len_k

    place = Place()
    chunks = [(11, 0, 8)]
    for which, shard in enumerate(shard_refs[0:11]):
        height = shard.shape[0]
        pieces = 1 if which < 8 else (2 if which < 10 else 4)
        for piece in range(pieces):
            chunks.append((which, piece * height // pieces, height // pieces))
    gather = Gather(place, shard_refs, whole_refs, chunks, (send_sems, recv_sems, own_sems))

    loads = {}

    def load(name, source, target, sem):
        loads[name] = pltpu.make_async_copy(source, target, load_sems.at[sem])
        loads[name].start()

    load("dec", dec_hbm, dec, 0)
    load("enc", enc_hbm, enc, 1)
    greet(gather.peers)
    for index in range(WINDOW):
        gather.begin(index)
    for index in range(len(chunks)):
        gather.keep(index).start()

    timed = []
    clock = 3.0
    for index, (which, start, height) in enumerate(chunks):
        bytes_sent = height * shard_refs[which].shape[1] * 2
        clock += bytes_sent / LINK_BYTES_PER_US
        again = clock + bytes_sent / LINK_BYTES_PER_US + 3.0

        def first_step(index=index):
            gather.relay_first(index)
            if index + WINDOW < len(chunks):
                gather.begin(index + WINDOW)

        def rest_step(index=index):
            gather.relay_rest(index)

        def last_step(index=index, which=which):
            gather.finish(index)
            if which < 8:
                load(which, whole_refs[which], weights.at[which], 2 + which)
            if which == 11:
                load("gains", whole_refs[11], gains, 10)

        timed.append((clock, 0, index, first_step))
        timed.append((again, 1, index, rest_step))
        timed.append((again + 2.0, 2, index, last_step))
    timed.sort(key=lambda item: item[:3])
    steps = [(item[0], item[3]) for item in timed]
    where = {item[1:3]: position for position, item in enumerate(timed)}
    whole_at = {}
    for index, (which, _, _) in enumerate(chunks):
        whole_at[which] = where[(2, index)]

    stores = []

    def store(source, target):
        stores.append(pltpu.make_async_copy(source, target, store_sems.at[len(stores)]))
        stores[-1].start()

    def keep_small(index):
        store(small.at[index], small_out.at[index])

    def project(acts, which, target, scale=None):
        loads[which].wait()
        result = dot_nn(acts[...], weights[which])
        if scale is not None:
            result = result * scale
        target[...] = result.astype(target.dtype)

    work = []

    def masks():
        make_masks(seg_dec, seg_enc, mask_self, mask_cross)
        loads["dec"].wait()

    def norm_self():
        loads["gains"].wait()
        norm_rows(dec, gain_row(gains, 0, count), small.at[0], tokens)
        keep_small(0)

    def query_self():
        project(small.at[0], 0, small.at[1], HD ** (-0.5))
        keep_small(1)

    def key_self():
        project(small.at[0], 1, small.at[2])
        keep_small(2)

    def value_self():
        project(small.at[0], 2, small.at[3])
        keep_small(3)

    def mix_self(first, last):
        attend_pairs(
            small.at[1], small.at[2], small.at[3], mask_self, small.at[4], len_q, len_q, first, last
        )

    def out_self():
        keep_small(4)
        loads[3].wait()
        floats[0] = dec[...].astype(jnp.float32) + dot_nn(small[4], weights[3])
        store(floats.at[0], float_out.at[0])
        norm_rows(floats.at[0], gain_row(gains, 1, count), small.at[5], tokens)
        keep_small(5)

    def key_cross():
        loads["enc"].wait()
        project(enc, 4, large.at[0])
        store(large.at[0], large_out.at[0])

    def value_cross():
        project(enc, 5, large.at[1])
        store(large.at[1], large_out.at[1])

    def query_cross():
        project(small.at[5], 6, small.at[6], HD ** (-0.5))
        keep_small(6)

    def mix_cross(first, last):
        attend_pairs(
            small.at[6], large.at[0], large.at[1], mask_cross, small.at[7], len_q, len_k, first, last
        )

    def out_cross():
        keep_small(7)
        loads[7].wait()
        floats[1] = floats[0] + dot_nn(small[7], weights[7])
        store(floats.at[1], float_out.at[1])
        norm_rows(floats.at[1], gain_row(gains, 2, count), small.at[8], tokens)
        keep_small(8)

    total = rows * (MODEL // (2 * HD))
    work.append((-1, 1.0, masks))
    work.append((whole_at[11], 1.0, norm_self))
    work.append((whole_at[0], 1.2, query_self))
    work.append((whole_at[1], 1.2, key_self))
    work.append((whole_at[2], 1.2, value_self))
    for part in range(2):
        bounds = (part * total // 2, (part + 1) * total // 2)
        work.append((-1, 2.0, functools.partial(mix_self, *bounds)))
    work.append((whole_at[3], 2.0, out_self))
    work.append((whole_at[4], 2.5, key_cross))
    work.append((whole_at[5], 2.5, value_cross))
    work.append((whole_at[6], 1.2, query_cross))
    for part in range(4):
        bounds = (part * total // 4, (part + 1) * total // 4)
        work.append((-1, 2.5, functools.partial(mix_cross, *bounds)))
    work.append((whole_at[7], 2.0, out_cross))
    interleave(work, steps)
    gather.drain()
    for copy in stores:
        copy.wait()


def forward_call(shards, gain_tile, dec, enc, seg_dec, seg_enc):
    rows, len_q = seg_dec.shape
    len_k = seg_enc.shape[1]
    count = lax.axis_size("fsdp")
    tokens, enc_tokens = rows * len_q, rows * len_k
    wholes = [
        jax.ShapeDtypeStruct((shard.shape[0] * count, shard.shape[1]), shard.dtype)
        for shard in (*shards, gain_tile)
    ]
    n_chunks = 17
    half = jnp.bfloat16
    in_any = pl.BlockSpec(memory_space=pl.ANY)
    in_vmem = pl.BlockSpec(memory_space=pltpu.VMEM)
    return pl.pallas_call(
        functools.partial(forward_kernel, (rows, len_q, len_k, count)),
        out_shape=wholes
        + [
            jax.ShapeDtypeStruct((9, tokens, MODEL), half),
            jax.ShapeDtypeStruct((2, enc_tokens, MODEL), half),
            jax.ShapeDtypeStruct((2, tokens, MODEL), jnp.float32),
        ],
        in_specs=[in_any] * 14 + [in_vmem] * 2,
        out_specs=[in_any] * 15,
        scratch_shapes=[
            pltpu.VMEM((8, MODEL, MODEL), half),
            pltpu.VMEM((9, tokens, MODEL), half),
            pltpu.VMEM((2, enc_tokens, MODEL), half),
            pltpu.VMEM((2, tokens, MODEL), jnp.float32),
            pltpu.VMEM((tokens, MODEL), half),
            pltpu.VMEM((enc_tokens, MODEL), half),
            pltpu.VMEM((8 * count, 128), jnp.float32),
            pltpu.VMEM((rows, len_q, len_q), jnp.float32),
            pltpu.VMEM((rows, len_q, len_k), jnp.float32),
            pltpu.SemaphoreType.DMA((n_chunks, 7)),
            pltpu.SemaphoreType.DMA((n_chunks, 7)),
            pltpu.SemaphoreType.DMA((n_chunks,)),
            pltpu.SemaphoreType.DMA((11,)),
            pltpu.SemaphoreType.DMA((13,)),
        ],
        compiler_params=pltpu.CompilerParams(
            collective_id=0, has_side_effects=True, vmem_limit_bytes=60 * 1024 * 1024
        ),
        name="gather_forward",
    )(*shards, gain_tile, dec, enc, seg_dec, seg_enc)


def body(
    dec_in,
    enc_out,
    seg_dec,
    seg_enc,
    out_grad,
    gain_self,
    wq_self,
    wk_self,
    wv_self,
    wo_self,
    gain_cross,
    wq_cross,
    wk_cross,
    wv_cross,
    wo_cross,
    gain_ffn,
    w_gate,
    w_up,
    w_down,
):
    narrow = (wq_self, wk_self, wv_self, wo_self, wq_cross, wk_cross, wv_cross, wo_cross, w_down)
    position = jnp.arange(seg_dec.shape[1])
    causal = position[:, None] >= position[None, :]
    self_ok = (seg_dec[:, :, None] == seg_dec[:, None, :]) & causal[None]
    cross_ok = seg_dec[:, :, None] == seg_enc[:, None, :]
    if lax.axis_size("fsdp") == 8 and lax.axis_size("dp") % 2 == 0:
        gain_tile = jnp.pad(
            jnp.stack([gain_self, gain_cross, gain_ffn]).astype(jnp.float32),
            ((0, 5), (0, 128 - gain_self.shape[0])),
        )
        got = forward_call(
            (wq_self, wk_self, wv_self, wo_self)
            + (wk_cross, wv_cross, wq_cross, wo_cross, w_gate, w_up, w_down),
            gain_tile,
            dec_in.reshape(-1, MODEL),
            enc_out.reshape(-1, MODEL),
            seg_dec,
            seg_enc,
        )
        gains = got[11].reshape(-1, 8, 128)[:, :3, : gain_self.shape[0]].astype(jnp.bfloat16)
        gain_a, gain_c, gain_f = (gains[:, g].reshape(-1) for g in range(3))
        get_self = lambda: (gain_a, *got[0:4])
        get_cross = lambda: (gain_c, got[6], got[4], got[5], got[7])
        get_ffn = lambda: (gain_f, got[8], got[9], got[10])
        small = [got[12][index].reshape(dec_in.shape) for index in range(8)]
        kept = (
            small,
            tuple(got[13][index].reshape(enc_out.shape) for index in range(2)),
            tuple(got[14][index].reshape(dec_in.shape) for index in range(2)),
        )
    else:
        gain_a, gain_c, gain_f = gather_group((gain_self, gain_cross, gain_ffn))
        full = gather_group(narrow)
        gate_full, up_full = gather_group((w_gate, w_up))
        get_self = lambda: (gain_a, *full[0:4])
        get_cross = lambda: (gain_c, *full[4:8])
        get_ffn = lambda: (gain_f, gate_full, up_full, full[8])
        kept = forward(dec_in, enc_out, self_ok, cross_ok, get_self, get_cross)
    result_rows, grad_rows_dec, grad_rows_enc, grads = backward(
        dec_in, enc_out, self_ok, cross_ok, out_grad, kept, get_self, get_cross, get_ffn
    )
    gains = reduce_group((grads[0], grads[5], grads[10]), (gain_self, gain_cross, gain_ffn))
    wide = reduce_group(grads[11:13], (w_gate, w_up))
    thin = reduce_group(grads[1:5] + grads[6:10] + grads[13:14], narrow)
    return (
        (result_rows, grad_rows_dec, grad_rows_enc, gains[0])
        + tuple(thin[0:4])
        + (gains[1],)
        + tuple(thin[4:8])
        + (gains[2], *wide, thin[8])
    )


def solution(mesh):
    placed = (
        P(("dp", "fsdp"), None, None),
        P(("dp", "fsdp"), None, None),
        P(("dp", "fsdp"), None),
        P(("dp", "fsdp"), None),
        P(("dp", "fsdp"), None, None),
        P("fsdp"),
        P("fsdp", None),
        P("fsdp", None),
        P("fsdp", None),
        P("fsdp", None),
        P("fsdp"),
        P("fsdp", None),
        P("fsdp", None),
        P("fsdp", None),
        P("fsdp", None),
        P("fsdp"),
        P("fsdp", None),
        P("fsdp", None),
        P("fsdp", None),
    )
    return jax.shard_map(
        body,
        mesh=mesh,
        in_specs=placed,
        out_specs=(
            P(("dp", "fsdp"), None, None),
            P(("dp", "fsdp"), None, None),
            P(("dp", "fsdp"), None, None),
            P("fsdp"),
            P("fsdp", None),
            P("fsdp", None),
            P("fsdp", None),
            P("fsdp", None),
            P("fsdp"),
            P("fsdp", None),
            P("fsdp", None),
            P("fsdp", None),
            P("fsdp", None),
            P("fsdp"),
            P("fsdp", None),
            P("fsdp", None),
            P("fsdp", None),
        ),
        check_vma=False,
    )
```

```python
import functools
import heapq
import math

import jax
import jax.numpy as jnp
from jax import lax
from jax.experimental import pallas as pl
from jax.experimental.pallas import tpu as pltpu
from jax.sharding import PartitionSpec as P

HD = 64
MODEL = 768


EPSILON = 1e-06
MASKED = -1000000000.0


def rms_forward(values_in, gain_vec):
    return (
        values_in
        * lax.rsqrt(jnp.mean(values_in * values_in, axis=-1, keepdims=True) + EPSILON)
        * gain_vec
    )


def rms_backward(values_in, gain_low, grad_out):
    _, pullback = jax.vjp(rms_forward, values_in, gain_low.astype(jnp.float32))
    return pullback(grad_out)


def project(acts, weight):
    return jnp.einsum("rld,dn->rln", acts, weight, preferred_element_type=jnp.float32)


def weight_grad(acts, grad_out):
    return jnp.einsum("rld,rln->dn", acts, grad_out, preferred_element_type=jnp.float32)


def input_grad(grad_out, weight):
    return jnp.einsum("rln,dn->rld", grad_out, weight, preferred_element_type=jnp.float32)


def split_heads(tensor):
    return tensor.reshape(tensor.shape[0], tensor.shape[1], -1, HD)


def merge_heads(tensor):
    return tensor.reshape(tensor.shape[0], tensor.shape[1], -1)


def attention_probs(queries, keys_all, allowed):
    scores = jnp.einsum(
        "rqhd,rkhd->rhqk",
        split_heads(queries),
        split_heads(keys_all),
        preferred_element_type=jnp.float32,
    )
    scores = jnp.where(allowed[:, None], scores, MASKED)
    return jax.nn.softmax(scores, axis=-1)


def attend_forward(queries, keys_all, values, allowed):
    probs = attention_probs(queries, keys_all, allowed).astype(jnp.bfloat16)
    mixture = jnp.einsum(
        "rhqk,rkhd->rqhd", probs, split_heads(values), preferred_element_type=jnp.float32
    )
    return merge_heads(mixture).astype(jnp.bfloat16)


def attend_backward(queries, keys_all, values, allowed, grad_mix):
    weights_full = attention_probs(queries, keys_all, allowed)
    grad_heads = split_heads(grad_mix)
    grad_values = jnp.einsum(
        "rhqk,rqhd->rkhd",
        weights_full.astype(jnp.bfloat16),
        grad_heads,
        preferred_element_type=jnp.float32,
    )
    grad_weights = jnp.einsum(
        "rqhd,rkhd->rhqk", grad_heads, split_heads(values), preferred_element_type=jnp.float32
    )
    grad_scores = (
        weights_full * (grad_weights - jnp.sum(weights_full * grad_weights, axis=-1, keepdims=True))
    ).astype(jnp.bfloat16)
    grad_queries = jnp.einsum(
        "rhqk,rkhd->rqhd", grad_scores, split_heads(keys_all), preferred_element_type=jnp.float32
    ) * HD ** (-0.5)
    grad_keys = jnp.einsum(
        "rhqk,rqhd->rkhd", grad_scores, split_heads(queries), preferred_element_type=jnp.float32
    )
    return (
        merge_heads(grad_queries).astype(jnp.bfloat16),
        merge_heads(grad_keys).astype(jnp.bfloat16),
        merge_heads(grad_values).astype(jnp.bfloat16),
    )


def gather_group(shards):
    joined = jnp.concatenate(shards, axis=0)
    whole = lax.all_gather(joined, "fsdp", axis=0, tiled=False)
    parts = []
    start = 0
    for shard in shards:
        part = whole[:, start : start + shard.shape[0]]
        parts.append(part.reshape((-1,) + shard.shape[1:]))
        start += shard.shape[0]
    return parts


def reduce_group(gradients, shards):
    count = lax.axis_size("fsdp")
    joined = jnp.concatenate(
        [
            gradient.astype(jnp.bfloat16).reshape((count, -1) + gradient.shape[1:])
            for gradient in gradients
        ],
        axis=1,
    )
    owned = lax.psum_scatter(joined, "fsdp", scatter_dimension=0, tiled=False)
    quarter = lax.psum_scatter(owned, "dp", scatter_dimension=0, tiled=True)
    summed = lax.all_gather(quarter, "dp", axis=0, tiled=True)
    parts = []
    start = 0
    for shard in shards:
        part = summed[start : start + shard.shape[0]]
        parts.append(part.astype(jnp.float32))
        start += shard.shape[0]
    return parts


def forward(dec_rows, enc_rows, self_ok, cross_ok, get_self, get_cross):
    gain_a, wq_a, wk_a, wv_a, wo_a = get_self()
    dec_float = dec_rows.astype(jnp.float32)
    normed_a = rms_forward(dec_float, gain_a.astype(jnp.float32)).astype(jnp.bfloat16)
    query_a = (project(normed_a, wq_a) * HD ** (-0.5)).astype(jnp.bfloat16)
    keys_a = project(normed_a, wk_a).astype(jnp.bfloat16)
    values_a = project(normed_a, wv_a).astype(jnp.bfloat16)
    mix_a = attend_forward(query_a, keys_a, values_a, self_ok)
    after_self = dec_float + project(mix_a, wo_a)
    gain_c, wq_c, wk_c, wv_c, wo_c = get_cross()
    normed_c = rms_forward(after_self, gain_c.astype(jnp.float32)).astype(jnp.bfloat16)
    query_c = (project(normed_c, wq_c) * HD ** (-0.5)).astype(jnp.bfloat16)
    keys_c = project(enc_rows, wk_c).astype(jnp.bfloat16)
    values_c = project(enc_rows, wv_c).astype(jnp.bfloat16)
    mix_c = attend_forward(query_c, keys_c, values_c, cross_ok)
    after_cross = after_self + project(mix_c, wo_c)
    return (
        (normed_a, query_a, keys_a, values_a, mix_a, normed_c, query_c, mix_c),
        (keys_c, values_c),
        (after_self, after_cross),
    )


def backward(dec_rows, enc_rows, self_ok, cross_ok, grad_rows, kept, get_self, get_cross, get_ffn):
    (normed_a, query_a, keys_a, values_a, mix_a, normed_c, query_c, mix_c) = kept[0]
    keys_c, values_c = kept[1]
    after_self, after_cross = kept[2]
    dec_float = dec_rows.astype(jnp.float32)
    gain_f, gate_w, up_w, down_w = get_ffn()
    normed_f = rms_forward(after_cross, gain_f.astype(jnp.float32)).astype(jnp.bfloat16)
    gate_pre = project(normed_f, gate_w)
    up_pre = project(normed_f, up_w)
    hidden_low = (jax.nn.gelu(gate_pre, approximate=True) * up_pre).astype(jnp.bfloat16)
    dec_result = (after_cross + project(hidden_low, down_w)).astype(jnp.bfloat16)
    grad_res = grad_rows.astype(jnp.float32)
    grad_branch = grad_res.astype(jnp.bfloat16)
    grad_down = weight_grad(hidden_low, grad_branch)
    grad_hidden = input_grad(grad_branch, down_w)
    _, gelu_pull = jax.vjp(
        lambda gate_in, up_in: jax.nn.gelu(gate_in, approximate=True) * up_in, gate_pre, up_pre
    )
    grad_gate_pre, grad_up_pre = gelu_pull(grad_hidden)
    grad_gate_low = grad_gate_pre.astype(jnp.bfloat16)
    grad_up_low = grad_up_pre.astype(jnp.bfloat16)
    grad_gate = weight_grad(normed_f, grad_gate_low)
    grad_up = weight_grad(normed_f, grad_up_low)
    grad_normed = input_grad(grad_gate_low, gate_w) + input_grad(grad_up_low, up_w)
    grad_input, grad_gain_f = rms_backward(after_cross, gain_f, grad_normed)
    grad_res = grad_res + grad_input
    gain_c, wq_c, wk_c, wv_c, wo_c = get_cross()
    grad_branch = grad_res.astype(jnp.bfloat16)
    grad_wo_c = weight_grad(mix_c, grad_branch)
    grad_mix = input_grad(grad_branch, wo_c).astype(jnp.bfloat16)
    grad_query, grad_keys, grad_values = attend_backward(
        query_c, keys_c, values_c, cross_ok, grad_mix
    )
    grad_wq_c = weight_grad(normed_c, grad_query)
    grad_wk_c = weight_grad(enc_rows, grad_keys)
    grad_wv_c = weight_grad(enc_rows, grad_values)
    grad_enc_rows = input_grad(grad_keys, wk_c) + input_grad(grad_values, wv_c)
    grad_normed = input_grad(grad_query, wq_c)
    grad_input, grad_gain_c = rms_backward(after_self, gain_c, grad_normed)
    grad_res = grad_res + grad_input
    gain_a, wq_a, wk_a, wv_a, wo_a = get_self()
    grad_branch = grad_res.astype(jnp.bfloat16)
    grad_wo_a = weight_grad(mix_a, grad_branch)
    grad_mix = input_grad(grad_branch, wo_a).astype(jnp.bfloat16)
    grad_query, grad_keys, grad_values = attend_backward(
        query_a, keys_a, values_a, self_ok, grad_mix
    )
    grad_wq_a = weight_grad(normed_a, grad_query)
    grad_wk_a = weight_grad(normed_a, grad_keys)
    grad_wv_a = weight_grad(normed_a, grad_values)
    grad_normed = (
        input_grad(grad_query, wq_a) + input_grad(grad_keys, wk_a) + input_grad(grad_values, wv_a)
    )
    grad_input, grad_gain_a = rms_backward(dec_float, gain_a, grad_normed)
    grad_dec_rows = grad_res + grad_input
    full_grads = (
        grad_gain_a,
        grad_wq_a,
        grad_wk_a,
        grad_wv_a,
        grad_wo_a,
        grad_gain_c,
        grad_wq_c,
        grad_wk_c,
        grad_wv_c,
        grad_wo_c,
        grad_gain_f,
        grad_gate,
        grad_up,
        grad_down,
    )
    return (dec_result, grad_dec_rows, grad_enc_rows, full_grads)


def dot_nn(left, right):
    return lax.dot_general(left, right, (((1,), (0,)), ((), ())), preferred_element_type=jnp.float32)


def dot_nt(left, right):
    return lax.dot_general(left, right, (((1,), (1,)), ((), ())), preferred_element_type=jnp.float32)


def dot_tn(left, right):
    return lax.dot_general(left, right, (((0,), (0,)), ((), ())), preferred_element_type=jnp.float32)


def flip(index, step):
    return index + step - 2 * step * ((index // step) % 2)


class Place:
    def __init__(self):
        self.dp = lax.axis_index("dp")
        self.fs = lax.axis_index("fsdp")
        self.core = self.fs % 2
        self.x = (self.fs // 2) % 2
        self.y = (self.fs // 4) % 2

    def to_core(self):
        return (self.dp, flip(self.fs, 1))

    def to_x(self):
        return (self.dp, flip(self.fs, 2))

    def to_y(self):
        return (self.dp, flip(self.fs, 4))

    def to_z(self, step):
        return (flip(self.dp, step), self.fs)


def remote(source, target, send_sem, recv_sem, device):
    return pltpu.make_async_remote_copy(
        src_ref=source,
        dst_ref=target,
        send_sem=send_sem,
        recv_sem=recv_sem,
        device_id=device,
        device_id_type=pl.DeviceIdType.MESH,
    )


def greet(devices):
    barrier = pltpu.get_barrier_semaphore()
    for device in devices:
        pl.semaphore_signal(
            barrier, inc=1, device_id=device, device_id_type=pl.DeviceIdType.MESH
        )
    pl.semaphore_wait(barrier, len(devices))


class Gather:
    def __init__(self, place, shards, wholes, chunks, sems):
        self.place = place
        self.shards = shards
        self.wholes = wholes
        self.chunks = chunks
        self.send_sems, self.recv_sems, self.own_sems = sems
        even = 1 - place.dp % 2
        fs = place.fs
        self.first = even * flip(fs, 2) + (1 - even) * flip(fs, 4)
        self.second = even * flip(fs, 4) + (1 - even) * flip(fs, 2)
        self.cross = flip(flip(fs, 2), 4)
        self.peers = [
            (place.dp, self.first),
            (place.dp, self.second),
            place.to_z(1),
            place.to_core(),
        ]

    def block(self, index, owner):
        which, start, rows = self.chunks[index]
        count = self.shards[which].shape[0]
        return self.wholes[which].at[pl.ds(owner * count + start, rows)]

    def copy(self, index, flow, owner, device, own=False):
        which, start, rows = self.chunks[index]
        source = self.shards[which].at[pl.ds(start, rows)] if own else self.block(index, owner)
        return remote(
            source,
            self.block(index, owner),
            self.send_sems.at[index, flow],
            self.recv_sems.at[index, flow],
            device,
        )

    def begin(self, index):
        fs = self.place.fs
        self.copy(index, 0, fs, self.peers[0], own=True).start()
        self.copy(index, 3, fs, self.peers[3], own=True).start()

    def keep(self, index):
        which, start, rows = self.chunks[index]
        return pltpu.make_async_copy(
            self.shards[which].at[pl.ds(start, rows)],
            self.block(index, self.place.fs),
            self.own_sems.at[index],
        )

    def relay_first(self, index):
        self.copy(index, 0, self.first, self.peers[0]).wait_recv()
        self.copy(index, 1, self.first, self.peers[1]).start()
        self.copy(index, 2, self.first, self.peers[2]).start()
        self.copy(index, 4, self.first, self.peers[3]).start()

    def relay_rest(self, index):
        self.copy(index, 1, self.cross, self.peers[1]).wait_recv()
        self.copy(index, 5, self.cross, self.peers[3]).start()
        self.copy(index, 2, self.second, self.peers[2]).wait_recv()
        self.copy(index, 6, self.second, self.peers[3]).start()

    def finish(self, index):
        self.keep(index).wait()
        for flow, owner in ((3, self.place.fs), (4, self.first), (5, self.cross), (6, self.second)):
            self.copy(index, flow, flip(owner, 1), self.peers[3]).wait_recv()

    def drain(self):
        fs = self.place.fs
        owners = (fs, self.first, self.first, fs, self.first, self.cross, self.second)
        targets = (0, 1, 2, 3, 3, 3, 3)
        for index in range(len(self.chunks)):
            for flow in range(7):
                self.copy(
                    index, flow, owners[flow], self.peers[targets[flow]], own=flow in (0, 3)
                ).wait_send()


def row_blocks(body, rows, step):
    def run(index, carry):
        body(pl.ds(pl.multiple_of(index * step, step), step))
        return carry

    lax.fori_loop(0, rows // step, run, 0)


def norm_rows(source, gain, target, rows, step=32):
    def body(block):
        values = source[block, :].astype(jnp.float32)
        scale = lax.rsqrt(jnp.mean(values * values, axis=-1, keepdims=True) + EPSILON)
        target[block, :] = (values * scale * gain).astype(target.dtype)

    row_blocks(body, rows, step)


def lane_halves():
    lane = lax.broadcasted_iota(jnp.int32, (1, 2 * HD), 1)
    low_half = (lane < HD).astype(jnp.float32)
    return low_half.astype(jnp.bfloat16), (1.0 - low_half).astype(jnp.bfloat16)


def make_masks(seg_dec, seg_enc, mask_self, mask_cross):
    rows, length = seg_dec.shape
    query = lax.broadcasted_iota(jnp.int32, (length, length), 0)
    key = lax.broadcasted_iota(jnp.int32, (length, length), 1)
    for row in range(rows):
        along = seg_dec[row : row + 1, :].astype(jnp.float32)
        down = jnp.sum(jnp.where(query == key, along, 0.0), axis=1, keepdims=True)
        same = jnp.where((down == along) & (key <= query), 1.0, 0.0)
        mask_self[row] = same
        enc = seg_enc[row : row + 1, :].astype(jnp.float32)
        mask_cross[row] = jnp.where(down == enc, 1.0, 0.0)


def softmax_rows(queries, keys, mask):
    scores = jnp.where(mask > 0.0, dot_nt(queries, keys), MASKED)
    powers = jnp.exp(scores - jnp.max(scores, axis=-1, keepdims=True))
    return powers * (1.0 / jnp.sum(powers, axis=-1, keepdims=True))


def attend_pairs(queries, keys, values, mask, target, len_q, len_k, first, last):
    pairs = queries.shape[1] // (2 * HD)

    def body(index, carry):
        row, pair = index // pairs, index % pairs
        cols = pl.ds(pl.multiple_of(pair * 2 * HD, 2 * HD), 2 * HD)
        at_q = pl.ds(pl.multiple_of(row * len_q, 16), len_q)
        at_k = pl.ds(pl.multiple_of(row * len_k, 16), len_k)
        both_q, both_k, both_v = queries[at_q, cols], keys[at_k, cols], values[at_k, cols]
        allowed = mask[row]
        total = None
        for half in lane_halves():
            probs = softmax_rows(both_q * half, both_k, allowed).astype(jnp.bfloat16)
            part = dot_nn(probs, both_v * half)
            total = part if total is None else total + part
        target[at_q, cols] = total.astype(jnp.bfloat16)
        return carry

    lax.fori_loop(first, last, body, 0)


def interleave(work, steps):
    now = 0.0
    done = 0

    def do_step():
        nonlocal now, done
        ready, action = steps[done]
        action()
        now = max(now, ready) + 0.2
        done += 1

    for needed, duration, action in work:
        while done <= needed:
            do_step()
        while done < len(steps) and steps[done][0] <= now:
            do_step()
        action()
        now += duration
    while done < len(steps):
        do_step()


FORWARD_ORDER = ("wq_a", "wk_a", "wv_a", "wo_a", "wk_c", "wv_c", "wq_c", "wo_c", "gate", "up", "down")
LINK_BYTES_PER_US = 45000.0
WINDOW = 3


def gain_row(gains, which, count):
    width = MODEL // count
    return jnp.concatenate(
        [gains[8 * owner + which : 8 * owner + which + 1, 0:width] for owner in range(count)], axis=1
    )


def forward_kernel(dims, *refs):
    shard_refs = refs[0:12]
    dec_hbm, enc_hbm, seg_dec, seg_enc = refs[12:16]
    whole_refs = refs[16:28]
    small_out, large_out, float_out = refs[28:31]
    (weights, small, large, floats, dec, enc, gains, mask_self, mask_cross) = refs[31:40]
    send_sems, recv_sems, own_sems, load_sems, store_sems = refs[40:45]
    rows, len_q, len_k, count = dims
    tokens, enc_tokens = rows * len_q, rows * len_k

    place = Place()
    chunks = [(11, 0, 8)]
    for which, shard in enumerate(shard_refs[0:11]):
        height = shard.shape[0]
        pieces = 1 if which < 8 else (2 if which < 10 else 4)
        for piece in range(pieces):
            chunks.append((which, piece * height // pieces, height // pieces))
    gather = Gather(place, shard_refs, whole_refs, chunks, (send_sems, recv_sems, own_sems))

    loads = {}

    def load(name, source, target, sem):
        loads[name] = pltpu.make_async_copy(source, target, load_sems.at[sem])
        loads[name].start()

    load("dec", dec_hbm, dec, 0)
    load("enc", enc_hbm, enc, 1)
    greet(gather.peers)
    for index in range(WINDOW):
        gather.begin(index)
    for index in range(len(chunks)):
        gather.keep(index).start()

    timed = []
    clock = 3.0
    for index, (which, start, height) in enumerate(chunks):
        bytes_sent = height * shard_refs[which].shape[1] * 2
        clock += bytes_sent / LINK_BYTES_PER_US
        again = clock + bytes_sent / LINK_BYTES_PER_US + 3.0

        def first_step(index=index):
            gather.relay_first(index)
            if index + WINDOW < len(chunks):
                gather.begin(index + WINDOW)

        def rest_step(index=index):
            gather.relay_rest(index)

        def last_step(index=index, which=which):
            gather.finish(index)
            if which < 8:
                load(which, whole_refs[which], weights.at[which], 2 + which)
            if which == 11:
                load("gains", whole_refs[11], gains, 10)

        timed.append((clock, 0, index, first_step))
        timed.append((again, 1, index, rest_step))
        timed.append((again + 2.0, 2, index, last_step))
    timed.sort(key=lambda item: item[:3])
    steps = [(item[0], item[3]) for item in timed]
    where = {item[1:3]: position for position, item in enumerate(timed)}
    whole_at = {}
    for index, (which, _, _) in enumerate(chunks):
        whole_at[which] = where[(2, index)]

    stores = []

    def store(source, target):
        stores.append(pltpu.make_async_copy(source, target, store_sems.at[len(stores)]))
        stores[-1].start()

    def keep_small(index):
        store(small.at[index], small_out.at[index])

    def project(acts, which, target, scale=None):
        loads[which].wait()
        result = dot_nn(acts[...], weights[which])
        if scale is not None:
            result = result * scale
        target[...] = result.astype(target.dtype)

    work = []

    def masks():
        make_masks(seg_dec, seg_enc, mask_self, mask_cross)
        loads["dec"].wait()

    def norm_self():
        loads["gains"].wait()
        norm_rows(dec, gain_row(gains, 0, count), small.at[0], tokens)
        keep_small(0)

    def query_self():
        project(small.at[0], 0, small.at[1], HD ** (-0.5))
        keep_small(1)

    def key_self():
        project(small.at[0], 1, small.at[2])
        keep_small(2)

    def value_self():
        project(small.at[0], 2, small.at[3])
        keep_small(3)

    def mix_self(first, last):
        attend_pairs(
            small.at[1], small.at[2], small.at[3], mask_self, small.at[4], len_q, len_q, first, last
        )

    def out_self():
        keep_small(4)
        loads[3].wait()
        floats[0] = dec[...].astype(jnp.float32) + dot_nn(small[4], weights[3])
        store(floats.at[0], float_out.at[0])
        norm_rows(floats.at[0], gain_row(gains, 1, count), small.at[5], tokens)
        keep_small(5)

    def key_cross():
        loads["enc"].wait()
        project(enc, 4, large.at[0])
        store(large.at[0], large_out.at[0])

    def value_cross():
        project(enc, 5, large.at[1])
        store(large.at[1], large_out.at[1])

    def query_cross():
        project(small.at[5], 6, small.at[6], HD ** (-0.5))
        keep_small(6)

    def mix_cross(first, last):
        attend_pairs(
            small.at[6], large.at[0], large.at[1], mask_cross, small.at[7], len_q, len_k, first, last
        )

    def out_cross():
        keep_small(7)
        loads[7].wait()
        floats[1] = floats[0] + dot_nn(small[7], weights[7])
        store(floats.at[1], float_out.at[1])
        norm_rows(floats.at[1], gain_row(gains, 2, count), small.at[8], tokens)
        keep_small(8)

    total = rows * (MODEL // (2 * HD))
    work.append((-1, 1.0, masks))
    work.append((whole_at[11], 1.0, norm_self))
    work.append((whole_at[0], 1.2, query_self))
    work.append((whole_at[1], 1.2, key_self))
    work.append((whole_at[2], 1.2, value_self))
    for part in range(2):
        bounds = (part * total // 2, (part + 1) * total // 2)
        work.append((-1, 2.0, functools.partial(mix_self, *bounds)))
    work.append((whole_at[3], 2.0, out_self))
    work.append((whole_at[4], 2.5, key_cross))
    work.append((whole_at[5], 2.5, value_cross))
    work.append((whole_at[6], 1.2, query_cross))
    for part in range(4):
        bounds = (part * total // 4, (part + 1) * total // 4)
        work.append((-1, 2.5, functools.partial(mix_cross, *bounds)))
    work.append((whole_at[7], 2.0, out_cross))
    interleave(work, steps)
    gather.drain()
    for copy in stores:
        copy.wait()


def forward_call(shards, gain_tile, dec, enc, seg_dec, seg_enc):
    rows, len_q = seg_dec.shape
    len_k = seg_enc.shape[1]
    count = lax.axis_size("fsdp")
    tokens, enc_tokens = rows * len_q, rows * len_k
    wholes = [
        jax.ShapeDtypeStruct((shard.shape[0] * count, shard.shape[1]), shard.dtype)
        for shard in (*shards, gain_tile)
    ]
    n_chunks = 17
    half = jnp.bfloat16
    in_any = pl.BlockSpec(memory_space=pl.ANY)
    in_vmem = pl.BlockSpec(memory_space=pltpu.VMEM)
    return pl.pallas_call(
        functools.partial(forward_kernel, (rows, len_q, len_k, count)),
        out_shape=wholes
        + [
            jax.ShapeDtypeStruct((9, tokens, MODEL), half),
            jax.ShapeDtypeStruct((2, enc_tokens, MODEL), half),
            jax.ShapeDtypeStruct((2, tokens, MODEL), jnp.float32),
        ],
        in_specs=[in_any] * 14 + [in_vmem] * 2,
        out_specs=[in_any] * 15,
        scratch_shapes=[
            pltpu.VMEM((8, MODEL, MODEL), half),
            pltpu.VMEM((9, tokens, MODEL), half),
            pltpu.VMEM((2, enc_tokens, MODEL), half),
            pltpu.VMEM((2, tokens, MODEL), jnp.float32),
            pltpu.VMEM((tokens, MODEL), half),
            pltpu.VMEM((enc_tokens, MODEL), half),
            pltpu.VMEM((8 * count, 128), jnp.float32),
            pltpu.VMEM((rows, len_q, len_q), jnp.float32),
            pltpu.VMEM((rows, len_q, len_k), jnp.float32),
            pltpu.SemaphoreType.DMA((n_chunks, 7)),
            pltpu.SemaphoreType.DMA((n_chunks, 7)),
            pltpu.SemaphoreType.DMA((n_chunks,)),
            pltpu.SemaphoreType.DMA((11,)),
            pltpu.SemaphoreType.DMA((13,)),
        ],
        compiler_params=pltpu.CompilerParams(
            collective_id=0, has_side_effects=True, vmem_limit_bytes=60 * 1024 * 1024
        ),
        name="gather_forward",
    )(*shards, gain_tile, dec, enc, seg_dec, seg_enc)


class Events:
    def __init__(self):
        self.now = 0.0
        self.heap = []
        self.count = 0
        self.free = {}

    def post(self, ready, action):
        self.count += 1
        heapq.heappush(self.heap, (ready, self.count, action))

    def sent(self, link, micros, delay=2.5):
        start = max(self.now, self.free.get(link, 0.0))
        self.free[link] = start + micros
        return start + micros + delay

    def step(self):
        ready, _, action = heapq.heappop(self.heap)
        self.now = max(self.now, ready) + 0.3
        action()

    def work(self, micros, action):
        while self.heap and self.heap[0][0] <= self.now:
            self.step()
        action()
        self.now += micros

    def drain(self):
        while self.heap:
            self.step()


class Reduction:
    def __init__(self, events, place, buffers, sems, rows, cols, itemsize, finish):
        self.events = events
        self.place = place
        self.outgoing, self.first, self.along_x, self.along_y = buffers[0:4]
        self.second, self.near, self.far, self.final = buffers[4:8]
        self.send_sems, self.recv_sems = sems
        self.half_us = rows * cols * itemsize / LINK_BYTES_PER_US
        self.finish = finish
        self.merged = False

    def copy(self, flow, source, target, device):
        return remote(source, target, self.send_sems.at[flow], self.recv_sems.at[flow], device)

    def flows(self):
        at = self.place
        zb = at.dp % 2
        return (
            (self.outgoing.at[1 - at.core], self.first, at.to_core()),
            (self.first.at[:, 1 - at.x, 0], self.along_x, at.to_x()),
            (self.first.at[1 - at.y, :, 1], self.along_y, at.to_y()),
            (self.along_x.at[1 - at.y], self.second.at[0], at.to_y()),
            (self.along_y.at[1 - at.x], self.second.at[1], at.to_x()),
            (self.second.at[1 - zb], self.near, at.to_z(1)),
            (self.near, self.far, at.to_z(2)),
            (self.final.at[zb], self.final.at[zb], at.to_z(1)),
        )

    def start(self, flow):
        self.copy(flow, *self.flows()[flow]).start()

    def received(self, flow):
        self.copy(flow, *self.flows()[flow]).wait_recv()

    def begin(self):
        self.start(0)
        self.events.post(self.events.sent("core", self.half_us * 0.8, 1.0), self.merge_cores)

    def merge_cores(self):
        at = self.place
        self.received(0)

        def add(index, carry):
            y, x, half = index // 4, (index // 2) % 2, index % 2
            self.first[y, x, half] = self.first[y, x, half] + self.outgoing[at.core, y, x, half]
            return carry

        lax.fori_loop(0, 8, add, 0)
        self.copy(0, *self.flows()[0]).wait_send()
        self.merged = True
        self.start(1)
        self.start(2)
        self.events.post(self.events.sent("plane", 2 * self.half_us), self.merge_first)

    def merge_first(self):
        at = self.place
        self.received(1)
        self.received(2)
        for index in range(2):
            self.along_x[index] = self.along_x[index] + self.first[index, at.x, 0]
            self.along_y[index] = self.along_y[index] + self.first[at.y, index, 1]
        self.start(3)
        self.start(4)
        self.events.post(self.events.sent("plane", self.half_us), self.merge_second)

    def merge_second(self):
        at = self.place
        self.received(3)
        self.received(4)
        self.second[0] = self.second[0] + self.along_x[at.y]
        self.second[1] = self.second[1] + self.along_y[at.x]
        self.start(5)
        self.events.post(self.events.sent("z", self.half_us), self.merge_near)

    def merge_near(self):
        self.received(5)
        self.near[...] = self.near[...] + self.second[self.place.dp % 2]
        self.start(6)
        self.events.post(self.events.sent("z", 2 * self.half_us), self.merge_far)

    def merge_far(self):
        self.received(6)
        self.final[self.place.dp % 2] = self.near[...] + self.far[...]
        self.start(7)
        self.events.post(self.events.sent("z", self.half_us), self.complete)

    def complete(self):
        zb = self.place.dp % 2
        self.copy(7, self.final.at[zb], self.final.at[1 - zb], self.place.to_z(1)).wait_recv()
        self.finish(self.final)

    def drain(self):
        for flow in range(1, 8):
            self.copy(flow, *self.flows()[flow]).wait_send()


def attend_pairs_back(queries, keys, values, grads, mask, len_q, len_k, first, last):
    pairs = queries.shape[1] // (2 * HD)

    def body(index, carry):
        row, pair = index // pairs, index % pairs
        cols = pl.ds(pl.multiple_of(pair * 2 * HD, 2 * HD), 2 * HD)
        at_q = pl.ds(pl.multiple_of(row * len_q, 16), len_q)
        at_k = pl.ds(pl.multiple_of(row * len_k, 16), len_k)
        both_q, both_k, both_v = queries[at_q, cols], keys[at_k, cols], values[at_k, cols]
        both_g = grads[at_q, cols]
        allowed = mask[row]
        sums = None
        for half in lane_halves():
            half_q, half_g = both_q * half, both_g * half
            probs = softmax_rows(half_q, both_k, allowed)
            grad_v = dot_tn(probs.astype(jnp.bfloat16), half_g)
            grad_p = dot_nt(half_g, both_v)
            inner = jnp.sum(probs * grad_p, axis=-1, keepdims=True)
            grad_s = (probs * (grad_p - inner)).astype(jnp.bfloat16)
            grad_q = dot_nn(grad_s, both_k * half)
            grad_k = dot_tn(grad_s, half_q)
            parts = (grad_q, grad_k, grad_v)
            sums = parts if sums is None else tuple(a + b for a, b in zip(sums, parts))
        queries[at_q, cols] = (sums[0] * HD ** (-0.5)).astype(jnp.bfloat16)
        keys[at_k, cols] = sums[1].astype(jnp.bfloat16)
        values[at_k, cols] = sums[2].astype(jnp.bfloat16)
        return carry

    lax.fori_loop(first, last, body, 0)


def norm_back(source, gain, grad_norm, residual, low, rows, step=32):
    def body(index, total):
        block = pl.ds(pl.multiple_of(index * step, step), step)
        values = source[block, :].astype(jnp.float32)
        scale = lax.rsqrt(jnp.mean(values * values, axis=-1, keepdims=True) + EPSILON)
        unit = values * scale
        grad = grad_norm[block, :]
        scaled = grad * gain
        change = scale * (scaled - unit * jnp.mean(scaled * unit, axis=-1, keepdims=True))
        updated = residual[block, :].astype(jnp.float32) + change
        if residual.dtype == jnp.float32:
            residual[block, :] = updated
        low[block, :] = updated.astype(low.dtype)
        product = grad * unit
        for start in range(0, step, 8):
            total = total + product[start : start + 8]
        return total

    total = lax.fori_loop(0, rows // step, body, jnp.zeros((8, MODEL), jnp.float32))
    return jnp.sum(total, axis=0, keepdims=True)


GELU_SCALE = (2.0 / math.pi) ** 0.5


def gelu_rows(gate_pre, up_pre, grad_hidden, hidden, grad_gate, grad_up, rows, step=16):
    def body(block):
        gate, up, grad = gate_pre[block, :], up_pre[block, :], grad_hidden[block, :]
        square = gate * gate
        bend = jnp.tanh(GELU_SCALE * gate * (1.0 + 0.044715 * square))
        rise = 0.5 * (1.0 + bend)
        value = gate * rise
        slope = rise + 0.5 * gate * (1.0 - bend * bend) * GELU_SCALE * (1.0 + 3 * 0.044715 * square)
        hidden[block, :] = (value * up).astype(jnp.bfloat16)
        grad_gate[block, :] = (grad * up * slope).astype(jnp.bfloat16)
        grad_up[block, :] = (grad * value).astype(jnp.bfloat16)

    row_blocks(body, rows, step)


QUARTERS = 4


def backward_kernel(dims, *refs):
    rows, len_q, len_k, count = dims
    tokens = rows * len_q
    whole = refs[0:12]
    small_hbm, large_hbm, float_hbm, dec_hbm, enc_hbm, grad_hbm, seg_dec, seg_enc = refs[12:20]
    dec_out, grad_dec_out, grad_enc_out, gate_out, up_out, down_out, square_out, gain_out = refs[20:28]
    (gate_w, up_w, down_w, square_w, small, large, floats, dec, enc, grad_low, gains) = refs[28:39]
    (mask_self, mask_cross, gate_pre, up_pre, grad_hidden, hidden, grad_gate, grad_up) = refs[39:47]
    (grad_norm, result, grad_mix, gain_grads) = refs[47:51]
    residual = result
    wide_bufs, tall_bufs, square_bufs, gain_bufs = refs[51:59], refs[59:67], refs[67:75], refs[75:83]
    send_sems, recv_sems, load_sems, weight_sems, store_sems = refs[83:88]

    place = Place()
    events = Events()
    loads = {}

    def load(name, source, target, sem):
        loads[name] = pltpu.make_async_copy(source, target, sem)
        loads[name].start()

    def load_quarter(quarter):
        slot = quarter % 2
        part = pl.ds(quarter * ff_part, ff_part)
        load(("gate", quarter), whole[8].at[:, part], gate_w.at[slot], weight_sems.at[slot])
        load(("up", quarter), whole[9].at[:, part], up_w.at[slot], weight_sems.at[2 + slot])
        load(("down", quarter), whole[10].at[part], down_w.at[slot], weight_sems.at[4 + slot])

    ff_part = whole[10].shape[0] // QUARTERS
    load("normed", small_hbm.at[8], small.at[8], load_sems.at[0])
    load_quarter(0)
    load("grad", grad_hbm, grad_low, load_sems.at[1])
    load("gains", whole[11], gains, load_sems.at[2])
    load_quarter(1)
    load("after_cross", float_hbm.at[1], floats.at[1], load_sems.at[3])
    square_slots = {7: 0, 4: 1, 5: 2, 6: 3, 3: 4, 0: 1, 1: 2, 2: 3}

    def load_square(which):
        slot = square_slots[which]
        load(("square", which), whole[which], square_w.at[slot], weight_sems.at[6 + which])

    for which in (7, 4, 5, 6, 3):
        load_square(which)
    load("small", small_hbm.at[pl.ds(0, 8)], small.at[pl.ds(0, 8)], load_sems.at[4])
    load("large", large_hbm, large, load_sems.at[5])
    load("enc", enc_hbm, enc, load_sems.at[6])
    load("after_self", float_hbm.at[0], floats.at[0], load_sems.at[7])
    load("dec", dec_hbm, dec, load_sems.at[8])
    greet([place.to_core(), place.to_x(), place.to_y(), place.to_z(1), place.to_z(2)])

    stores = []

    def store(source, target):
        stores.append(pltpu.make_async_copy(source, target, store_sems.at[len(stores)]))
        stores[-1].start()

    units = []

    def unit_of(buffers, index, slot, finish):
        outgoing = buffers[0].at[slot]
        shape = buffers[7].shape
        chosen = (outgoing, *(buffer.at[index] for buffer in buffers[1:8]))
        number = len(units)
        unit = Reduction(
            events,
            place,
            chosen,
            (send_sems.at[number], recv_sems.at[number]),
            shape[-2],
            shape[-1],
            jnp.dtype(buffers[7].dtype).itemsize,
            finish,
        )
        units.append(unit)
        return unit

    def claim(earlier):
        while not earlier.merged:
            events.step()

    gain_grads[...] = jnp.zeros(gain_grads.shape, jnp.float32)

    wide_units = []

    def make_wide(quarter):
        def finish(final):
            part = pl.ds(quarter * ff_part, ff_part)
            store(final.at[0], gate_out.at[:, part])
            store(final.at[1], up_out.at[:, part])

        return unit_of(wide_bufs, quarter, quarter % 2, finish)

    def ffn_forward(quarter):
        slot = quarter % 2
        loads["gate", quarter].wait()
        gate_pre[...] = dot_nn(small[8], gate_w[slot])
        loads["up", quarter].wait()
        up_pre[...] = dot_nn(small[8], up_w[slot])
        loads["down", quarter].wait()
        grad_hidden[...] = dot_nt(grad_low[...], down_w[slot])

    def ffn_gelu():
        gelu_rows(gate_pre, up_pre, grad_hidden, hidden, grad_gate, grad_up, tokens)

    def ffn_wide(quarter):
        unit = make_wide(quarter)
        wide_units.append(unit)
        height = MODEL // count
        for half, grads in enumerate((grad_gate, grad_up)):
            value = dot_tn(small[8], grads[...]).astype(jnp.bfloat16)
            for owner in range(count):
                unit.outgoing[owner % 2, owner // 4, (owner // 2) % 2, half] = value[
                    owner * height : (owner + 1) * height
                ]
        unit.begin()

    def ffn_rest(quarter):
        slot = quarter % 2
        value = dot_tn(hidden[...], grad_low[...]).astype(jnp.bfloat16)
        owners = count // QUARTERS
        height = ff_part // owners
        piece = height // 4
        for near in range(owners):
            owner = quarter * owners + near
            for part in range(4):
                start = near * height + part * piece
                tall_bufs[0][part // 2, owner % 2, owner // 4, (owner // 2) % 2, part % 2] = value[
                    start : start + piece
                ]
        change = dot_nt(grad_gate[...], gate_w[slot]) + dot_nt(grad_up[...], up_w[slot])
        output = dot_nn(hidden[...], down_w[slot])
        if quarter == 0:
            grad_norm[...] = change
            result[...] = floats[1] + output
        else:
            grad_norm[...] += change
            result[...] += output
        if quarter + 2 < QUARTERS:
            load_quarter(quarter + 2)

    def start_tall():
        for part in range(2):

            def finish(final, part=part):
                piece = final.shape[1]
                for half in range(2):
                    store(final.at[half], down_out.at[pl.ds((2 * part + half) * piece, piece)])

            unit_of(tall_bufs, part, part, finish).begin()

    def ffn_norm():
        dec_low = small.at[8]
        dec_low[...] = result[...].astype(jnp.bfloat16)
        store(dec_low, dec_out)
        residual[...] = grad_low[...].astype(jnp.float32)
        gain_grads[2:3, :] = norm_back(
            floats.at[1], gain_row(gains, 2, count), grad_norm, residual, grad_low, tokens
        )

    for quarter in range(QUARTERS):
        if quarter == 0:
            loads["normed"].wait()
            loads["grad"].wait()
        events.work(2.0, functools.partial(ffn_forward, quarter))
        events.work(1.2, ffn_gelu)
        if quarter >= 2:
            claim(wide_units[quarter - 2])
        events.work(1.5, functools.partial(ffn_wide, quarter))
        if quarter == 0:
            loads["after_cross"].wait()
        events.work(2.5, functools.partial(ffn_rest, quarter))
    events.work(0.1, start_tall)
    loads["gains"].wait()
    events.work(1.5, ffn_norm)

    square_units = []

    def square_grad(which, acts, grads):
        index = len(square_units)
        height = MODEL // count

        def finish(final):
            piece = final.shape[1]
            for half in range(2):
                store(final.at[half], square_out.at[which, pl.ds(half * piece, piece)])

        if index >= SQUARE_RING:
            claim(square_units[index - SQUARE_RING])
        unit = unit_of(square_bufs, index, index % SQUARE_RING, finish)
        square_units.append(unit)

        def compute():
            value = dot_tn(acts[...], grads[...]).astype(jnp.bfloat16)
            piece = height // 2
            for owner in range(count):
                for half in range(2):
                    start = owner * height + half * piece
                    unit.outgoing[owner % 2, owner // 4, (owner // 2) % 2, half] = value[
                        start : start + piece
                    ]
            unit.begin()

        events.work(1.2, compute)

    def mix_grad(which):
        loads["square", which].wait()
        grad_mix[...] = dot_nt(grad_low[...], square_w[square_slots[which]]).astype(jnp.bfloat16)

    def square_back(pairs):
        total = None
        for which, grads in pairs:
            loads["square", which].wait()
            part = dot_nt(grads[...], square_w[square_slots[which]])
            total = part if total is None else total + part
        grad_norm[...] = total

    def masks():
        make_masks(seg_dec, seg_enc, mask_self, mask_cross)

    pairs_all = rows * (MODEL // (2 * HD))
    events.work(1.0, masks)
    for name in ("small", "large", "enc", "after_self", "dec"):
        loads[name].wait()

    square_grad(7, small.at[7], grad_low)
    events.work(0.8, functools.partial(mix_grad, 7))
    for part in range(6):
        bounds = (part * pairs_all // 6, (part + 1) * pairs_all // 6)
        events.work(
            4.0,
            functools.partial(
                attend_pairs_back,
                small.at[6],
                large.at[0],
                large.at[1],
                grad_mix,
                mask_cross,
                len_q,
                len_k,
                *bounds,
            ),
        )
    square_grad(4, enc, large.at[0])
    square_grad(5, enc, large.at[1])
    square_grad(6, small.at[5], small.at[6])
    events.work(0.8, functools.partial(square_back, ((6, small.at[6]),)))

    def cross_norm():
        gain_grads[1:2, :] = norm_back(
            floats.at[0], gain_row(gains, 1, count), grad_norm, residual, grad_low, tokens
        )

    events.work(1.2, cross_norm)

    def enc_grad(part):
        block = pl.ds(part * (enc.shape[0] // 2), enc.shape[0] // 2)
        loads["square", 4].wait() if part == 0 else None
        loads["square", 5].wait() if part == 0 else None
        value = dot_nt(large[0, block], square_w[square_slots[4]])
        value = value + dot_nt(large[1, block], square_w[square_slots[5]])
        enc[block, :] = value.astype(jnp.bfloat16)

    square_grad(3, small.at[4], grad_low)
    events.work(0.8, functools.partial(mix_grad, 3))
    for part in range(2):
        bounds = (part * pairs_all // 2, (part + 1) * pairs_all // 2)
        events.work(
            4.0,
            functools.partial(
                attend_pairs_back,
                small.at[1],
                small.at[2],
                small.at[3],
                grad_mix,
                mask_self,
                len_q,
                len_q,
                *bounds,
            ),
        )
    square_grad(0, small.at[0], small.at[1])
    square_grad(1, small.at[0], small.at[2])
    square_grad(2, small.at[0], small.at[3])

    def enc_grads():
        enc_grad(0)
        enc_grad(1)
        store(enc, grad_enc_out)
        for which in (0, 1, 2):
            load_square(which)

    events.work(4.0, enc_grads)
    events.work(
        2.0,
        functools.partial(
            square_back, ((0, small.at[1]), (1, small.at[2]), (2, small.at[3]))
        ),
    )

    def self_norm():
        gain_grads[0:1, :] = norm_back(
            dec, gain_row(gains, 0, count), grad_norm, residual, grad_low, tokens
        )
        store(grad_low, grad_dec_out)
        width = MODEL // count
        unit = unit_of(gain_bufs, 0, 0, lambda final: store(final, gain_out))
        unit.outgoing[...] = jnp.zeros(unit.outgoing.shape, jnp.float32)
        for owner in range(count):
            unit.outgoing[owner % 2, owner // 4, (owner // 2) % 2, 0, :, 0:width] = gain_grads[
                :, owner * width : (owner + 1) * width
            ]
        unit.begin()

    events.work(1.5, self_norm)
    events.drain()
    for unit in units:
        unit.drain()
    for copy in stores:
        copy.wait()


SQUARE_RING = 3


def backward_call(got, dec, enc, grad, seg_dec, seg_enc):
    rows, len_q = seg_dec.shape
    len_k = seg_enc.shape[1]
    count = lax.axis_size("fsdp")
    tokens, enc_tokens = rows * len_q, rows * len_k
    half = jnp.bfloat16
    full = jnp.float32
    hidden_units = got[10].shape[0]
    ff_part = hidden_units // QUARTERS
    shard = MODEL // count
    down_shard = hidden_units // count
    in_any = pl.BlockSpec(memory_space=pl.ANY)
    in_vmem = pl.BlockSpec(memory_space=pltpu.VMEM)

    def buffers(number, ring, height, width, kind):
        return [
            pltpu.VMEM((ring, 2, 2, 2, 2, height, width), kind),
            pltpu.VMEM((number, 2, 2, 2, height, width), kind),
            pltpu.VMEM((number, 2, height, width), kind),
            pltpu.VMEM((number, 2, height, width), kind),
            pltpu.VMEM((number, 2, height, width), kind),
            pltpu.VMEM((number, height, width), kind),
            pltpu.VMEM((number, height, width), kind),
            pltpu.VMEM((number, 2, height, width), kind),
        ]

    number = QUARTERS + 2 + 8 + 1
    return pl.pallas_call(
        functools.partial(backward_kernel, (rows, len_q, len_k, count)),
        out_shape=[
            jax.ShapeDtypeStruct((tokens, MODEL), half),
            jax.ShapeDtypeStruct((tokens, MODEL), half),
            jax.ShapeDtypeStruct((enc_tokens, MODEL), half),
            jax.ShapeDtypeStruct((shard, hidden_units), half),
            jax.ShapeDtypeStruct((shard, hidden_units), half),
            jax.ShapeDtypeStruct((down_shard, MODEL), half),
            jax.ShapeDtypeStruct((8, shard, MODEL), half),
            jax.ShapeDtypeStruct((2, 8, 128), full),
        ],
        in_specs=[in_any] * 18 + [in_vmem] * 2,
        out_specs=[in_any] * 8,
        scratch_shapes=[
            pltpu.VMEM((2, MODEL, ff_part), half),
            pltpu.VMEM((2, MODEL, ff_part), half),
            pltpu.VMEM((2, ff_part, MODEL), half),
            pltpu.VMEM((5, MODEL, MODEL), half),
            pltpu.VMEM((9, tokens, MODEL), half),
            pltpu.VMEM((2, enc_tokens, MODEL), half),
            pltpu.VMEM((2, tokens, MODEL), full),
            pltpu.VMEM((tokens, MODEL), half),
            pltpu.VMEM((enc_tokens, MODEL), half),
            pltpu.VMEM((tokens, MODEL), half),
            pltpu.VMEM((8 * count, 128), full),
            pltpu.VMEM((rows, len_q, len_q), full),
            pltpu.VMEM((rows, len_q, len_k), full),
            pltpu.VMEM((tokens, ff_part), full),
            pltpu.VMEM((tokens, ff_part), full),
            pltpu.VMEM((tokens, ff_part), full),
            pltpu.VMEM((tokens, ff_part), half),
            pltpu.VMEM((tokens, ff_part), half),
            pltpu.VMEM((tokens, ff_part), half),
            pltpu.VMEM((tokens, MODEL), full),
            pltpu.VMEM((tokens, MODEL), full),
            pltpu.VMEM((tokens, MODEL), half),
            pltpu.VMEM((8, MODEL), full),
            *buffers(QUARTERS, 2, shard, ff_part, half),
            *buffers(2, 2, down_shard // 4, MODEL, half),
            *buffers(8, SQUARE_RING, shard // 2, MODEL, half),
            *buffers(1, 1, 8, 128, full),
            pltpu.SemaphoreType.DMA((number, 8)),
            pltpu.SemaphoreType.DMA((number, 8)),
            pltpu.SemaphoreType.DMA((9,)),
            pltpu.SemaphoreType.DMA((14,)),
            pltpu.SemaphoreType.DMA((32,)),
        ],
        compiler_params=pltpu.CompilerParams(
            collective_id=1, has_side_effects=True, vmem_limit_bytes=63 * 1024 * 1024
        ),
        name="backward_reduce",
    )(*got[0:12], *got[12:15], dec, enc, grad, seg_dec, seg_enc)


def body(
    dec_in,
    enc_out,
    seg_dec,
    seg_enc,
    out_grad,
    gain_self,
    wq_self,
    wk_self,
    wv_self,
    wo_self,
    gain_cross,
    wq_cross,
    wk_cross,
    wv_cross,
    wo_cross,
    gain_ffn,
    w_gate,
    w_up,
    w_down,
):
    narrow = (wq_self, wk_self, wv_self, wo_self, wq_cross, wk_cross, wv_cross, wo_cross, w_down)
    position = jnp.arange(seg_dec.shape[1])
    causal = position[:, None] >= position[None, :]
    self_ok = (seg_dec[:, :, None] == seg_dec[:, None, :]) & causal[None]
    cross_ok = seg_dec[:, :, None] == seg_enc[:, None, :]
    if lax.axis_size("fsdp") == 8 and lax.axis_size("dp") == 4:
        gain_tile = jnp.pad(
            jnp.stack([gain_self, gain_cross, gain_ffn]).astype(jnp.float32),
            ((0, 5), (0, 128 - gain_self.shape[0])),
        )
        dec_flat = dec_in.reshape(-1, MODEL)
        enc_flat = enc_out.reshape(-1, MODEL)
        got = forward_call(
            (wq_self, wk_self, wv_self, wo_self)
            + (wk_cross, wv_cross, wq_cross, wo_cross, w_gate, w_up, w_down),
            gain_tile,
            dec_flat,
            enc_flat,
            seg_dec,
            seg_enc,
        )
        back = backward_call(
            got, dec_flat, enc_flat, out_grad.reshape(-1, MODEL), seg_dec, seg_enc
        )
        gain_grads = back[7][0, :3, : gain_self.shape[0]]
        squares = back[6].astype(jnp.float32)
        return (
            back[0].reshape(dec_in.shape),
            back[1].astype(jnp.float32).reshape(dec_in.shape),
            back[2].astype(jnp.float32).reshape(enc_out.shape),
            gain_grads[0],
            squares[0],
            squares[1],
            squares[2],
            squares[3],
            gain_grads[1],
            squares[6],
            squares[4],
            squares[5],
            squares[7],
            gain_grads[2],
            back[3].astype(jnp.float32),
            back[4].astype(jnp.float32),
            back[5].astype(jnp.float32),
        )
    gain_a, gain_c, gain_f = gather_group((gain_self, gain_cross, gain_ffn))
    full = gather_group(narrow)
    gate_full, up_full = gather_group((w_gate, w_up))
    get_self = lambda: (gain_a, *full[0:4])
    get_cross = lambda: (gain_c, *full[4:8])
    get_ffn = lambda: (gain_f, gate_full, up_full, full[8])
    kept = forward(dec_in, enc_out, self_ok, cross_ok, get_self, get_cross)
    result_rows, grad_rows_dec, grad_rows_enc, grads = backward(
        dec_in, enc_out, self_ok, cross_ok, out_grad, kept, get_self, get_cross, get_ffn
    )
    gains = reduce_group((grads[0], grads[5], grads[10]), (gain_self, gain_cross, gain_ffn))
    wide = reduce_group(grads[11:13], (w_gate, w_up))
    thin = reduce_group(grads[1:5] + grads[6:10] + grads[13:14], narrow)
    return (
        (result_rows, grad_rows_dec, grad_rows_enc, gains[0])
        + tuple(thin[0:4])
        + (gains[1],)
        + tuple(thin[4:8])
        + (gains[2], *wide, thin[8])
    )


def solution(mesh):
    placed = (
        P(("dp", "fsdp"), None, None),
        P(("dp", "fsdp"), None, None),
        P(("dp", "fsdp"), None),
        P(("dp", "fsdp"), None),
        P(("dp", "fsdp"), None, None),
        P("fsdp"),
        P("fsdp", None),
        P("fsdp", None),
        P("fsdp", None),
        P("fsdp", None),
        P("fsdp"),
        P("fsdp", None),
        P("fsdp", None),
        P("fsdp", None),
        P("fsdp", None),
        P("fsdp"),
        P("fsdp", None),
        P("fsdp", None),
        P("fsdp", None),
    )
    return jax.shard_map(
        body,
        mesh=mesh,
        in_specs=placed,
        out_specs=(
            P(("dp", "fsdp"), None, None),
            P(("dp", "fsdp"), None, None),
            P(("dp", "fsdp"), None, None),
            P("fsdp"),
            P("fsdp", None),
            P("fsdp", None),
            P("fsdp", None),
            P("fsdp", None),
            P("fsdp"),
            P("fsdp", None),
            P("fsdp", None),
            P("fsdp", None),
            P("fsdp", None),
            P("fsdp"),
            P("fsdp", None),
            P("fsdp", None),
            P("fsdp", None),
        ),
        check_vma=False,
    )
```

```python
import functools
import heapq
import math

import jax
import jax.numpy as jnp
from jax import lax
from jax.experimental import pallas as pl
from jax.experimental.pallas import tpu as pltpu
from jax.sharding import PartitionSpec as P

HD = 64
MODEL = 768


EPSILON = 1e-06
MASKED = -1000000000.0


def rms_forward(values_in, gain_vec):
    return (
        values_in
        * lax.rsqrt(jnp.mean(values_in * values_in, axis=-1, keepdims=True) + EPSILON)
        * gain_vec
    )


def rms_backward(values_in, gain_low, grad_out):
    _, pullback = jax.vjp(rms_forward, values_in, gain_low.astype(jnp.float32))
    return pullback(grad_out)


def project(acts, weight):
    return jnp.einsum("rld,dn->rln", acts, weight, preferred_element_type=jnp.float32)


def weight_grad(acts, grad_out):
    return jnp.einsum("rld,rln->dn", acts, grad_out, preferred_element_type=jnp.float32)


def input_grad(grad_out, weight):
    return jnp.einsum("rln,dn->rld", grad_out, weight, preferred_element_type=jnp.float32)


def split_heads(tensor):
    return tensor.reshape(tensor.shape[0], tensor.shape[1], -1, HD)


def merge_heads(tensor):
    return tensor.reshape(tensor.shape[0], tensor.shape[1], -1)


def attention_probs(queries, keys_all, allowed):
    scores = jnp.einsum(
        "rqhd,rkhd->rhqk",
        split_heads(queries),
        split_heads(keys_all),
        preferred_element_type=jnp.float32,
    )
    scores = jnp.where(allowed[:, None], scores, MASKED)
    return jax.nn.softmax(scores, axis=-1)


def attend_forward(queries, keys_all, values, allowed):
    probs = attention_probs(queries, keys_all, allowed).astype(jnp.bfloat16)
    mixture = jnp.einsum(
        "rhqk,rkhd->rqhd", probs, split_heads(values), preferred_element_type=jnp.float32
    )
    return merge_heads(mixture).astype(jnp.bfloat16)


def attend_backward(queries, keys_all, values, allowed, grad_mix):
    weights_full = attention_probs(queries, keys_all, allowed)
    grad_heads = split_heads(grad_mix)
    grad_values = jnp.einsum(
        "rhqk,rqhd->rkhd",
        weights_full.astype(jnp.bfloat16),
        grad_heads,
        preferred_element_type=jnp.float32,
    )
    grad_weights = jnp.einsum(
        "rqhd,rkhd->rhqk", grad_heads, split_heads(values), preferred_element_type=jnp.float32
    )
    grad_scores = (
        weights_full * (grad_weights - jnp.sum(weights_full * grad_weights, axis=-1, keepdims=True))
    ).astype(jnp.bfloat16)
    grad_queries = jnp.einsum(
        "rhqk,rkhd->rqhd", grad_scores, split_heads(keys_all), preferred_element_type=jnp.float32
    ) * HD ** (-0.5)
    grad_keys = jnp.einsum(
        "rhqk,rqhd->rkhd", grad_scores, split_heads(queries), preferred_element_type=jnp.float32
    )
    return (
        merge_heads(grad_queries).astype(jnp.bfloat16),
        merge_heads(grad_keys).astype(jnp.bfloat16),
        merge_heads(grad_values).astype(jnp.bfloat16),
    )


def gather_group(shards):
    joined = jnp.concatenate(shards, axis=0)
    whole = lax.all_gather(joined, "fsdp", axis=0, tiled=False)
    parts = []
    start = 0
    for shard in shards:
        part = whole[:, start : start + shard.shape[0]]
        parts.append(part.reshape((-1,) + shard.shape[1:]))
        start += shard.shape[0]
    return parts


def reduce_group(gradients, shards):
    count = lax.axis_size("fsdp")
    joined = jnp.concatenate(
        [
            gradient.astype(jnp.bfloat16).reshape((count, -1) + gradient.shape[1:])
            for gradient in gradients
        ],
        axis=1,
    )
    owned = lax.psum_scatter(joined, "fsdp", scatter_dimension=0, tiled=False)
    quarter = lax.psum_scatter(owned, "dp", scatter_dimension=0, tiled=True)
    summed = lax.all_gather(quarter, "dp", axis=0, tiled=True)
    parts = []
    start = 0
    for shard in shards:
        part = summed[start : start + shard.shape[0]]
        parts.append(part.astype(jnp.float32))
        start += shard.shape[0]
    return parts


def forward(dec_rows, enc_rows, self_ok, cross_ok, get_self, get_cross):
    gain_a, wq_a, wk_a, wv_a, wo_a = get_self()
    dec_float = dec_rows.astype(jnp.float32)
    normed_a = rms_forward(dec_float, gain_a.astype(jnp.float32)).astype(jnp.bfloat16)
    query_a = (project(normed_a, wq_a) * HD ** (-0.5)).astype(jnp.bfloat16)
    keys_a = project(normed_a, wk_a).astype(jnp.bfloat16)
    values_a = project(normed_a, wv_a).astype(jnp.bfloat16)
    mix_a = attend_forward(query_a, keys_a, values_a, self_ok)
    after_self = dec_float + project(mix_a, wo_a)
    gain_c, wq_c, wk_c, wv_c, wo_c = get_cross()
    normed_c = rms_forward(after_self, gain_c.astype(jnp.float32)).astype(jnp.bfloat16)
    query_c = (project(normed_c, wq_c) * HD ** (-0.5)).astype(jnp.bfloat16)
    keys_c = project(enc_rows, wk_c).astype(jnp.bfloat16)
    values_c = project(enc_rows, wv_c).astype(jnp.bfloat16)
    mix_c = attend_forward(query_c, keys_c, values_c, cross_ok)
    after_cross = after_self + project(mix_c, wo_c)
    return (
        (normed_a, query_a, keys_a, values_a, mix_a, normed_c, query_c, mix_c),
        (keys_c, values_c),
        (after_self, after_cross),
    )


def backward(dec_rows, enc_rows, self_ok, cross_ok, grad_rows, kept, get_self, get_cross, get_ffn):
    (normed_a, query_a, keys_a, values_a, mix_a, normed_c, query_c, mix_c) = kept[0]
    keys_c, values_c = kept[1]
    after_self, after_cross = kept[2]
    dec_float = dec_rows.astype(jnp.float32)
    gain_f, gate_w, up_w, down_w = get_ffn()
    normed_f = rms_forward(after_cross, gain_f.astype(jnp.float32)).astype(jnp.bfloat16)
    gate_pre = project(normed_f, gate_w)
    up_pre = project(normed_f, up_w)
    hidden_low = (jax.nn.gelu(gate_pre, approximate=True) * up_pre).astype(jnp.bfloat16)
    dec_result = (after_cross + project(hidden_low, down_w)).astype(jnp.bfloat16)
    grad_res = grad_rows.astype(jnp.float32)
    grad_branch = grad_res.astype(jnp.bfloat16)
    grad_down = weight_grad(hidden_low, grad_branch)
    grad_hidden = input_grad(grad_branch, down_w)
    _, gelu_pull = jax.vjp(
        lambda gate_in, up_in: jax.nn.gelu(gate_in, approximate=True) * up_in, gate_pre, up_pre
    )
    grad_gate_pre, grad_up_pre = gelu_pull(grad_hidden)
    grad_gate_low = grad_gate_pre.astype(jnp.bfloat16)
    grad_up_low = grad_up_pre.astype(jnp.bfloat16)
    grad_gate = weight_grad(normed_f, grad_gate_low)
    grad_up = weight_grad(normed_f, grad_up_low)
    grad_normed = input_grad(grad_gate_low, gate_w) + input_grad(grad_up_low, up_w)
    grad_input, grad_gain_f = rms_backward(after_cross, gain_f, grad_normed)
    grad_res = grad_res + grad_input
    gain_c, wq_c, wk_c, wv_c, wo_c = get_cross()
    grad_branch = grad_res.astype(jnp.bfloat16)
    grad_wo_c = weight_grad(mix_c, grad_branch)
    grad_mix = input_grad(grad_branch, wo_c).astype(jnp.bfloat16)
    grad_query, grad_keys, grad_values = attend_backward(
        query_c, keys_c, values_c, cross_ok, grad_mix
    )
    grad_wq_c = weight_grad(normed_c, grad_query)
    grad_wk_c = weight_grad(enc_rows, grad_keys)
    grad_wv_c = weight_grad(enc_rows, grad_values)
    grad_enc_rows = input_grad(grad_keys, wk_c) + input_grad(grad_values, wv_c)
    grad_normed = input_grad(grad_query, wq_c)
    grad_input, grad_gain_c = rms_backward(after_self, gain_c, grad_normed)
    grad_res = grad_res + grad_input
    gain_a, wq_a, wk_a, wv_a, wo_a = get_self()
    grad_branch = grad_res.astype(jnp.bfloat16)
    grad_wo_a = weight_grad(mix_a, grad_branch)
    grad_mix = input_grad(grad_branch, wo_a).astype(jnp.bfloat16)
    grad_query, grad_keys, grad_values = attend_backward(
        query_a, keys_a, values_a, self_ok, grad_mix
    )
    grad_wq_a = weight_grad(normed_a, grad_query)
    grad_wk_a = weight_grad(normed_a, grad_keys)
    grad_wv_a = weight_grad(normed_a, grad_values)
    grad_normed = (
        input_grad(grad_query, wq_a) + input_grad(grad_keys, wk_a) + input_grad(grad_values, wv_a)
    )
    grad_input, grad_gain_a = rms_backward(dec_float, gain_a, grad_normed)
    grad_dec_rows = grad_res + grad_input
    full_grads = (
        grad_gain_a,
        grad_wq_a,
        grad_wk_a,
        grad_wv_a,
        grad_wo_a,
        grad_gain_c,
        grad_wq_c,
        grad_wk_c,
        grad_wv_c,
        grad_wo_c,
        grad_gain_f,
        grad_gate,
        grad_up,
        grad_down,
    )
    return (dec_result, grad_dec_rows, grad_enc_rows, full_grads)


def dot_nn(left, right):
    return lax.dot_general(left, right, (((1,), (0,)), ((), ())), preferred_element_type=jnp.float32)


def dot_nt(left, right):
    return lax.dot_general(left, right, (((1,), (1,)), ((), ())), preferred_element_type=jnp.float32)


def dot_tn(left, right):
    return lax.dot_general(left, right, (((0,), (0,)), ((), ())), preferred_element_type=jnp.float32)


def flip(index, step):
    return index + step - 2 * step * ((index // step) % 2)


class Place:
    def __init__(self):
        self.dp = lax.axis_index("dp")
        self.fs = lax.axis_index("fsdp")
        self.core = self.fs % 2
        self.x = (self.fs // 2) % 2
        self.y = (self.fs // 4) % 2
        self.inner = (self.dp * (3 - self.dp)) // 2

    def to_core(self):
        return (self.dp, flip(self.fs, 1))

    def to_x(self):
        return (self.dp, flip(self.fs, 2))

    def to_y(self):
        return (self.dp, flip(self.fs, 4))

    def to_pair(self):
        return (flip(self.dp, 1), self.fs)

    def to_middle(self):
        return (3 - self.dp, self.fs)


def remote(source, target, send_sem, recv_sem, device):
    return pltpu.make_async_remote_copy(
        src_ref=source,
        dst_ref=target,
        send_sem=send_sem,
        recv_sem=recv_sem,
        device_id=device,
        device_id_type=pl.DeviceIdType.MESH,
    )


def greet(devices):
    barrier = pltpu.get_barrier_semaphore()
    for device in devices:
        pl.semaphore_signal(
            barrier, inc=1, device_id=device, device_id_type=pl.DeviceIdType.MESH
        )
    pl.semaphore_wait(barrier, len(devices))


LINK_BYTES_PER_US = 45000.0
WINDOW = 3
QUARTERS = 4
SQUARE_RING = 3
HALF = jnp.bfloat16
FULL = jnp.float32


class Events:
    def __init__(self):
        self.now = 0.0
        self.heap = []
        self.count = 0
        self.free = {}

    def post(self, ready, action):
        self.count += 1
        heapq.heappush(self.heap, (ready, self.count, action))

    def sent(self, link, micros, delay=2.5):
        start = max(self.now, self.free.get(link, 0.0))
        self.free[link] = start + micros
        return start + micros + delay

    def step(self):
        ready, _, action = heapq.heappop(self.heap)
        self.now = max(self.now, ready) + 0.2
        action()

    def until(self, holds):
        while not holds():
            self.step()

    def work(self, micros, action):
        while self.heap and self.heap[0][0] <= self.now:
            self.step()
        action()
        self.now += micros

    def drain(self):
        while self.heap:
            self.step()


class Chunk:
    def __init__(self, events, place, shard, whole, part, micros, sems, stages, ready):
        self.events = events
        self.place = place
        self.shard = shard
        self.whole = whole
        self.start, self.rows, self.cols = part
        self.micros = micros
        self.send_sems, self.recv_sems, self.stage_sems, self.own_sems = sems
        self.stages = stages
        self.ready = ready
        self.following = None
        fs = place.fs
        even = 1 - place.dp % 2
        self.first = even * flip(fs, 2) + (1 - even) * flip(fs, 4)
        self.second = even * flip(fs, 4) + (1 - even) * flip(fs, 2)
        self.cross = flip(flip(fs, 2), 4)
        self.to = [
            (place.dp, self.first),
            (place.dp, self.second),
            place.to_pair(),
            place.to_core(),
        ]

    def own(self):
        return self.shard.at[pl.ds(self.start, self.rows), self.cols]

    def block(self, owner):
        return self.whole.at[pl.ds(owner * self.shard.shape[0] + self.start, self.rows), self.cols]

    def copy(self, flow, owner, own=False):
        return remote(
            self.own() if own else self.block(owner),
            self.block(owner),
            self.send_sems.at[flow],
            self.recv_sems.at[flow],
            self.to[min(flow, 3)],
        )

    def piece(self, ref, index):
        rows = self.rows // len(self.stages)
        return ref.at[pl.ds(index * rows, rows)] if len(self.stages) > 1 else ref

    def stage(self):
        return [
            pltpu.make_async_copy(self.piece(self.own(), index), held, self.stage_sems.at[index])
            for index, held in enumerate(self.stages)
        ]

    def keep(self):
        block = self.block(self.place.fs)
        return [
            pltpu.make_async_copy(held, self.piece(block, index), self.own_sems.at[index])
            for index, held in enumerate(self.stages)
        ]

    def begin(self):
        self.copy(0, self.place.fs, own=True).start()
        self.copy(3, self.place.fs, own=True).start()
        self.events.post(self.events.sent("gather first", self.micros), self.relay_first)

    def relay_first(self):
        self.copy(0, self.first).wait_recv()
        self.copy(1, self.first).start()
        self.copy(2, self.first).start()
        self.copy(4, self.first).start()
        if self.following is not None:
            self.following.begin()
        self.events.post(self.events.sent("gather second", self.micros), self.relay_rest)

    def relay_rest(self):
        self.copy(1, self.cross).wait_recv()
        self.copy(5, self.cross).start()
        self.copy(2, self.second).wait_recv()
        self.copy(6, self.second).start()
        self.events.post(self.events.now + 1.5, self.finish)

    def finish(self):
        for flow, owner in ((3, self.place.fs), (4, self.first), (5, self.cross), (6, self.second)):
            self.copy(flow, flip(owner, 1)).wait_recv()
        self.ready()

    def drain(self):
        fs = self.place.fs
        owners = (fs, self.first, self.first, fs, self.first, self.cross, self.second)
        for flow in range(7):
            self.copy(flow, owners[flow], own=flow in (0, 3)).wait_send()


class Reduction:
    def __init__(self, events, place, buffers, sems, rows, cols, itemsize, finish):
        self.events = events
        self.place = place
        self.outgoing, self.first, self.along_x, self.along_y = buffers[0:4]
        self.second, self.far, self.final = buffers[4:7]
        self.send_sems, self.recv_sems = sems
        self.half_us = rows * cols * itemsize / LINK_BYTES_PER_US
        self.finish = finish
        self.merged = False

    def flows(self):
        at = self.place
        return (
            (self.outgoing.at[1 - at.core], self.first, at.to_core()),
            (self.first.at[:, 1 - at.x, 0], self.along_x, at.to_x()),
            (self.first.at[1 - at.y, :, 1], self.along_y, at.to_y()),
            (self.along_x.at[1 - at.y], self.second.at[0], at.to_y()),
            (self.along_y.at[1 - at.x], self.second.at[1], at.to_x()),
            (self.second, self.final, at.to_pair()),
            (self.second, self.far, at.to_middle()),
            (self.final, self.final, at.to_pair()),
        )

    def copy(self, flow):
        source, target, device = self.flows()[flow]
        return remote(source, target, self.send_sems.at[flow], self.recv_sems.at[flow], device)

    def begin(self):
        self.copy(0).start()
        self.events.post(self.events.sent("core", self.half_us * 0.8, 1.0), self.merge_cores)

    def merge_cores(self):
        at = self.place
        self.copy(0).wait_recv()

        def add(index, carry):
            y, x, half = index // 4, (index // 2) % 2, index % 2
            self.first[y, x, half] = self.first[y, x, half] + self.outgoing[at.core, y, x, half]
            return carry

        lax.fori_loop(0, 8, add, 0)
        self.copy(0).wait_send()
        self.merged = True
        self.copy(1).start()
        self.copy(2).start()
        self.events.post(self.events.sent("plane", 2 * self.half_us), self.merge_first)

    def merge_first(self):
        at = self.place
        self.copy(1).wait_recv()
        self.copy(2).wait_recv()
        for index in range(2):
            self.along_x[index] = self.along_x[index] + self.first[index, at.x, 0]
            self.along_y[index] = self.along_y[index] + self.first[at.y, index, 1]
        self.copy(3).start()
        self.copy(4).start()
        self.events.post(self.events.sent("plane", self.half_us), self.merge_second)

    def merge_second(self):
        at = self.place
        self.copy(3).wait_recv()
        self.copy(4).wait_recv()
        self.second[0] = self.second[0] + self.along_x[at.y]
        self.second[1] = self.second[1] + self.along_y[at.x]

        @pl.when(at.inner == 0)
        def _():
            self.copy(5).start()

        self.events.post(self.events.sent("z inwards", 2 * self.half_us), self.merge_near)

    def merge_near(self):
        @pl.when(self.place.inner == 1)
        def _():
            self.copy(5).wait_recv()
            for half in range(2):
                self.second[half] = self.second[half] + self.final[half]
            self.copy(6).start()

        self.events.post(self.events.sent("z middle", 2 * self.half_us), self.merge_far)

    def merge_far(self):
        @pl.when(self.place.inner == 1)
        def _():
            self.copy(6).wait_recv()
            for half in range(2):
                self.final[half] = self.second[half] + self.far[half]
            self.copy(7).start()

        self.events.post(self.events.sent("z outwards", 2 * self.half_us), self.complete)

    def complete(self):
        @pl.when(self.place.inner == 0)
        def _():
            self.copy(7).wait_recv()

        self.finish(self.final)

    def drain(self):
        for flow in range(1, 5):
            self.copy(flow).wait_send()

        @pl.when(self.place.inner == 0)
        def _():
            self.copy(5).wait_send()

        @pl.when(self.place.inner == 1)
        def _():
            self.copy(6).wait_send()
            self.copy(7).wait_send()


def norm_rows(source, gain, target, rows, step=32):
    def body(index, carry):
        block = pl.ds(pl.multiple_of(index * step, step), step)
        values = source[block, :].astype(FULL)
        scale = lax.rsqrt(jnp.mean(values * values, axis=-1, keepdims=True) + EPSILON)
        target[block, :] = (values * scale * gain).astype(target.dtype)
        return carry

    lax.fori_loop(0, rows // step, body, 0)


def norm_back(source, gain, grad_norm, residual, low, rows, step=32):
    def body(index, total):
        block = pl.ds(pl.multiple_of(index * step, step), step)
        values = source[block, :].astype(FULL)
        scale = lax.rsqrt(jnp.mean(values * values, axis=-1, keepdims=True) + EPSILON)
        unit = values * scale
        grad = grad_norm[block, :]
        scaled = grad * gain
        change = scale * (scaled - unit * jnp.mean(scaled * unit, axis=-1, keepdims=True))
        updated = residual[block, :] + change
        residual[block, :] = updated
        low[block, :] = updated.astype(low.dtype)
        product = grad * unit
        for start in range(0, step, 8):
            total = total + product[start : start + 8]
        return total

    total = lax.fori_loop(0, rows // step, body, jnp.zeros((8, MODEL), FULL))
    return jnp.sum(total, axis=0, keepdims=True)


def make_masks(seg_dec, seg_enc, mask_self, mask_cross):
    rows, length = seg_dec.shape
    query = lax.broadcasted_iota(jnp.int32, (length, length), 0)
    key = lax.broadcasted_iota(jnp.int32, (length, length), 1)
    for row in range(rows):
        along = seg_dec[row : row + 1, :].astype(FULL)
        down = jnp.sum(jnp.where(query == key, along, 0.0), axis=1, keepdims=True)
        mask_self[row] = jnp.where((down == along) & (key <= query), 1.0, 0.0)
        enc = seg_enc[row : row + 1, :].astype(FULL)
        mask_cross[row] = jnp.where(down == enc, 1.0, 0.0)


class Heads:
    def __init__(self, queries, keys, values, mask, len_q, len_k):
        self.queries, self.keys, self.values, self.mask = queries, keys, values, mask
        self.len_q, self.len_k = len_q, len_k
        self.pairs = MODEL // (2 * HD)

    def lower(self, shape):
        return lax.broadcasted_iota(jnp.int32, shape, 1) < HD

    def stack(self, both):
        lower = self.lower((1, 2 * HD)).astype(FULL)
        upper = 1.0 - lower
        return jnp.concatenate([both * lower.astype(HALF), both * upper.astype(HALF)], axis=0)

    def join(self, stacked):
        top, bottom = stacked[: self.len_q], stacked[self.len_q :]
        return jnp.where(self.lower(top.shape), top, bottom)

    def at(self, index):
        row, pair = index // self.pairs, index % self.pairs
        cols = pl.ds(pl.multiple_of(pair * 2 * HD, 2 * HD), 2 * HD)
        at_q = pl.ds(pl.multiple_of(row * self.len_q, 16), self.len_q)
        at_k = pl.ds(pl.multiple_of(row * self.len_k, 16), self.len_k)
        return row, at_q, at_k, cols

    def probs(self, row, queries, keys):
        scores = dot_nt(queries, keys).reshape(2, self.len_q, self.len_k)
        scores = jnp.where(self.mask[row][None] > 0.0, scores, MASKED)
        scores = scores.reshape(2 * self.len_q, self.len_k)
        powers = jnp.exp(scores - jnp.max(scores, axis=-1, keepdims=True))
        return powers * (1.0 / jnp.sum(powers, axis=-1, keepdims=True))

    def forward(self, target, first, last):
        def body(index, carry):
            row, at_q, at_k, cols = self.at(index)
            queries = self.stack(self.queries[at_q, cols])
            probs = self.probs(row, queries, self.keys[at_k, cols]).astype(HALF)
            target[at_q, cols] = self.join(dot_nn(probs, self.values[at_k, cols])).astype(HALF)
            return carry

        lax.fori_loop(first, last, body, 0)

    def backward(self, grads, first, last):
        def body(index, carry):
            row, at_q, at_k, cols = self.at(index)
            queries, grad = self.stack(self.queries[at_q, cols]), self.stack(grads[at_q, cols])
            keys, values = self.keys[at_k, cols], self.values[at_k, cols]
            probs = self.probs(row, queries, keys)
            grad_v = dot_tn(probs.astype(HALF), grad)
            grad_p = dot_nt(grad, values)
            inner = jnp.sum(probs * grad_p, axis=-1, keepdims=True)
            grad_s = (probs * (grad_p - inner)).astype(HALF)
            grad_q = self.join(dot_nn(grad_s, keys)) * HD ** (-0.5)
            grad_k = dot_tn(grad_s, queries)
            self.queries[at_q, cols] = grad_q.astype(HALF)
            self.keys[at_k, cols] = grad_k.astype(HALF)
            self.values[at_k, cols] = grad_v.astype(HALF)
            return carry

        lax.fori_loop(first, last, body, 0)


GELU_SCALE = (2.0 / math.pi) ** 0.5


def gelu_rows(gate_pre, up_pre, grad_hidden, hidden, grad_gate, grad_up, rows, step=16):
    def body(index, carry):
        block = pl.ds(pl.multiple_of(index * step, step), step)
        gate, up, grad = gate_pre[block, :], up_pre[block, :], grad_hidden[block, :]
        square = gate * gate
        bend = jnp.tanh(GELU_SCALE * gate * (1.0 + 0.044715 * square))
        rise = 0.5 * (1.0 + bend)
        value = gate * rise
        slope = rise + 0.5 * gate * (1.0 - bend * bend) * GELU_SCALE * (1.0 + 3 * 0.044715 * square)
        hidden[block, :] = (value * up).astype(HALF)
        grad_gate[block, :] = (grad * up * slope).astype(HALF)
        grad_up[block, :] = (grad * value).astype(HALF)
        return carry

    lax.fori_loop(0, rows // step, body, 0)


WQ_A, WK_A, WV_A, WO_A, WK_C, WV_C, WQ_C, WO_C, GATE, UP, DOWN, GAINS = range(12)
GATHER_ORDER = (WK_C, WQ_A, WK_A, WV_A, WO_A, WV_C, WQ_C, WO_C)
SLOTS = {WK_C: 1, WQ_A: 0, WK_A: 3, WV_A: 2, WO_A: 4, WV_C: 2, WQ_C: 3, WO_C: 0}
SLOTS_BACK = {WQ_A: 0, WK_A: 3, WV_A: 4}


def layer_kernel(dims, *refs):
    rows, len_q, len_k, count = dims
    tokens = rows * len_q
    shards, gain_shards = refs[0:11], refs[11:14]
    dec_hbm, enc_hbm, grad_hbm, seg_dec, seg_enc = refs[14:19]
    whole = refs[19:30]
    dec_out, grad_dec_out, grad_enc_out, gate_out, up_out, down_out, square_out, gain_out = refs[30:38]
    (gate_w, up_w, down_w, square_w, small, large, floats, dec, enc, grad_low) = refs[38:48]
    (gain_tile, gains, mask_self, mask_cross, gate_pre, up_pre, grad_hidden) = refs[48:55]
    (hidden, grad_gate, grad_up, grad_norm, result, grad_mix, gain_grads) = refs[55:62]
    residual = result
    wide_bufs, tall_bufs, square_bufs, gain_bufs = refs[62:69], refs[69:76], refs[76:83], refs[83:90]
    gather_send, gather_recv, stage_sems, own_sems, send_sems, recv_sems = refs[90:96]
    load_sems, weight_sems, store_sems = refs[96:99]

    place = Place()
    events = Events()
    loads = {}
    stores = []
    ff_part = whole[DOWN].shape[0] // QUARTERS
    pairs_all = rows * (MODEL // (2 * HD))

    def load(name, source, target, sem):
        loads[name] = pltpu.make_async_copy(source, target, sem)
        loads[name].start()

    def store(source, target):
        stores.append(pltpu.make_async_copy(source, target, store_sems.at[len(stores)]))
        stores[-1].start()

    load("dec", dec_hbm, dec, load_sems.at[0])
    load("enc", enc_hbm, enc, load_sems.at[1])
    load("grad", grad_hbm, grad_low, load_sems.at[2])
    gain_tile[...] = jnp.zeros(gain_tile.shape, FULL)
    for which, shard in enumerate(gain_shards):
        gain_tile[which : which + 1, 0 : shard.shape[1]] = shard[...].astype(FULL)

    gathered = {}
    slot_free = {slot: True for slot in range(5)}
    waiting = []

    def try_loads():
        for entry in list(waiting):
            ready, slot, start = entry
            if ready() and slot_free[slot]:
                slot_free[slot] = False
                start()
                waiting.remove(entry)

    def want(name, ready, slot, start):
        slot_free.setdefault(slot, True)
        waiting.append((ready, slot, start))
        try_loads()

    def release(slot):
        slot_free[slot] = True
        try_loads()

    def want_square(which, slot, name):
        want(
            name,
            lambda: gathered.get(which, False),
            slot,
            lambda: load(name, whole[which], square_w.at[slot], weight_sems.at[slot]),
        )

    def want_quarter(quarter):
        slot = quarter % 2
        part = pl.ds(quarter * ff_part, ff_part)

        def start():
            load(("gate", quarter), whole[GATE].at[:, part], gate_w.at[slot], weight_sems.at[5 + slot])
            load(("up", quarter), whole[UP].at[:, part], up_w.at[slot], weight_sems.at[7 + slot])
            load(("down", quarter), whole[DOWN].at[part], down_w.at[slot], weight_sems.at[9 + slot])

        want(
            ("quarter", quarter),
            lambda: gathered.get(DOWN, False) and gathered.get((UP, quarter), False),
            ("ffn", slot),
            start,
        )

    for which in GATHER_ORDER:
        want_square(which, SLOTS[which], ("square", which))
    for quarter in range(QUARTERS):
        want_quarter(quarter)

    def need(name):
        events.until(lambda: name in loads)
        loads[name].wait()

    chunks = []

    def add_chunk(shard, target, start, height, cols, name, stages):
        index = len(chunks)
        width = cols.size if cols is not None else shard.shape[1]
        itemsize = jnp.dtype(shard.dtype).itemsize

        def ready():
            if name is not None:
                gathered[name] = True
                try_loads()

        chunks.append(
            Chunk(
                events,
                place,
                shard,
                target,
                (start, height, slice(None) if cols is None else cols),
                height * width * itemsize / LINK_BYTES_PER_US,
                (
                    gather_send.at[index],
                    gather_recv.at[index],
                    stage_sems.at[index],
                    own_sems.at[index],
                ),
                stages,
                ready,
            )
        )

    add_chunk(gain_tile, gains, 0, 8, None, GAINS, [gain_bufs[0].at[0, 0, 0, 0, 0]])
    for index, which in enumerate(GATHER_ORDER):
        held = square_bufs[0].at[0, index // 4, (index // 2) % 2, index % 2]
        add_chunk(
            shards[which],
            whole[which],
            0,
            shards[which].shape[0],
            None,
            which,
            [held.at[0], held.at[1]],
        )
    down_rows = shards[DOWN].shape[0]
    for part in range(4):
        piece = down_rows // 4
        add_chunk(
            shards[DOWN],
            whole[DOWN],
            part * piece,
            piece,
            None,
            DOWN if part == 3 else None,
            [tall_bufs[0].at[0, 0, 0, part // 2, part % 2]],
        )
    for quarter in range(QUARTERS):
        for which in (GATE, UP):
            add_chunk(
                shards[which],
                whole[which],
                0,
                shards[which].shape[0],
                pl.ds(quarter * ff_part, ff_part),
                (which, quarter),
                [wide_bufs[0].at[0, 0, quarter // 2, quarter % 2, which - GATE]],
            )
    for index, chunk in enumerate(chunks):
        if index + WINDOW < len(chunks):
            chunk.following = chunks[index + WINDOW]
    for chunk in chunks:
        for copy in chunk.stage():
            copy.start()
    greet(
        [place.to_core(), place.to_x(), place.to_y(), place.to_pair(), place.to_middle()]
    )
    for chunk in chunks[:WINDOW]:
        chunk.begin()
    for chunk in chunks:
        for staged, kept in zip(chunk.stage(), chunk.keep()):
            staged.wait()
            kept.start()

    def gain_row(which):
        width = MODEL // count
        return jnp.concatenate(
            [gains[8 * owner + which : 8 * owner + which + 1, 0:width] for owner in range(count)],
            axis=1,
        )

    def masks():
        make_masks(seg_dec, seg_enc, mask_self, mask_cross)
        gain_grads[...] = jnp.zeros(gain_grads.shape, FULL)
        loads["dec"].wait()
        for chunk in chunks:
            for kept in chunk.keep():
                kept.wait()

    def project(acts, which, target, scale=None, free=True):
        name = ("square", which)
        need(name)

        def run():
            value = dot_nn(acts[...], square_w[SLOTS[which]])
            if scale is not None:
                value = value * scale
            target[...] = value.astype(target.dtype)
            if free:
                release(SLOTS[which])

        events.work(1.0 * acts.shape[0] / tokens, run)

    def residual_add(before, acts, which, after, free):
        need(("square", which))

        def run():
            after[...] = before[...].astype(FULL) + dot_nn(acts[...], square_w[SLOTS[which]])

        events.work(1.2, run)

    def norm(source, which, target):
        events.work(
            1.0, lambda: norm_rows(source, gain_row(which), target, tokens)
        )

    def attend(heads, target, parts, micros):
        for part in range(parts):
            bounds = (part * pairs_all // parts, (part + 1) * pairs_all // parts)
            events.work(micros / parts, functools.partial(heads.forward, target, *bounds))

    self_heads = Heads(small.at[1], small.at[2], small.at[3], mask_self, len_q, len_q)
    cross_heads = Heads(small.at[6], large.at[0], large.at[1], mask_cross, len_q, len_k)
    root = HD ** (-0.5)

    events.work(1.0, masks)
    events.until(lambda: GAINS in gathered)
    norm(dec, 0, small.at[0])
    loads["enc"].wait()
    project(enc, WK_C, large.at[0], free=False)
    project(small.at[0], WQ_A, small.at[1], scale=root)
    project(small.at[0], WK_A, small.at[2])
    project(small.at[0], WV_A, small.at[3])
    attend(self_heads, small.at[4], 2, 3.0)
    residual_add(dec, small.at[4], WO_A, floats.at[0], False)
    norm(floats.at[0], 1, small.at[5])
    project(enc, WV_C, large.at[1], free=False)
    project(small.at[5], WQ_C, small.at[6], scale=root, free=False)
    attend(cross_heads, small.at[7], 4, 8.0)
    residual_add(floats.at[0], small.at[7], WO_C, floats.at[1], False)
    norm(floats.at[1], 2, small.at[8])
    loads["grad"].wait()

    units = []

    def unit_of(buffers, index, slot, finish):
        number = len(units)
        final = buffers[6]
        unit = Reduction(
            events,
            place,
            (buffers[0].at[slot], *(buffer.at[index] for buffer in buffers[1:7])),
            (send_sems.at[number], recv_sems.at[number]),
            final.shape[-2],
            final.shape[-1],
            jnp.dtype(final.dtype).itemsize,
            finish,
        )
        units.append(unit)
        return unit

    def claim(earlier):
        events.until(lambda: earlier.merged)

    wide_units = []

    def ffn_forward(quarter):
        slot = quarter % 2
        gate_pre[...] = dot_nn(small[8], gate_w[slot])
        up_pre[...] = dot_nn(small[8], up_w[slot])
        grad_hidden[...] = dot_nt(grad_low[...], down_w[slot])

    def ffn_gelu():
        gelu_rows(gate_pre, up_pre, grad_hidden, hidden, grad_gate, grad_up, tokens)

    def ffn_wide(quarter):
        def finish(final):
            part = pl.ds(quarter * ff_part, ff_part)
            store(final.at[0], gate_out.at[:, part])
            store(final.at[1], up_out.at[:, part])

        unit = unit_of(wide_bufs, quarter, quarter % 2, finish)
        wide_units.append(unit)
        height = MODEL // count
        for half, grads in enumerate((grad_gate, grad_up)):
            value = dot_tn(small[8], grads[...]).astype(HALF)
            for owner in range(count):
                unit.outgoing[owner % 2, owner // 4, (owner // 2) % 2, half] = value[
                    owner * height : (owner + 1) * height
                ]
        unit.begin()

    def ffn_tall(quarter):
        value = dot_tn(hidden[...], grad_low[...]).astype(HALF)
        owners = count // QUARTERS
        height = ff_part // owners
        piece = height // 4
        for near in range(owners):
            owner = quarter * owners + near
            for part in range(4):
                start = near * height + part * piece
                tall_bufs[0][part // 2, owner % 2, owner // 4, (owner // 2) % 2, part % 2] = value[
                    start : start + piece
                ]

    def ffn_rest(quarter):
        slot = quarter % 2
        change = dot_nt(grad_gate[...], gate_w[slot]) + dot_nt(grad_up[...], up_w[slot])
        output = dot_nn(hidden[...], down_w[slot])
        if quarter == 0:
            grad_norm[...] = change
            result[...] = floats[1] + output
        else:
            grad_norm[...] += change
            result[...] += output
        release(("ffn", slot))

    for quarter in range(QUARTERS):
        for kind in ("gate", "up", "down"):
            need((kind, quarter))
        events.work(2.0, functools.partial(ffn_forward, quarter))
        events.work(1.0, ffn_gelu)
        if quarter >= 2:
            claim(wide_units[quarter - 2])
        events.work(1.8, functools.partial(ffn_wide, quarter))
        events.work(1.0, functools.partial(ffn_tall, quarter))
        events.work(1.6, functools.partial(ffn_rest, quarter))

    def start_tall():
        for part in range(2):

            def finish(final, part=part):
                piece = final.shape[1]
                for half in range(2):
                    store(final.at[half], down_out.at[pl.ds((2 * part + half) * piece, piece)])

            unit_of(tall_bufs, part, part, finish).begin()

    def ffn_norm():
        small[8] = result[...].astype(HALF)
        store(small.at[8], dec_out)
        residual[...] = grad_low[...].astype(FULL)
        gain_grads[2:3, :] = norm_back(
            floats.at[1], gain_row(2), grad_norm, residual, grad_low, tokens
        )

    events.work(0.1, start_tall)
    events.work(2.0, ffn_norm)

    square_units = []

    def square_grad(which, acts, grads):
        index = len(square_units)
        height = MODEL // count

        def finish(final):
            piece = final.shape[1]
            for half in range(2):
                store(final.at[half], square_out.at[which, pl.ds(half * piece, piece)])

        if index >= SQUARE_RING:
            claim(square_units[index - SQUARE_RING])
        unit = unit_of(square_bufs, index, index % SQUARE_RING, finish)
        square_units.append(unit)

        def compute():
            value = dot_tn(acts[...], grads[...]).astype(HALF)
            piece = height // 2
            for owner in range(count):
                for half in range(2):
                    start = owner * height + half * piece
                    unit.outgoing[owner % 2, owner // 4, (owner // 2) % 2, half] = value[
                        start : start + piece
                    ]
            unit.begin()

        events.work(1.3, compute)

    def mix_grad(which):
        def run():
            grad_mix[...] = dot_nt(grad_low[...], square_w[SLOTS[which]]).astype(HALF)
            release(SLOTS[which])

        events.work(0.8, run)

    def attend_back(heads, parts, micros):
        for part in range(parts):
            bounds = (part * pairs_all // parts, (part + 1) * pairs_all // parts)
            events.work(micros / parts, functools.partial(heads.backward, grad_mix, *bounds))

    square_grad(WO_C, small.at[7], grad_low)
    mix_grad(WO_C)
    want_square(WQ_A, SLOTS_BACK[WQ_A], ("back", WQ_A))
    attend_back(cross_heads, 6, 16.0)
    square_grad(WK_C, enc, large.at[0])
    square_grad(WV_C, enc, large.at[1])
    square_grad(WQ_C, small.at[5], small.at[6])

    def cross_norm():
        grad_norm[...] = dot_nt(small[6], square_w[SLOTS[WQ_C]])
        release(SLOTS[WQ_C])
        gain_grads[1:2, :] = norm_back(
            floats.at[0], gain_row(1), grad_norm, residual, grad_low, tokens
        )

    events.work(2.0, cross_norm)
    want_square(WK_A, SLOTS_BACK[WK_A], ("back", WK_A))

    square_grad(WO_A, small.at[4], grad_low)
    mix_grad(WO_A)
    want_square(WV_A, SLOTS_BACK[WV_A], ("back", WV_A))
    attend_back(self_heads, 2, 6.0)
    square_grad(WQ_A, small.at[0], small.at[1])
    square_grad(WK_A, small.at[0], small.at[2])
    square_grad(WV_A, small.at[0], small.at[3])

    def self_norm():
        total = None
        for index, which in enumerate((WQ_A, WK_A, WV_A)):
            need(("back", which))
            part = dot_nt(small[1 + index], square_w[SLOTS_BACK[which]])
            total = part if total is None else total + part
        grad_norm[...] = total
        gain_grads[0:1, :] = norm_back(dec, gain_row(0), grad_norm, residual, grad_low, tokens)
        store(grad_low, grad_dec_out)
        width = MODEL // count
        unit = unit_of(gain_bufs, 0, 0, lambda final: store(final, gain_out))
        unit.outgoing[...] = jnp.zeros(unit.outgoing.shape, FULL)
        for owner in range(count):
            unit.outgoing[owner % 2, owner // 4, (owner // 2) % 2, 0, :, 0:width] = gain_grads[
                :, owner * width : (owner + 1) * width
            ]
        unit.begin()

    events.work(3.0, self_norm)

    def enc_grad(part):
        block = pl.ds(part * (enc.shape[0] // 2), enc.shape[0] // 2)
        value = dot_nt(large[0, block], square_w[SLOTS[WK_C]])
        value = value + dot_nt(large[1, block], square_w[SLOTS[WV_C]])
        enc[block, :] = value.astype(HALF)
        store(enc.at[block], grad_enc_out.at[block])

    for part in range(2):
        events.work(2.5, functools.partial(enc_grad, part))
    events.drain()
    for chunk in chunks:
        chunk.drain()
    for unit in units:
        unit.drain()
    for copy in stores:
        copy.wait()


def layer_call(shards, gain_shards, dec, enc, grad, seg_dec, seg_enc):
    rows, len_q = seg_dec.shape
    len_k = seg_enc.shape[1]
    count = lax.axis_size("fsdp")
    tokens, enc_tokens = rows * len_q, rows * len_k
    hidden_units = shards[DOWN].shape[0] * count
    ff_part = hidden_units // QUARTERS
    height = MODEL // count
    down_height = hidden_units // count
    in_any = pl.BlockSpec(memory_space=pl.ANY)
    in_vmem = pl.BlockSpec(memory_space=pltpu.VMEM)

    def buffers(number, ring, height, width, kind):
        return [
            pltpu.VMEM((ring, 2, 2, 2, 2, height, width), kind),
            pltpu.VMEM((number, 2, 2, 2, height, width), kind),
            *[pltpu.VMEM((number, 2, height, width), kind)] * 5,
        ]

    n_chunks = 1 + 8 + 4 + 2 * QUARTERS
    n_units = QUARTERS + 2 + 8 + 1
    wholes = [
        jax.ShapeDtypeStruct((shard.shape[0] * count, shard.shape[1]), shard.dtype)
        for shard in shards
    ]
    results = pl.pallas_call(
        functools.partial(layer_kernel, (rows, len_q, len_k, count)),
        out_shape=wholes
        + [
            jax.ShapeDtypeStruct((tokens, MODEL), HALF),
            jax.ShapeDtypeStruct((tokens, MODEL), HALF),
            jax.ShapeDtypeStruct((enc_tokens, MODEL), HALF),
            jax.ShapeDtypeStruct((height, hidden_units), HALF),
            jax.ShapeDtypeStruct((height, hidden_units), HALF),
            jax.ShapeDtypeStruct((down_height, MODEL), HALF),
            jax.ShapeDtypeStruct((8, height, MODEL), HALF),
            jax.ShapeDtypeStruct((2, 8, 128), FULL),
        ],
        in_specs=[in_any] * 11 + [in_vmem] * 3 + [in_any] * 3 + [in_vmem] * 2,
        out_specs=[in_any] * 19,
        scratch_shapes=[
            pltpu.VMEM((2, MODEL, ff_part), HALF),
            pltpu.VMEM((2, MODEL, ff_part), HALF),
            pltpu.VMEM((2, ff_part, MODEL), HALF),
            pltpu.VMEM((5, MODEL, MODEL), HALF),
            pltpu.VMEM((9, tokens, MODEL), HALF),
            pltpu.VMEM((2, enc_tokens, MODEL), HALF),
            pltpu.VMEM((2, tokens, MODEL), FULL),
            pltpu.VMEM((tokens, MODEL), HALF),
            pltpu.VMEM((enc_tokens, MODEL), HALF),
            pltpu.VMEM((tokens, MODEL), HALF),
            pltpu.VMEM((8, 128), FULL),
            pltpu.VMEM((8 * count, 128), FULL),
            pltpu.VMEM((rows, len_q, len_q), FULL),
            pltpu.VMEM((rows, len_q, len_k), FULL),
            *[pltpu.VMEM((tokens, ff_part), FULL)] * 3,
            *[pltpu.VMEM((tokens, ff_part), HALF)] * 3,
            pltpu.VMEM((tokens, MODEL), FULL),
            pltpu.VMEM((tokens, MODEL), FULL),
            pltpu.VMEM((tokens, MODEL), HALF),
            pltpu.VMEM((8, MODEL), FULL),
            *buffers(QUARTERS, 2, height, ff_part, HALF),
            *buffers(2, 2, down_height // 4, MODEL, HALF),
            *buffers(8, SQUARE_RING, height // 2, MODEL, HALF),
            *buffers(1, 1, 8, 128, FULL),
            pltpu.SemaphoreType.DMA((n_chunks, 7)),
            pltpu.SemaphoreType.DMA((n_chunks, 7)),
            pltpu.SemaphoreType.DMA((n_chunks, 2)),
            pltpu.SemaphoreType.DMA((n_chunks, 2)),
            pltpu.SemaphoreType.DMA((n_units, 8)),
            pltpu.SemaphoreType.DMA((n_units, 8)),
            pltpu.SemaphoreType.DMA((3,)),
            pltpu.SemaphoreType.DMA((11,)),
            pltpu.SemaphoreType.DMA((34,)),
        ],
        compiler_params=pltpu.CompilerParams(
            collective_id=0, has_side_effects=True, vmem_limit_bytes=63 * 1024 * 1024
        ),
        name="layer",
    )(*shards, *gain_shards, dec, enc, grad, seg_dec, seg_enc)
    return results[11:]


def finish_kernel(plan, *refs):
    n_in, n_out = 7, 14
    sources, gain_grads = refs[0:n_in], refs[n_in]
    targets = refs[n_in + 1 : n_in + 1 + n_out]
    gain_targets = refs[n_in + 1 + n_out : n_in + 4 + n_out]
    taken, made = refs[n_in + 4 + n_out : n_in + 6 + n_out]
    in_sems, out_sems = refs[n_in + 6 + n_out :]
    reads, writes = [], []
    for index, (source, source_at, target, target_at, _, _) in enumerate(plan):
        reads.append(
            pltpu.make_async_copy(
                sources[source].at[source_at], taken[index], in_sems.at[index]
            )
        )
        writes.append(
            pltpu.make_async_copy(made[index], targets[target].at[target_at], out_sems.at[index])
        )
    for copy in reads:
        copy.start()
    for index, target in enumerate(gain_targets):
        target[...] = gain_grads[0, index : index + 1, 0 : target.shape[1]]
    for index in range(len(plan)):
        reads[index].wait()
        made[index][...] = taken[index][...].astype(made[index].dtype)
        writes[index].start()
    for copy in writes:
        copy.wait()


def finish_call(results):
    everything = slice(None)
    plan = []

    def add(source, source_at, target, target_at, shape):
        plan.append((source, source_at, target, target_at, *shape))

    enc_rows = results[2].shape[0]
    for part in range(4):
        block = pl.ds(part * enc_rows // 4, enc_rows // 4)
        add(2, (block, everything), 2, (block, everything), (enc_rows // 4, MODEL))
    for index in (3, 4, 5, 1):
        add(index, (everything, everything), index, (everything, everything), results[index].shape)
    for index in range(8):
        add(6, (index, everything, everything), 6 + index, (everything, everything), results[6].shape[1:])
    add(0, (everything, everything), 0, (everything, everything), results[0].shape)
    shapes = [jax.ShapeDtypeStruct(results[0].shape, HALF)]
    shapes += [jax.ShapeDtypeStruct(results[index].shape, FULL) for index in range(1, 6)]
    shapes += [jax.ShapeDtypeStruct(results[6].shape[1:], FULL)] * 8
    gain = results[6].shape[1]
    in_any = pl.BlockSpec(memory_space=pl.ANY)
    in_vmem = pl.BlockSpec(memory_space=pltpu.VMEM)
    return pl.pallas_call(
        functools.partial(finish_kernel, plan),
        out_shape=shapes + [jax.ShapeDtypeStruct((1, gain), FULL)] * 3,
        in_specs=[in_any] * 7 + [in_vmem],
        out_specs=[in_any] * 14 + [in_vmem] * 3,
        scratch_shapes=[
            [pltpu.VMEM(entry[4:6], HALF) for entry in plan],
            [pltpu.VMEM(entry[4:6], HALF if entry[2] == 0 else FULL) for entry in plan],
            pltpu.SemaphoreType.DMA((len(plan),)),
            pltpu.SemaphoreType.DMA((len(plan),)),
        ],
        compiler_params=pltpu.CompilerParams(vmem_limit_bytes=63 * 1024 * 1024),
        name="finish",
    )(*results)


def body(
    dec_in,
    enc_out,
    seg_dec,
    seg_enc,
    out_grad,
    gain_self,
    wq_self,
    wk_self,
    wv_self,
    wo_self,
    gain_cross,
    wq_cross,
    wk_cross,
    wv_cross,
    wo_cross,
    gain_ffn,
    w_gate,
    w_up,
    w_down,
):
    narrow = (wq_self, wk_self, wv_self, wo_self, wq_cross, wk_cross, wv_cross, wo_cross, w_down)
    position = jnp.arange(seg_dec.shape[1])
    causal = position[:, None] >= position[None, :]
    self_ok = (seg_dec[:, :, None] == seg_dec[:, None, :]) & causal[None]
    cross_ok = seg_dec[:, :, None] == seg_enc[:, None, :]
    if lax.axis_size("fsdp") == 8 and lax.axis_size("dp") == 4:
        back = layer_call(
            (wq_self, wk_self, wv_self, wo_self)
            + (wk_cross, wv_cross, wq_cross, wo_cross, w_gate, w_up, w_down),
            tuple(gain.reshape(1, -1) for gain in (gain_self, gain_cross, gain_ffn)),
            dec_in.reshape(-1, MODEL),
            enc_out.reshape(-1, MODEL),
            out_grad.reshape(-1, MODEL),
            seg_dec,
            seg_enc,
        )
        final = finish_call(back)
        squares = final[6:14]
        gain_grads = [grad.reshape(-1) for grad in final[14:17]]
        return (
            final[0].reshape(dec_in.shape),
            final[1].reshape(dec_in.shape),
            final[2].reshape(enc_out.shape),
            gain_grads[0],
            squares[WQ_A],
            squares[WK_A],
            squares[WV_A],
            squares[WO_A],
            gain_grads[1],
            squares[WQ_C],
            squares[WK_C],
            squares[WV_C],
            squares[WO_C],
            gain_grads[2],
            final[3],
            final[4],
            final[5],
        )
    gain_a, gain_c, gain_f = gather_group((gain_self, gain_cross, gain_ffn))
    full = gather_group(narrow)
    gate_full, up_full = gather_group((w_gate, w_up))
    get_self = lambda: (gain_a, *full[0:4])
    get_cross = lambda: (gain_c, *full[4:8])
    get_ffn = lambda: (gain_f, gate_full, up_full, full[8])
    kept = forward(dec_in, enc_out, self_ok, cross_ok, get_self, get_cross)
    result_rows, grad_rows_dec, grad_rows_enc, grads = backward(
        dec_in, enc_out, self_ok, cross_ok, out_grad, kept, get_self, get_cross, get_ffn
    )
    gains = reduce_group((grads[0], grads[5], grads[10]), (gain_self, gain_cross, gain_ffn))
    wide = reduce_group(grads[11:13], (w_gate, w_up))
    thin = reduce_group(grads[1:5] + grads[6:10] + grads[13:14], narrow)
    return (
        (result_rows, grad_rows_dec, grad_rows_enc, gains[0])
        + tuple(thin[0:4])
        + (gains[1],)
        + tuple(thin[4:8])
        + (gains[2], *wide, thin[8])
    )


def solution(mesh):
    placed = (
        P(("dp", "fsdp"), None, None),
        P(("dp", "fsdp"), None, None),
        P(("dp", "fsdp"), None),
        P(("dp", "fsdp"), None),
        P(("dp", "fsdp"), None, None),
        P("fsdp"),
        P("fsdp", None),
        P("fsdp", None),
        P("fsdp", None),
        P("fsdp", None),
        P("fsdp"),
        P("fsdp", None),
        P("fsdp", None),
        P("fsdp", None),
        P("fsdp", None),
        P("fsdp"),
        P("fsdp", None),
        P("fsdp", None),
        P("fsdp", None),
    )
    return jax.shard_map(
        body,
        mesh=mesh,
        in_specs=placed,
        out_specs=(
            P(("dp", "fsdp"), None, None),
            P(("dp", "fsdp"), None, None),
            P(("dp", "fsdp"), None, None),
            P("fsdp"),
            P("fsdp", None),
            P("fsdp", None),
            P("fsdp", None),
            P("fsdp", None),
            P("fsdp"),
            P("fsdp", None),
            P("fsdp", None),
            P("fsdp", None),
            P("fsdp", None),
            P("fsdp"),
            P("fsdp", None),
            P("fsdp", None),
            P("fsdp", None),
        ),
        check_vma=False,
    )
```

```python
import functools
import heapq
import math

import jax
import jax.numpy as jnp
from jax import lax
from jax.experimental import pallas as pl
from jax.experimental.pallas import tpu as pltpu
from jax.sharding import PartitionSpec as P

HD = 64
MODEL = 768


EPSILON = 1e-06
MASKED = -1000000000.0


def rms_forward(values_in, gain_vec):
    return (
        values_in
        * lax.rsqrt(jnp.mean(values_in * values_in, axis=-1, keepdims=True) + EPSILON)
        * gain_vec
    )


def rms_backward(values_in, gain_low, grad_out):
    _, pullback = jax.vjp(rms_forward, values_in, gain_low.astype(jnp.float32))
    return pullback(grad_out)


def project(acts, weight):
    return jnp.einsum("rld,dn->rln", acts, weight, preferred_element_type=jnp.float32)


def weight_grad(acts, grad_out):
    return jnp.einsum("rld,rln->dn", acts, grad_out, preferred_element_type=jnp.float32)


def input_grad(grad_out, weight):
    return jnp.einsum("rln,dn->rld", grad_out, weight, preferred_element_type=jnp.float32)


def split_heads(tensor):
    return tensor.reshape(tensor.shape[0], tensor.shape[1], -1, HD)


def merge_heads(tensor):
    return tensor.reshape(tensor.shape[0], tensor.shape[1], -1)


def attention_probs(queries, keys_all, allowed):
    scores = jnp.einsum(
        "rqhd,rkhd->rhqk",
        split_heads(queries),
        split_heads(keys_all),
        preferred_element_type=jnp.float32,
    )
    scores = jnp.where(allowed[:, None], scores, MASKED)
    return jax.nn.softmax(scores, axis=-1)


def attend_forward(queries, keys_all, values, allowed):
    probs = attention_probs(queries, keys_all, allowed).astype(jnp.bfloat16)
    mixture = jnp.einsum(
        "rhqk,rkhd->rqhd", probs, split_heads(values), preferred_element_type=jnp.float32
    )
    return merge_heads(mixture).astype(jnp.bfloat16)


def attend_backward(queries, keys_all, values, allowed, grad_mix):
    weights_full = attention_probs(queries, keys_all, allowed)
    grad_heads = split_heads(grad_mix)
    grad_values = jnp.einsum(
        "rhqk,rqhd->rkhd",
        weights_full.astype(jnp.bfloat16),
        grad_heads,
        preferred_element_type=jnp.float32,
    )
    grad_weights = jnp.einsum(
        "rqhd,rkhd->rhqk", grad_heads, split_heads(values), preferred_element_type=jnp.float32
    )
    grad_scores = (
        weights_full * (grad_weights - jnp.sum(weights_full * grad_weights, axis=-1, keepdims=True))
    ).astype(jnp.bfloat16)
    grad_queries = jnp.einsum(
        "rhqk,rkhd->rqhd", grad_scores, split_heads(keys_all), preferred_element_type=jnp.float32
    ) * HD ** (-0.5)
    grad_keys = jnp.einsum(
        "rhqk,rqhd->rkhd", grad_scores, split_heads(queries), preferred_element_type=jnp.float32
    )
    return (
        merge_heads(grad_queries).astype(jnp.bfloat16),
        merge_heads(grad_keys).astype(jnp.bfloat16),
        merge_heads(grad_values).astype(jnp.bfloat16),
    )


def gather_group(shards):
    joined = jnp.concatenate(shards, axis=0)
    whole = lax.all_gather(joined, "fsdp", axis=0, tiled=False)
    parts = []
    start = 0
    for shard in shards:
        part = whole[:, start : start + shard.shape[0]]
        parts.append(part.reshape((-1,) + shard.shape[1:]))
        start += shard.shape[0]
    return parts


def reduce_group(gradients, shards):
    count = lax.axis_size("fsdp")
    joined = jnp.concatenate(
        [
            gradient.astype(jnp.bfloat16).reshape((count, -1) + gradient.shape[1:])
            for gradient in gradients
        ],
        axis=1,
    )
    owned = lax.psum_scatter(joined, "fsdp", scatter_dimension=0, tiled=False)
    quarter = lax.psum_scatter(owned, "dp", scatter_dimension=0, tiled=True)
    summed = lax.all_gather(quarter, "dp", axis=0, tiled=True)
    parts = []
    start = 0
    for shard in shards:
        part = summed[start : start + shard.shape[0]]
        parts.append(part.astype(jnp.float32))
        start += shard.shape[0]
    return parts


def forward(dec_rows, enc_rows, self_ok, cross_ok, get_self, get_cross):
    gain_a, wq_a, wk_a, wv_a, wo_a = get_self()
    dec_float = dec_rows.astype(jnp.float32)
    normed_a = rms_forward(dec_float, gain_a.astype(jnp.float32)).astype(jnp.bfloat16)
    query_a = (project(normed_a, wq_a) * HD ** (-0.5)).astype(jnp.bfloat16)
    keys_a = project(normed_a, wk_a).astype(jnp.bfloat16)
    values_a = project(normed_a, wv_a).astype(jnp.bfloat16)
    mix_a = attend_forward(query_a, keys_a, values_a, self_ok)
    after_self = dec_float + project(mix_a, wo_a)
    gain_c, wq_c, wk_c, wv_c, wo_c = get_cross()
    normed_c = rms_forward(after_self, gain_c.astype(jnp.float32)).astype(jnp.bfloat16)
    query_c = (project(normed_c, wq_c) * HD ** (-0.5)).astype(jnp.bfloat16)
    keys_c = project(enc_rows, wk_c).astype(jnp.bfloat16)
    values_c = project(enc_rows, wv_c).astype(jnp.bfloat16)
    mix_c = attend_forward(query_c, keys_c, values_c, cross_ok)
    after_cross = after_self + project(mix_c, wo_c)
    return (
        (normed_a, query_a, keys_a, values_a, mix_a, normed_c, query_c, mix_c),
        (keys_c, values_c),
        (after_self, after_cross),
    )


def backward(dec_rows, enc_rows, self_ok, cross_ok, grad_rows, kept, get_self, get_cross, get_ffn):
    (normed_a, query_a, keys_a, values_a, mix_a, normed_c, query_c, mix_c) = kept[0]
    keys_c, values_c = kept[1]
    after_self, after_cross = kept[2]
    dec_float = dec_rows.astype(jnp.float32)
    gain_f, gate_w, up_w, down_w = get_ffn()
    normed_f = rms_forward(after_cross, gain_f.astype(jnp.float32)).astype(jnp.bfloat16)
    gate_pre = project(normed_f, gate_w)
    up_pre = project(normed_f, up_w)
    hidden_low = (jax.nn.gelu(gate_pre, approximate=True) * up_pre).astype(jnp.bfloat16)
    dec_result = (after_cross + project(hidden_low, down_w)).astype(jnp.bfloat16)
    grad_res = grad_rows.astype(jnp.float32)
    grad_branch = grad_res.astype(jnp.bfloat16)
    grad_down = weight_grad(hidden_low, grad_branch)
    grad_hidden = input_grad(grad_branch, down_w)
    _, gelu_pull = jax.vjp(
        lambda gate_in, up_in: jax.nn.gelu(gate_in, approximate=True) * up_in, gate_pre, up_pre
    )
    grad_gate_pre, grad_up_pre = gelu_pull(grad_hidden)
    grad_gate_low = grad_gate_pre.astype(jnp.bfloat16)
    grad_up_low = grad_up_pre.astype(jnp.bfloat16)
    grad_gate = weight_grad(normed_f, grad_gate_low)
    grad_up = weight_grad(normed_f, grad_up_low)
    grad_normed = input_grad(grad_gate_low, gate_w) + input_grad(grad_up_low, up_w)
    grad_input, grad_gain_f = rms_backward(after_cross, gain_f, grad_normed)
    grad_res = grad_res + grad_input
    gain_c, wq_c, wk_c, wv_c, wo_c = get_cross()
    grad_branch = grad_res.astype(jnp.bfloat16)
    grad_wo_c = weight_grad(mix_c, grad_branch)
    grad_mix = input_grad(grad_branch, wo_c).astype(jnp.bfloat16)
    grad_query, grad_keys, grad_values = attend_backward(
        query_c, keys_c, values_c, cross_ok, grad_mix
    )
    grad_wq_c = weight_grad(normed_c, grad_query)
    grad_wk_c = weight_grad(enc_rows, grad_keys)
    grad_wv_c = weight_grad(enc_rows, grad_values)
    grad_enc_rows = input_grad(grad_keys, wk_c) + input_grad(grad_values, wv_c)
    grad_normed = input_grad(grad_query, wq_c)
    grad_input, grad_gain_c = rms_backward(after_self, gain_c, grad_normed)
    grad_res = grad_res + grad_input
    gain_a, wq_a, wk_a, wv_a, wo_a = get_self()
    grad_branch = grad_res.astype(jnp.bfloat16)
    grad_wo_a = weight_grad(mix_a, grad_branch)
    grad_mix = input_grad(grad_branch, wo_a).astype(jnp.bfloat16)
    grad_query, grad_keys, grad_values = attend_backward(
        query_a, keys_a, values_a, self_ok, grad_mix
    )
    grad_wq_a = weight_grad(normed_a, grad_query)
    grad_wk_a = weight_grad(normed_a, grad_keys)
    grad_wv_a = weight_grad(normed_a, grad_values)
    grad_normed = (
        input_grad(grad_query, wq_a) + input_grad(grad_keys, wk_a) + input_grad(grad_values, wv_a)
    )
    grad_input, grad_gain_a = rms_backward(dec_float, gain_a, grad_normed)
    grad_dec_rows = grad_res + grad_input
    full_grads = (
        grad_gain_a,
        grad_wq_a,
        grad_wk_a,
        grad_wv_a,
        grad_wo_a,
        grad_gain_c,
        grad_wq_c,
        grad_wk_c,
        grad_wv_c,
        grad_wo_c,
        grad_gain_f,
        grad_gate,
        grad_up,
        grad_down,
    )
    return (dec_result, grad_dec_rows, grad_enc_rows, full_grads)


def dot_nn(left, right):
    return lax.dot_general(left, right, (((1,), (0,)), ((), ())), preferred_element_type=jnp.float32)


def dot_nt(left, right):
    return lax.dot_general(left, right, (((1,), (1,)), ((), ())), preferred_element_type=jnp.float32)


def dot_tn(left, right):
    return lax.dot_general(left, right, (((0,), (0,)), ((), ())), preferred_element_type=jnp.float32)


def flip(index, step):
    return index + step - 2 * step * ((index // step) % 2)


class Place:
    def __init__(self):
        self.dp = lax.axis_index("dp")
        self.fs = lax.axis_index("fsdp")
        self.core = self.fs % 2
        self.x = (self.fs // 2) % 2
        self.y = (self.fs // 4) % 2
        self.inner = (self.dp * (3 - self.dp)) // 2

    def to_core(self):
        return (self.dp, flip(self.fs, 1))

    def to_x(self):
        return (self.dp, flip(self.fs, 2))

    def to_y(self):
        return (self.dp, flip(self.fs, 4))

    def to_pair(self):
        return (flip(self.dp, 1), self.fs)

    def to_middle(self):
        return (3 - self.dp, self.fs)


def remote(source, target, send_sem, recv_sem, device):
    return pltpu.make_async_remote_copy(
        src_ref=source,
        dst_ref=target,
        send_sem=send_sem,
        recv_sem=recv_sem,
        device_id=device,
        device_id_type=pl.DeviceIdType.MESH,
    )


def greet(devices):
    barrier = pltpu.get_barrier_semaphore()
    for device in devices:
        pl.semaphore_signal(
            barrier, inc=1, device_id=device, device_id_type=pl.DeviceIdType.MESH
        )


LINK_BYTES_PER_US = 45000.0
WINDOW = 8
QUARTERS = 4
SQUARE_RING = 2
PLANE_WINDOW_US = 5.0
WORK_SCALE = 1.0
GATHER_DELAY, REST_DELAY, WHOLE_DELAY = 2.5, 5.5, 4.5
CORE_DELAY, PLANE_DELAY, COLUMN_DELAY = 1.0, 2.5, 2.5
PAIRED = (("wide", 1), ("wide", 3), ("square", 0), ("square", 2), ("square", 4))
LAST_PARTS = 3
HALF = jnp.bfloat16
FULL = jnp.float32


class Events:
    def __init__(self):
        self.now = 0.0
        self.heap = []
        self.count = 0
        self.free = {}
        self.plane_load = 0.0
        self.plane_queue = []

    def enter_plane(self, unit=None):
        if unit is not None:
            self.plane_queue.append(unit)
        while self.plane_queue and self.plane_load < PLANE_WINDOW_US:
            unit = self.plane_queue.pop(0)
            self.plane_load += unit.half_us
            unit.cross_plane()

    def leave_plane(self, unit):
        self.plane_load -= unit.half_us
        self.enter_plane()

    def post(self, ready, action):
        self.count += 1
        heapq.heappush(self.heap, (ready, self.count, action))

    def sent(self, links, micros, delay):
        ends = []
        for link in links:
            start = max(self.now, self.free.get(link, 0.0))
            self.free[link] = start + micros
            ends.append(start + micros + delay)
        return max(ends)

    def step(self):
        ready, _, action = heapq.heappop(self.heap)
        self.now = max(self.now, ready) + 0.2
        action()

    def until(self, holds):
        while not holds():
            self.step()

    def work(self, micros, action):
        while self.heap and self.heap[0][0] <= self.now:
            self.step()
        action()
        self.now += WORK_SCALE * micros

    def drain(self):
        while self.heap:
            self.step()


class Chunk:
    def __init__(self, events, place, shard, whole, part, micros, sems, stages, ready):
        self.events = events
        self.place = place
        self.shard = shard
        self.whole = whole
        self.start, self.rows, self.cols = part
        self.micros = micros
        self.send_sems, self.recv_sems, self.stage_sems, self.own_sems = sems
        self.stages = stages
        self.ready = ready
        self.following = None
        fs = place.fs
        even = 1 - place.dp % 2
        self.first = even * flip(fs, 2) + (1 - even) * flip(fs, 4)
        self.second = even * flip(fs, 4) + (1 - even) * flip(fs, 2)
        self.cross = flip(flip(fs, 2), 4)
        self.to = [
            (place.dp, self.first),
            (place.dp, self.second),
            place.to_pair(),
            place.to_core(),
        ]

    def own(self):
        return self.shard.at[pl.ds(self.start, self.rows), self.cols]

    def block(self, owner):
        return self.whole.at[pl.ds(owner * self.shard.shape[0] + self.start, self.rows), self.cols]

    def copy(self, flow, owner, own=False):
        return remote(
            self.own() if own else self.block(owner),
            self.block(owner),
            self.send_sems.at[flow],
            self.recv_sems.at[flow],
            self.to[min(flow, 3)],
        )

    def piece(self, ref, index):
        rows = self.rows // len(self.stages)
        return ref.at[pl.ds(index * rows, rows)] if len(self.stages) > 1 else ref

    def stage(self):
        return [
            pltpu.make_async_copy(self.piece(self.own(), index), held, self.stage_sems.at[index])
            for index, held in enumerate(self.stages)
        ]

    def keep(self):
        block = self.block(self.place.fs)
        return [
            pltpu.make_async_copy(held, self.piece(block, index), self.own_sems.at[index])
            for index, held in enumerate(self.stages)
        ]

    def begin(self):
        self.copy(0, self.place.fs, own=True).start()
        self.copy(3, self.place.fs, own=True).start()
        self.events.post(self.events.sent(["gather first"], self.micros, GATHER_DELAY), self.relay_first)

    def relay_first(self):
        self.copy(0, self.first).wait_recv()
        self.copy(1, self.first).start()
        self.copy(2, self.first).start()
        self.copy(4, self.first).start()
        if self.following is not None:
            self.following.begin()
        self.events.post(self.events.sent(["gather second"], self.micros, REST_DELAY), self.relay_rest)

    def relay_rest(self):
        self.copy(1, self.cross).wait_recv()
        self.copy(5, self.cross).start()
        self.copy(2, self.second).wait_recv()
        self.copy(6, self.second).start()
        self.events.post(self.events.now + WHOLE_DELAY, self.finish)

    def finish(self):
        for flow, owner in ((3, self.place.fs), (4, self.first), (5, self.cross), (6, self.second)):
            self.copy(flow, flip(owner, 1)).wait_recv()
        self.ready()

    def drain(self):
        fs = self.place.fs
        owners = (fs, self.first, self.first, fs, self.first, self.cross, self.second)
        for flow in range(7):
            self.copy(flow, owners[flow], own=flow in (0, 3)).wait_send()


class Reduction:
    plane_flows = (1, 2, 3, 4)

    def __init__(self, events, place, buffers, sems, rows, cols, itemsize, finish):
        self.events = events
        self.place = place
        self.outgoing, self.first, self.along_x, self.along_y = buffers[0:4]
        self.second, self.far, self.final = buffers[4:7]
        self.send_sems, self.recv_sems = sems
        self.half_us = rows * cols * itemsize / LINK_BYTES_PER_US
        self.finish = finish
        self.merged = False

    def flows(self):
        at = self.place
        return (
            (self.outgoing.at[1 - at.core], self.first, at.to_core()),
            (self.first.at[:, 1 - at.x, 0], self.along_x, at.to_x()),
            (self.first.at[1 - at.y, :, 1], self.along_y, at.to_y()),
            (self.along_x.at[1 - at.y], self.second.at[0], at.to_y()),
            (self.along_y.at[1 - at.x], self.second.at[1], at.to_x()),
            (self.second, self.final, at.to_pair()),
            (self.second, self.far, at.to_middle()),
            (self.final, self.final, at.to_pair()),
        )

    def copy(self, flow):
        source, target, device = self.flows()[flow]
        return remote(source, target, self.send_sems.at[flow], self.recv_sems.at[flow], device)

    def begin(self):
        self.copy(0).start()
        self.events.post(self.events.sent(["core"], self.half_us * 0.8, CORE_DELAY), self.merge_cores)

    def merge_cores(self):
        at = self.place
        self.copy(0).wait_recv()

        def add(index, carry):
            y, x, half = index // 4, (index // 2) % 2, index % 2
            self.first[y, x, half] = self.first[y, x, half] + self.outgoing[at.core, y, x, half]
            return carry

        lax.fori_loop(0, 8, add, 0)
        self.copy(0).wait_send()
        self.merged = True
        self.events.enter_plane(self)

    def cross_plane(self):
        self.copy(1).start()
        self.copy(2).start()
        self.events.post(self.events.sent(["first", "second"], 2 * self.half_us, PLANE_DELAY), self.merge_first)

    def merge_first(self):
        at = self.place
        self.copy(1).wait_recv()
        self.copy(2).wait_recv()
        for index in range(2):
            self.along_x[index] = self.along_x[index] + self.first[index, at.x, 0]
            self.along_y[index] = self.along_y[index] + self.first[at.y, index, 1]
        self.copy(3).start()
        self.copy(4).start()
        self.events.post(self.events.sent(["first", "second"], self.half_us, PLANE_DELAY), self.merge_second)
        self.events.leave_plane(self)

    def merge_second(self):
        at = self.place
        self.copy(3).wait_recv()
        self.copy(4).wait_recv()
        self.second[0] = self.second[0] + self.along_x[at.y]
        self.second[1] = self.second[1] + self.along_y[at.x]
        self.enter_column()

    def enter_column(self):
        at = self.place

        @pl.when(at.inner == 0)
        def _():
            self.copy(5).start()

        self.events.post(self.events.sent(["z"], 2 * self.half_us, COLUMN_DELAY), self.merge_near)

    def merge_near(self):
        @pl.when(self.place.inner == 1)
        def _():
            self.copy(5).wait_recv()
            for half in range(2):
                self.second[half] = self.second[half] + self.final[half]
            self.copy(6).start()

        self.events.post(self.events.sent(["z middle"], 2 * self.half_us, COLUMN_DELAY), self.merge_far)

    def merge_far(self):
        @pl.when(self.place.inner == 1)
        def _():
            self.copy(6).wait_recv()
            for half in range(2):
                self.final[half] = self.second[half] + self.far[half]
            self.copy(7).start()

        self.events.post(self.events.sent(["z back"], 2 * self.half_us, COLUMN_DELAY), self.complete)

    def complete(self):
        @pl.when(self.place.inner == 0)
        def _():
            self.copy(7).wait_recv()

        self.finish(self.final)

    def drain(self):
        for flow in self.plane_flows:
            self.copy(flow).wait_send()

        @pl.when(self.place.inner == 0)
        def _():
            self.copy(5).wait_send()

        @pl.when(self.place.inner == 1)
        def _():
            self.copy(6).wait_send()
            self.copy(7).wait_send()


class PairReduction(Reduction):
    plane_flows = (1, 2, 3)

    def chips(self):
        at = self.place
        odd = at.dp % 2
        even = 1 - odd
        first = (even * at.y + odd * (1 - at.y), even * (1 - at.x) + odd * at.x)
        second = (1 - first[0], 1 - first[1])
        return first, second, (1 - at.y, 1 - at.x)

    def flows(self):
        at = self.place
        even = 1 - at.dp % 2
        first, second, opposite = self.chips()
        to_first = (at.dp, even * flip(at.fs, 2) + (1 - even) * flip(at.fs, 4))
        to_second = (at.dp, even * flip(at.fs, 4) + (1 - even) * flip(at.fs, 2))
        base = super().flows()
        return (
            base[0],
            (self.first.at[opposite[0], opposite[1]], self.along_x, to_second),
            (self.first.at[second[0], second[1]], self.along_y, at.to_pair()),
            (self.along_x, self.second, to_first),
            None,
            *base[5:],
        )

    def cross_plane(self):
        self.copy(1).start()
        self.copy(2).start()
        self.events.post(self.events.sent(["second", "z"], 2 * self.half_us, PLANE_DELAY), self.merge_first)

    def merge_first(self):
        self.copy(1).wait_recv()
        self.copy(2).wait_recv()
        first = self.chips()[0]
        for half in range(2):
            self.along_x[half] = (
                self.along_x[half] + self.along_y[half] + self.first[first[0], first[1], half]
            )
        self.copy(3).start()
        self.events.post(self.events.sent(["first"], 2 * self.half_us, PLANE_DELAY), self.merge_second)
        self.events.leave_plane(self)

    def merge_second(self):
        at = self.place
        self.copy(3).wait_recv()
        for half in range(2):
            self.second[half] = self.second[half] + self.first[at.y, at.x, half]
        self.enter_column()


def norm_rows(source, gain, target, rows, step):
    def body(index, carry):
        block = pl.ds(pl.multiple_of(index * step, step), step)
        values = source[block, :].astype(FULL)
        scale = lax.rsqrt(jnp.mean(values * values, axis=-1, keepdims=True) + EPSILON)
        target[block, :] = (values * scale * gain).astype(target.dtype)
        return carry

    lax.fori_loop(0, rows // step, body, 0)


def norm_back(source, gain, grad_norm, residual, low, rows, step):
    def body(index, total):
        block = pl.ds(pl.multiple_of(index * step, step), step)
        values = source[block, :].astype(FULL)
        scale = lax.rsqrt(jnp.mean(values * values, axis=-1, keepdims=True) + EPSILON)
        unit = values * scale
        grad = grad_norm[block, :]
        scaled = grad * gain
        change = scale * (scaled - unit * jnp.mean(scaled * unit, axis=-1, keepdims=True))
        updated = residual[block, :] + change
        residual[block, :] = updated
        low[block, :] = updated.astype(low.dtype)
        product = grad * unit
        for start in range(0, step, 8):
            total = total + product[start : start + 8]
        return total

    total = lax.fori_loop(0, rows // step, body, jnp.zeros((8, MODEL), FULL))
    return jnp.sum(total, axis=0, keepdims=True)


def make_masks(seg_dec, seg_enc, mask_self, mask_cross):
    rows, length = seg_dec.shape
    query = lax.broadcasted_iota(jnp.int32, (length, length), 0)
    key = lax.broadcasted_iota(jnp.int32, (length, length), 1)
    for row in range(rows):
        along = seg_dec[row : row + 1, :].astype(FULL)
        down = jnp.sum(jnp.where(query == key, along, 0.0), axis=1, keepdims=True)
        mask_self[row] = jnp.where((down == along) & (key <= query), 1.0, 0.0)
        enc = seg_enc[row : row + 1, :].astype(FULL)
        mask_cross[row] = jnp.where(down == enc, 1.0, 0.0)


class Heads:
    def __init__(self, queries, keys, values, mask, len_q, len_k, width):
        self.queries, self.keys, self.values, self.mask = queries, keys, values, mask
        self.len_q, self.len_k, self.width = len_q, len_k, width
        self.pairs = MODEL // (2 * HD)

    def lower(self, shape):
        return lax.broadcasted_iota(jnp.int32, shape, 1) < HD

    def stack(self, both):
        lower = self.lower((1, 2 * HD)).astype(FULL)
        upper = 1.0 - lower
        return jnp.concatenate([both * lower.astype(HALF), both * upper.astype(HALF)], axis=0)

    def join(self, stacked):
        top, bottom = stacked[: self.len_q], stacked[self.len_q :]
        return jnp.where(self.lower(top.shape), top, bottom)

    def places(self, step):
        found = []
        for near in range(self.width):
            index = step * self.width + near
            row, pair = index // self.pairs, index % self.pairs
            cols = pl.ds(pl.multiple_of(pair * 2 * HD, 2 * HD), 2 * HD)
            at_q = pl.ds(pl.multiple_of(row * self.len_q, 16), self.len_q)
            at_k = pl.ds(pl.multiple_of(row * self.len_k, 16), self.len_k)
            found.append((row, at_q, at_k, cols))
        return found

    def probs(self, rows, queries, keys):
        scores = [dot_nt(query, key) for query, key in zip(queries, keys)]
        split = (2, self.len_q, self.len_k)
        scores = [
            jnp.where(self.mask[row][None] > 0.0, score.reshape(split), MASKED)
            for row, score in zip(rows, scores)
        ]
        scores = [score.reshape(2 * self.len_q, self.len_k) for score in scores]
        powers = [jnp.exp(score - jnp.max(score, axis=-1, keepdims=True)) for score in scores]
        return [power * (1.0 / jnp.sum(power, axis=-1, keepdims=True)) for power in powers]

    def forward(self, target, first, last):
        def body(step, carry):
            places = self.places(step)
            rows = [place[0] for place in places]
            queries = [self.stack(self.queries[at_q, cols]) for _, at_q, _, cols in places]
            keys = [self.keys[at_k, cols] for _, _, at_k, cols in places]
            values = [self.values[at_k, cols] for _, _, at_k, cols in places]
            probs = self.probs(rows, queries, keys)
            mixed = [dot_nn(prob.astype(HALF), value) for prob, value in zip(probs, values)]
            for (_, at_q, _, cols), mix in zip(places, mixed):
                target[at_q, cols] = self.join(mix).astype(HALF)
            return carry

        lax.fori_loop(first // self.width, last // self.width, body, 0)

    def backward(self, grads, first, last):
        def body(step, carry):
            places = self.places(step)
            rows = [place[0] for place in places]
            queries = [self.stack(self.queries[at_q, cols]) for _, at_q, _, cols in places]
            keys = [self.keys[at_k, cols] for _, _, at_k, cols in places]
            values = [self.values[at_k, cols] for _, _, at_k, cols in places]
            grad = [self.stack(grads[at_q, cols]) for _, at_q, _, cols in places]
            each = range(self.width)
            grad_p = [dot_nt(grad[i], values[i]) for i in each]
            probs = self.probs(rows, queries, keys)
            grad_v = [dot_tn(probs[i].astype(HALF), grad[i]) for i in each]
            inner = [jnp.sum(probs[i] * grad_p[i], axis=-1, keepdims=True) for i in each]
            grad_s = [(probs[i] * (grad_p[i] - inner[i])).astype(HALF) for i in each]
            grad_q = [self.join(dot_nn(grad_s[i], keys[i])) * HD ** (-0.5) for i in each]
            grad_k = [dot_tn(grad_s[i], queries[i]) for i in each]
            for i, (_, at_q, at_k, cols) in enumerate(places):
                self.queries[at_q, cols] = grad_q[i].astype(HALF)
                self.keys[at_k, cols] = grad_k[i].astype(HALF)
                self.values[at_k, cols] = grad_v[i].astype(HALF)
            return carry

        lax.fori_loop(first // self.width, last // self.width, body, 0)


GELU_SCALE = (2.0 / math.pi) ** 0.5


def gelu_rows(gate_pre, up_pre, grad_hidden, hidden, grad_gate, grad_up, rows, step):
    def body(index, carry):
        block = pl.ds(pl.multiple_of(index * step, step), step)
        gate, up, grad = gate_pre[block, :], up_pre[block, :], grad_hidden[block, :]
        square = gate * gate
        bend = jnp.tanh(GELU_SCALE * gate * (1.0 + 0.044715 * square))
        rise = 0.5 * (1.0 + bend)
        value = gate * rise
        slope = rise + 0.5 * gate * (1.0 - bend * bend) * GELU_SCALE * (1.0 + 3 * 0.044715 * square)
        hidden[block, :] = (value * up).astype(HALF)
        grad_gate[block, :] = (grad * up * slope).astype(HALF)
        grad_up[block, :] = (grad * value).astype(HALF)
        return carry

    lax.fori_loop(0, rows // step, body, 0)


WQ_A, WK_A, WV_A, WO_A, WK_C, WV_C, WQ_C, WO_C, GATE, UP, DOWN, GAINS = range(12)
GATHER_ORDER = (WK_C, WQ_A, WK_A, WV_A, WO_A, WV_C, WQ_C, WO_C)
SLOTS = {WK_C: 1, WQ_A: 0, WK_A: 3, WV_A: 2, WO_A: 4, WV_C: 2, WQ_C: 3, WO_C: 0}
SLOTS_BACK = {WQ_A: 0, WK_A: 3, WV_A: 4}


def layer_kernel(dims, *refs):
    rows, len_q, len_k, count = dims
    tokens = rows * len_q
    shards, gain_shards = refs[0:11], refs[11:14]
    dec_hbm, enc_hbm, grad_hbm, seg_dec, seg_enc = refs[14:19]
    whole = refs[19:30]
    dec_out, grad_dec_out, grad_enc_out, gate_out, up_out, down_out, square_out, gain_out = refs[30:38]
    (gate_w, up_w, down_w, square_w, small, large, floats, enc, grad_low) = refs[38:47]
    (gain_tile, gains, mask_self, mask_cross, gate_pre, up_pre, grad_hidden) = refs[47:54]
    (hidden, grad_gate, grad_up, grad_norm, result, grad_mix, gain_grads) = refs[54:61]
    residual = result
    dec = grad_mix
    wide_bufs, tall_bufs, square_bufs, gain_bufs = refs[61:68], refs[68:75], refs[75:82], refs[82:89]
    last_bufs = refs[89:96]
    gather_send, gather_recv, stage_sems, own_sems, send_sems, recv_sems = refs[96:102]
    load_sems, weight_sems, store_sems = refs[102:105]

    place = Place()
    events = Events()
    loads = {}
    stores = []
    ff_part = whole[DOWN].shape[0] // QUARTERS
    pairs_all = rows * (MODEL // (2 * HD))

    def load(name, source, target, sem):
        loads[name] = pltpu.make_async_copy(source, target, sem)
        loads[name].start()

    def store(source, target):
        stores.append(pltpu.make_async_copy(source, target, store_sems.at[len(stores)]))
        stores[-1].start()

    neighbours = [
        place.to_core(), place.to_x(), place.to_y(), place.to_pair(), place.to_middle()
    ]
    greet(neighbours)
    load("dec", dec_hbm, dec, load_sems.at[0])
    load("enc", enc_hbm, enc, load_sems.at[1])
    load("grad", grad_hbm, grad_low, load_sems.at[2])
    gain_tile[...] = jnp.zeros(gain_tile.shape, FULL)
    for which, shard in enumerate(gain_shards):
        gain_tile[which : which + 1, 0 : shard.shape[1]] = shard[...].astype(FULL)

    gathered = {}
    slot_free = {slot: True for slot in range(5)}
    waiting = []

    def try_loads():
        for entry in list(waiting):
            ready, slot, start = entry
            if ready() and slot_free[slot]:
                slot_free[slot] = False
                start()
                waiting.remove(entry)

    def want(name, ready, slot, start):
        slot_free.setdefault(slot, True)
        waiting.append((ready, slot, start))
        try_loads()

    def release(slot):
        slot_free[slot] = True
        try_loads()

    def want_square(which, slot, name):
        want(
            name,
            lambda: gathered.get(which, False),
            slot,
            lambda: load(name, whole[which], square_w.at[slot], weight_sems.at[slot]),
        )

    def want_quarter(quarter):
        slot = quarter % 2
        part = pl.ds(quarter * ff_part, ff_part)

        def start():
            load(("gate", quarter), whole[GATE].at[:, part], gate_w.at[slot], weight_sems.at[5 + slot])
            load(("up", quarter), whole[UP].at[:, part], up_w.at[slot], weight_sems.at[7 + slot])
            load(("down", quarter), whole[DOWN].at[part], down_w.at[slot], weight_sems.at[9 + slot])

        want(
            ("quarter", quarter),
            lambda: gathered.get(DOWN, False) and gathered.get((UP, quarter), False),
            ("ffn", slot),
            start,
        )

    for which in GATHER_ORDER:
        want_square(which, SLOTS[which], ("square", which))
    for quarter in range(QUARTERS):
        want_quarter(quarter)

    def need(name):
        events.until(lambda: name in loads)
        loads[name].wait()

    chunks = []

    def add_chunk(shard, target, start, height, cols, name, stages):
        index = len(chunks)
        width = cols.size if cols is not None else shard.shape[1]
        itemsize = jnp.dtype(shard.dtype).itemsize

        def ready():
            if name is not None:
                gathered[name] = True
                try_loads()

        chunks.append(
            Chunk(
                events,
                place,
                shard,
                target,
                (start, height, slice(None) if cols is None else cols),
                height * width * itemsize / LINK_BYTES_PER_US,
                (
                    gather_send.at[index],
                    gather_recv.at[index],
                    stage_sems.at[index],
                    own_sems.at[index],
                ),
                stages,
                ready,
            )
        )

    add_chunk(gain_tile, gains, 0, 8, None, GAINS, [gain_bufs[0].at[0, 0, 0, 0, 0]])
    for index, which in enumerate(GATHER_ORDER):
        held = square_bufs[0].at[0, index // 4, (index // 2) % 2, index % 2]
        add_chunk(
            shards[which],
            whole[which],
            0,
            shards[which].shape[0],
            None,
            which,
            [held.at[0], held.at[1]],
        )
    down_rows = shards[DOWN].shape[0]
    for part in range(4):
        piece = down_rows // 4
        add_chunk(
            shards[DOWN],
            whole[DOWN],
            part * piece,
            piece,
            None,
            DOWN if part == 3 else None,
            [tall_bufs[0].at[0, 0, 0, part // 2, part % 2]],
        )
    for quarter in range(QUARTERS):
        for which in (GATE, UP):
            add_chunk(
                shards[which],
                whole[which],
                0,
                shards[which].shape[0],
                pl.ds(quarter * ff_part, ff_part),
                (which, quarter),
                [wide_bufs[0].at[0, 0, quarter // 2, quarter % 2, which - GATE]],
            )
    for index, chunk in enumerate(chunks):
        if index + WINDOW < len(chunks):
            chunk.following = chunks[index + WINDOW]
    for chunk in chunks:
        for copy in chunk.stage():
            copy.start()
    pl.semaphore_wait(pltpu.get_barrier_semaphore(), len(neighbours))
    for chunk in chunks[:WINDOW]:
        chunk.begin()
    for chunk in chunks:
        for staged, kept in zip(chunk.stage(), chunk.keep()):
            staged.wait()
            kept.start()

    def gain_row(which):
        width = MODEL // count
        return jnp.concatenate(
            [gains[8 * owner + which : 8 * owner + which + 1, 0:width] for owner in range(count)],
            axis=1,
        )

    def masks():
        make_masks(seg_dec, seg_enc, mask_self, mask_cross)
        gain_grads[...] = jnp.zeros(gain_grads.shape, FULL)
        loads["dec"].wait()
        for chunk in chunks:
            for kept in chunk.keep():
                kept.wait()

    def project(acts, which, target, scale=None, free=True):
        name = ("square", which)
        need(name)

        def run():
            value = dot_nn(acts[...], square_w[SLOTS[which]])
            if scale is not None:
                value = value * scale
            target[...] = value.astype(target.dtype)
            if free:
                release(SLOTS[which])

        events.work(0.6 * acts.shape[0] / tokens, run)

    def residual_add(before, acts, which, after, free):
        need(("square", which))

        def run():
            after[...] = before[...].astype(FULL) + dot_nn(acts[...], square_w[SLOTS[which]])

        events.work(0.8, run)

    def norm(source, which, target):
        events.work(
            0.4, lambda: norm_rows(source, gain_row(which), target, tokens, len_q)
        )

    def attend(heads, target, parts, micros):
        for part in range(parts):
            bounds = (part * pairs_all // parts, (part + 1) * pairs_all // parts)
            events.work(micros / parts, functools.partial(heads.forward, target, *bounds))

    self_heads = Heads(small.at[1], small.at[2], small.at[3], mask_self, len_q, len_q, 3)
    cross_heads = Heads(small.at[6], large.at[0], large.at[1], mask_cross, len_q, len_k, 2)
    root = HD ** (-0.5)

    events.work(0.5, masks)
    events.until(lambda: GAINS in gathered)
    norm(dec, 0, small.at[0])
    loads["enc"].wait()
    project(enc, WK_C, large.at[0], free=False)
    project(small.at[0], WQ_A, small.at[1], scale=root)
    project(small.at[0], WK_A, small.at[2])
    project(small.at[0], WV_A, small.at[3])
    attend(self_heads, small.at[4], 2, 2.6)
    residual_add(dec, small.at[4], WO_A, floats.at[0], False)
    norm(floats.at[0], 1, small.at[5])
    project(enc, WV_C, large.at[1], free=False)
    project(small.at[5], WQ_C, small.at[6], scale=root, free=False)
    attend(cross_heads, small.at[7], 3, 5.4)
    residual_add(floats.at[0], small.at[7], WO_C, floats.at[1], False)
    norm(floats.at[1], 2, small.at[8])
    loads["grad"].wait()

    units = []

    def unit_of(buffers, index, slot, finish, paired=False):
        number = len(units)
        final = buffers[6]
        unit = (PairReduction if paired else Reduction)(
            events,
            place,
            (buffers[0].at[slot], *(buffer.at[index] for buffer in buffers[1:7])),
            (send_sems.at[number], recv_sems.at[number]),
            final.shape[-2],
            final.shape[-1],
            jnp.dtype(final.dtype).itemsize,
            finish,
        )
        units.append(unit)
        return unit

    def claim(earlier):
        events.until(lambda: earlier.merged)

    wide_units = []

    def ffn_forward(quarter):
        slot = quarter % 2
        gate_pre[...] = dot_nn(small[8], gate_w[slot])
        up_pre[...] = dot_nn(small[8], up_w[slot])
        grad_hidden[...] = dot_nt(grad_low[...], down_w[slot])

    def ffn_gelu():
        gelu_rows(gate_pre, up_pre, grad_hidden, hidden, grad_gate, grad_up, tokens, len_q)

    def ffn_wide(quarter):
        def finish(final):
            part = pl.ds(quarter * ff_part, ff_part)
            store(final.at[0], gate_out.at[:, part])
            store(final.at[1], up_out.at[:, part])

        unit = unit_of(wide_bufs, quarter, 0, finish, ("wide", quarter) in PAIRED)
        wide_units.append(unit)
        height = MODEL // count
        for half, grads in enumerate((grad_gate, grad_up)):
            value = dot_tn(small[8], grads[...]).astype(HALF)
            for owner in range(count):
                unit.outgoing[owner % 2, owner // 4, (owner // 2) % 2, half] = value[
                    owner * height : (owner + 1) * height
                ]
        unit.begin()

    def ffn_tall(quarter):
        value = dot_tn(hidden[...], grad_low[...]).astype(HALF)
        owners = count // QUARTERS
        height = ff_part // owners
        piece = height // 4
        for near in range(owners):
            owner = quarter * owners + near
            for part in range(4):
                start = near * height + part * piece
                tall_bufs[0][part // 2, owner % 2, owner // 4, (owner // 2) % 2, part % 2] = value[
                    start : start + piece
                ]

    def ffn_rest(quarter):
        slot = quarter % 2
        change = dot_nt(grad_gate[...], gate_w[slot]) + dot_nt(grad_up[...], up_w[slot])
        output = dot_nn(hidden[...], down_w[slot])
        if quarter == 0:
            grad_norm[...] = change
            result[...] = floats[1] + output
        else:
            grad_norm[...] += change
            result[...] += output
        release(("ffn", slot))

    for quarter in range(QUARTERS):
        for kind in ("gate", "up", "down"):
            need((kind, quarter))
        events.work(1.1, functools.partial(ffn_forward, quarter))
        events.work(0.2, ffn_gelu)
        if quarter >= 1:
            claim(wide_units[quarter - 1])
        events.work(1.1, functools.partial(ffn_wide, quarter))
        events.work(0.8, functools.partial(ffn_tall, quarter))
        events.work(1.2, functools.partial(ffn_rest, quarter))

    def start_tall():
        for part in range(2):

            def finish(final, part=part):
                piece = final.shape[1]
                for half in range(2):
                    store(final.at[half], down_out.at[pl.ds((2 * part + half) * piece, piece)])

            unit_of(tall_bufs, part, part, finish).begin()

    def ffn_norm():
        small[8] = result[...].astype(HALF)
        store(small.at[8], dec_out)
        residual[...] = grad_low[...].astype(FULL)
        gain_grads[2:3, :] = norm_back(
            floats.at[1], gain_row(2), grad_norm, residual, grad_low, tokens, len_q
        )

    events.work(0.1, start_tall)
    events.work(1.0, ffn_norm)

    square_units = []

    def square_grad(which, acts, grads):
        index = len(square_units)
        height = MODEL // count

        def finish(final):
            piece = final.shape[1]
            for half in range(2):
                store(final.at[half], square_out.at[which, pl.ds(half * piece, piece)])

        if index >= SQUARE_RING:
            claim(square_units[index - SQUARE_RING])
        unit = unit_of(
            square_bufs, index, index % SQUARE_RING, finish, ("square", index) in PAIRED
        )
        square_units.append(unit)

        def compute():
            value = dot_tn(acts[...], grads[...]).astype(HALF)
            piece = height // 2
            for owner in range(count):
                for half in range(2):
                    start = owner * height + half * piece
                    unit.outgoing[owner % 2, owner // 4, (owner // 2) % 2, half] = value[
                        start : start + piece
                    ]
            unit.begin()

        events.work(0.9 if acts.shape[0] == tokens else 1.5, compute)

    last_units = []

    def last_grad(which, acts, grads):
        index = len(last_units)
        height = MODEL // count
        piece = height // 2
        width = MODEL // LAST_PARTS
        parts = []
        for part in range(LAST_PARTS):
            cols = pl.ds(part * width, width)

            def finish(final, cols=cols):
                for half in range(2):
                    store(final.at[half], square_out.at[which, pl.ds(half * piece, piece), cols])

            if index:
                claim(last_units[index - LAST_PARTS + part])
            parts.append(unit_of(last_bufs, index + part, part, finish))
        last_units.extend(parts)

        def compute():
            value = dot_tn(acts[...], grads[...]).astype(HALF)
            for part, unit in enumerate(parts):
                for owner in range(count):
                    for half in range(2):
                        start = owner * height + half * piece
                        unit.outgoing[owner % 2, owner // 4, (owner // 2) % 2, half] = value[
                            start : start + piece, part * width : (part + 1) * width
                        ]
                unit.begin()

        events.work(1.0, compute)

    def mix_grad(which):
        def run():
            grad_mix[...] = dot_nt(grad_low[...], square_w[SLOTS[which]]).astype(HALF)
            release(SLOTS[which])

        events.work(0.8, run)

    def attend_back(heads, parts, micros):
        for part in range(parts):
            bounds = (part * pairs_all // parts, (part + 1) * pairs_all // parts)
            events.work(micros / parts, functools.partial(heads.backward, grad_mix, *bounds))

    square_grad(WO_C, small.at[7], grad_low)
    mix_grad(WO_C)
    want_square(WQ_A, SLOTS_BACK[WQ_A], ("back", WQ_A))
    attend_back(cross_heads, 6, 10.0)
    square_grad(WK_C, enc, large.at[0])
    square_grad(WV_C, enc, large.at[1])
    square_grad(WQ_C, small.at[5], small.at[6])

    def cross_norm():
        grad_norm[...] = dot_nt(small[6], square_w[SLOTS[WQ_C]])
        release(SLOTS[WQ_C])
        gain_grads[1:2, :] = norm_back(
            floats.at[0], gain_row(1), grad_norm, residual, grad_low, tokens, len_q
        )

    events.work(1.3, cross_norm)
    want_square(WK_A, SLOTS_BACK[WK_A], ("back", WK_A))

    square_grad(WO_A, small.at[4], grad_low)
    mix_grad(WO_A)
    want_square(WV_A, SLOTS_BACK[WV_A], ("back", WV_A))
    attend_back(self_heads, 2, 4.8)
    load("dec again", dec_hbm, dec, load_sems.at[0])
    last_grad(WQ_A, small.at[0], small.at[1])
    last_grad(WK_A, small.at[0], small.at[2])
    last_grad(WV_A, small.at[0], small.at[3])

    def self_norm():
        total = None
        loads["dec again"].wait()
        for index, which in enumerate((WQ_A, WK_A, WV_A)):
            need(("back", which))
            part = dot_nt(small[1 + index], square_w[SLOTS_BACK[which]])
            total = part if total is None else total + part
        grad_norm[...] = total
        gain_grads[0:1, :] = norm_back(
            dec, gain_row(0), grad_norm, residual, grad_low, tokens, len_q
        )
        store(grad_low, grad_dec_out)
        width = MODEL // count
        unit = unit_of(gain_bufs, 0, 0, lambda final: store(final, gain_out))
        unit.outgoing[...] = jnp.zeros(unit.outgoing.shape, FULL)
        for owner in range(count):
            unit.outgoing[owner % 2, owner // 4, (owner // 2) % 2, 0, :, 0:width] = gain_grads[
                :, owner * width : (owner + 1) * width
            ]
        unit.begin()

    events.work(2.5, self_norm)

    def enc_grad(part):
        block = pl.ds(part * (enc.shape[0] // 2), enc.shape[0] // 2)
        value = dot_nt(large[0, block], square_w[SLOTS[WK_C]])
        value = value + dot_nt(large[1, block], square_w[SLOTS[WV_C]])
        enc[block, :] = value.astype(HALF)
        store(enc.at[block], grad_enc_out.at[block])

    for part in range(2):
        events.work(1.5, functools.partial(enc_grad, part))
    events.drain()
    for chunk in chunks:
        chunk.drain()
    for unit in units:
        unit.drain()
    for copy in stores:
        copy.wait()


def layer_call(shards, gain_shards, dec, enc, grad, seg_dec, seg_enc):
    rows, len_q = seg_dec.shape
    len_k = seg_enc.shape[1]
    count = lax.axis_size("fsdp")
    tokens, enc_tokens = rows * len_q, rows * len_k
    hidden_units = shards[DOWN].shape[0] * count
    ff_part = hidden_units // QUARTERS
    height = MODEL // count
    down_height = hidden_units // count
    in_any = pl.BlockSpec(memory_space=pl.ANY)
    in_vmem = pl.BlockSpec(memory_space=pltpu.VMEM)

    def buffers(number, ring, height, width, kind):
        return [
            pltpu.VMEM((ring, 2, 2, 2, 2, height, width), kind),
            pltpu.VMEM((number, 2, 2, 2, height, width), kind),
            *[pltpu.VMEM((number, 2, height, width), kind)] * 5,
        ]

    n_chunks = 1 + 8 + 4 + 2 * QUARTERS
    n_units = QUARTERS + 2 + 5 + 3 * LAST_PARTS + 1
    wholes = [
        jax.ShapeDtypeStruct((shard.shape[0] * count, shard.shape[1]), shard.dtype)
        for shard in shards
    ]
    results = pl.pallas_call(
        functools.partial(layer_kernel, (rows, len_q, len_k, count)),
        out_shape=wholes
        + [
            jax.ShapeDtypeStruct((tokens, MODEL), HALF),
            jax.ShapeDtypeStruct((tokens, MODEL), HALF),
            jax.ShapeDtypeStruct((enc_tokens, MODEL), HALF),
            jax.ShapeDtypeStruct((height, hidden_units), HALF),
            jax.ShapeDtypeStruct((height, hidden_units), HALF),
            jax.ShapeDtypeStruct((down_height, MODEL), HALF),
            jax.ShapeDtypeStruct((8, height, MODEL), HALF),
            jax.ShapeDtypeStruct((2, 8, 128), FULL),
        ],
        in_specs=[in_any] * 11 + [in_vmem] * 3 + [in_any] * 3 + [in_vmem] * 2,
        out_specs=[in_any] * 19,
        scratch_shapes=[
            pltpu.VMEM((2, MODEL, ff_part), HALF),
            pltpu.VMEM((2, MODEL, ff_part), HALF),
            pltpu.VMEM((2, ff_part, MODEL), HALF),
            pltpu.VMEM((5, MODEL, MODEL), HALF),
            pltpu.VMEM((9, tokens, MODEL), HALF),
            pltpu.VMEM((2, enc_tokens, MODEL), HALF),
            pltpu.VMEM((2, tokens, MODEL), FULL),
            pltpu.VMEM((enc_tokens, MODEL), HALF),
            pltpu.VMEM((tokens, MODEL), HALF),
            pltpu.VMEM((8, 128), FULL),
            pltpu.VMEM((8 * count, 128), FULL),
            pltpu.VMEM((rows, len_q, len_q), FULL),
            pltpu.VMEM((rows, len_q, len_k), FULL),
            *[pltpu.VMEM((tokens, ff_part), FULL)] * 3,
            *[pltpu.VMEM((tokens, ff_part), HALF)] * 3,
            pltpu.VMEM((tokens, MODEL), FULL),
            pltpu.VMEM((tokens, MODEL), FULL),
            pltpu.VMEM((tokens, MODEL), HALF),
            pltpu.VMEM((8, MODEL), FULL),
            *buffers(QUARTERS, 1, height, ff_part, HALF),
            *buffers(2, 2, down_height // 4, MODEL, HALF),
            *buffers(5, SQUARE_RING, height // 2, MODEL, HALF),
            *buffers(1, 1, 8, 128, FULL),
            *buffers(3 * LAST_PARTS, LAST_PARTS, height // 2, MODEL // LAST_PARTS, HALF),
            pltpu.SemaphoreType.DMA((n_chunks, 7)),
            pltpu.SemaphoreType.DMA((n_chunks, 7)),
            pltpu.SemaphoreType.DMA((n_chunks, 2)),
            pltpu.SemaphoreType.DMA((n_chunks, 2)),
            pltpu.SemaphoreType.DMA((n_units, 8)),
            pltpu.SemaphoreType.DMA((n_units, 8)),
            pltpu.SemaphoreType.DMA((3,)),
            pltpu.SemaphoreType.DMA((11,)),
            pltpu.SemaphoreType.DMA((46,)),
        ],
        compiler_params=pltpu.CompilerParams(
            collective_id=0,
            has_side_effects=True,
            vmem_limit_bytes=63 * 1024 * 1024 + 512 * 1024,
        ),
        name="layer",
    )(*shards, *gain_shards, dec, enc, grad, seg_dec, seg_enc)
    return results[11:]


def finish_kernel(plan, *refs):
    n_in, n_out = 7, 14
    sources, gain_grads = refs[0:n_in], refs[n_in]
    targets = refs[n_in + 1 : n_in + 1 + n_out]
    gain_targets = refs[n_in + 1 + n_out : n_in + 4 + n_out]
    taken, made = refs[n_in + 4 + n_out : n_in + 6 + n_out]
    in_sems, out_sems = refs[n_in + 6 + n_out :]
    reads, writes = [], []
    for index, (source, source_at, target, target_at, _, _) in enumerate(plan):
        reads.append(
            pltpu.make_async_copy(
                sources[source].at[source_at], taken[index], in_sems.at[index]
            )
        )
        writes.append(
            pltpu.make_async_copy(made[index], targets[target].at[target_at], out_sems.at[index])
        )
    for copy in reads:
        copy.start()
    for index, target in enumerate(gain_targets):
        target[...] = gain_grads[0, index : index + 1, 0 : target.shape[1]]
    for index in range(len(plan)):
        reads[index].wait()
        made[index][...] = taken[index][...].astype(made[index].dtype)
        writes[index].start()
    for copy in writes:
        copy.wait()


def finish_call(results):
    everything = slice(None)
    plan = []

    def add(source, source_at, target, target_at, shape):
        plan.append((source, source_at, target, target_at, *shape))

    enc_rows = results[2].shape[0]
    for part in range(4):
        block = pl.ds(part * enc_rows // 4, enc_rows // 4)
        add(2, (block, everything), 2, (block, everything), (enc_rows // 4, MODEL))
    for index in (3, 4, 5, 1):
        add(index, (everything, everything), index, (everything, everything), results[index].shape)
    for index in range(8):
        add(6, (index, everything, everything), 6 + index, (everything, everything), results[6].shape[1:])
    add(0, (everything, everything), 0, (everything, everything), results[0].shape)
    shapes = [jax.ShapeDtypeStruct(results[0].shape, HALF)]
    shapes += [jax.ShapeDtypeStruct(results[index].shape, FULL) for index in range(1, 6)]
    shapes += [jax.ShapeDtypeStruct(results[6].shape[1:], FULL)] * 8
    gain = results[6].shape[1]
    in_any = pl.BlockSpec(memory_space=pl.ANY)
    in_vmem = pl.BlockSpec(memory_space=pltpu.VMEM)
    return pl.pallas_call(
        functools.partial(finish_kernel, plan),
        out_shape=shapes + [jax.ShapeDtypeStruct((1, gain), FULL)] * 3,
        in_specs=[in_any] * 7 + [in_vmem],
        out_specs=[in_any] * 14 + [in_vmem] * 3,
        scratch_shapes=[
            [pltpu.VMEM(entry[4:6], HALF) for entry in plan],
            [pltpu.VMEM(entry[4:6], HALF if entry[2] == 0 else FULL) for entry in plan],
            pltpu.SemaphoreType.DMA((len(plan),)),
            pltpu.SemaphoreType.DMA((len(plan),)),
        ],
        compiler_params=pltpu.CompilerParams(vmem_limit_bytes=63 * 1024 * 1024),
        name="finish",
    )(*results)


def body(
    dec_in,
    enc_out,
    seg_dec,
    seg_enc,
    out_grad,
    gain_self,
    wq_self,
    wk_self,
    wv_self,
    wo_self,
    gain_cross,
    wq_cross,
    wk_cross,
    wv_cross,
    wo_cross,
    gain_ffn,
    w_gate,
    w_up,
    w_down,
):
    narrow = (wq_self, wk_self, wv_self, wo_self, wq_cross, wk_cross, wv_cross, wo_cross, w_down)
    position = jnp.arange(seg_dec.shape[1])
    causal = position[:, None] >= position[None, :]
    self_ok = (seg_dec[:, :, None] == seg_dec[:, None, :]) & causal[None]
    cross_ok = seg_dec[:, :, None] == seg_enc[:, None, :]
    if lax.axis_size("fsdp") == 8 and lax.axis_size("dp") == 4:
        back = layer_call(
            (wq_self, wk_self, wv_self, wo_self)
            + (wk_cross, wv_cross, wq_cross, wo_cross, w_gate, w_up, w_down),
            tuple(gain.reshape(1, -1) for gain in (gain_self, gain_cross, gain_ffn)),
            dec_in.reshape(-1, MODEL),
            enc_out.reshape(-1, MODEL),
            out_grad.reshape(-1, MODEL),
            seg_dec,
            seg_enc,
        )
        final = finish_call(back)
        squares = final[6:14]
        gain_grads = [grad.reshape(-1) for grad in final[14:17]]
        return (
            final[0].reshape(dec_in.shape),
            final[1].reshape(dec_in.shape),
            final[2].reshape(enc_out.shape),
            gain_grads[0],
            squares[WQ_A],
            squares[WK_A],
            squares[WV_A],
            squares[WO_A],
            gain_grads[1],
            squares[WQ_C],
            squares[WK_C],
            squares[WV_C],
            squares[WO_C],
            gain_grads[2],
            final[3],
            final[4],
            final[5],
        )
    gain_a, gain_c, gain_f = gather_group((gain_self, gain_cross, gain_ffn))
    full = gather_group(narrow)
    gate_full, up_full = gather_group((w_gate, w_up))
    get_self = lambda: (gain_a, *full[0:4])
    get_cross = lambda: (gain_c, *full[4:8])
    get_ffn = lambda: (gain_f, gate_full, up_full, full[8])
    kept = forward(dec_in, enc_out, self_ok, cross_ok, get_self, get_cross)
    result_rows, grad_rows_dec, grad_rows_enc, grads = backward(
        dec_in, enc_out, self_ok, cross_ok, out_grad, kept, get_self, get_cross, get_ffn
    )
    gains = reduce_group((grads[0], grads[5], grads[10]), (gain_self, gain_cross, gain_ffn))
    wide = reduce_group(grads[11:13], (w_gate, w_up))
    thin = reduce_group(grads[1:5] + grads[6:10] + grads[13:14], narrow)
    return (
        (result_rows, grad_rows_dec, grad_rows_enc, gains[0])
        + tuple(thin[0:4])
        + (gains[1],)
        + tuple(thin[4:8])
        + (gains[2], *wide, thin[8])
    )


def solution(mesh):
    placed = (
        P(("dp", "fsdp"), None, None),
        P(("dp", "fsdp"), None, None),
        P(("dp", "fsdp"), None),
        P(("dp", "fsdp"), None),
        P(("dp", "fsdp"), None, None),
        P("fsdp"),
        P("fsdp", None),
        P("fsdp", None),
        P("fsdp", None),
        P("fsdp", None),
        P("fsdp"),
        P("fsdp", None),
        P("fsdp", None),
        P("fsdp", None),
        P("fsdp", None),
        P("fsdp"),
        P("fsdp", None),
        P("fsdp", None),
        P("fsdp", None),
    )
    return jax.shard_map(
        body,
        mesh=mesh,
        in_specs=placed,
        out_specs=(
            P(("dp", "fsdp"), None, None),
            P(("dp", "fsdp"), None, None),
            P(("dp", "fsdp"), None, None),
            P("fsdp"),
            P("fsdp", None),
            P("fsdp", None),
            P("fsdp", None),
            P("fsdp", None),
            P("fsdp"),
            P("fsdp", None),
            P("fsdp", None),
            P("fsdp", None),
            P("fsdp", None),
            P("fsdp"),
            P("fsdp", None),
            P("fsdp", None),
            P("fsdp", None),
        ),
        check_vma=False,
    )
```

```python
import functools
import math

import jax
import jax.numpy as jnp
from jax import lax
from jax.experimental import pallas as pl
from jax.experimental.pallas import tpu as pltpu
from jax.sharding import PartitionSpec as P

HD = 64
MODEL = 768


EPSILON = 1e-06
MASKED = -1000000000.0


def rms_forward(values_in, gain_vec):
    return (
        values_in
        * lax.rsqrt(jnp.mean(values_in * values_in, axis=-1, keepdims=True) + EPSILON)
        * gain_vec
    )


def rms_backward(values_in, gain_low, grad_out):
    _, pullback = jax.vjp(rms_forward, values_in, gain_low.astype(jnp.float32))
    return pullback(grad_out)


def project(acts, weight):
    return jnp.einsum("rld,dn->rln", acts, weight, preferred_element_type=jnp.float32)


def weight_grad(acts, grad_out):
    return jnp.einsum("rld,rln->dn", acts, grad_out, preferred_element_type=jnp.float32)


def input_grad(grad_out, weight):
    return jnp.einsum("rln,dn->rld", grad_out, weight, preferred_element_type=jnp.float32)


def split_heads(tensor):
    return tensor.reshape(tensor.shape[0], tensor.shape[1], -1, HD)


def merge_heads(tensor):
    return tensor.reshape(tensor.shape[0], tensor.shape[1], -1)


def attention_probs(queries, keys_all, allowed):
    scores = jnp.einsum(
        "rqhd,rkhd->rhqk",
        split_heads(queries),
        split_heads(keys_all),
        preferred_element_type=jnp.float32,
    )
    scores = jnp.where(allowed[:, None], scores, MASKED)
    return jax.nn.softmax(scores, axis=-1)


def attend_forward(queries, keys_all, values, allowed):
    probs = attention_probs(queries, keys_all, allowed).astype(jnp.bfloat16)
    mixture = jnp.einsum(
        "rhqk,rkhd->rqhd", probs, split_heads(values), preferred_element_type=jnp.float32
    )
    return merge_heads(mixture).astype(jnp.bfloat16)


def attend_backward(queries, keys_all, values, allowed, grad_mix):
    weights_full = attention_probs(queries, keys_all, allowed)
    grad_heads = split_heads(grad_mix)
    grad_values = jnp.einsum(
        "rhqk,rqhd->rkhd",
        weights_full.astype(jnp.bfloat16),
        grad_heads,
        preferred_element_type=jnp.float32,
    )
    grad_weights = jnp.einsum(
        "rqhd,rkhd->rhqk", grad_heads, split_heads(values), preferred_element_type=jnp.float32
    )
    grad_scores = (
        weights_full * (grad_weights - jnp.sum(weights_full * grad_weights, axis=-1, keepdims=True))
    ).astype(jnp.bfloat16)
    grad_queries = jnp.einsum(
        "rhqk,rkhd->rqhd", grad_scores, split_heads(keys_all), preferred_element_type=jnp.float32
    ) * HD ** (-0.5)
    grad_keys = jnp.einsum(
        "rhqk,rqhd->rkhd", grad_scores, split_heads(queries), preferred_element_type=jnp.float32
    )
    return (
        merge_heads(grad_queries).astype(jnp.bfloat16),
        merge_heads(grad_keys).astype(jnp.bfloat16),
        merge_heads(grad_values).astype(jnp.bfloat16),
    )


def gather_group(shards):
    joined = jnp.concatenate(shards, axis=0)
    whole = lax.all_gather(joined, "fsdp", axis=0, tiled=False)
    parts = []
    start = 0
    for shard in shards:
        part = whole[:, start : start + shard.shape[0]]
        parts.append(part.reshape((-1,) + shard.shape[1:]))
        start += shard.shape[0]
    return parts


def reduce_group(gradients, shards):
    count = lax.axis_size("fsdp")
    joined = jnp.concatenate(
        [
            gradient.astype(jnp.bfloat16).reshape((count, -1) + gradient.shape[1:])
            for gradient in gradients
        ],
        axis=1,
    )
    owned = lax.psum_scatter(joined, "fsdp", scatter_dimension=0, tiled=False)
    quarter = lax.psum_scatter(owned, "dp", scatter_dimension=0, tiled=True)
    summed = lax.all_gather(quarter, "dp", axis=0, tiled=True)
    parts = []
    start = 0
    for shard in shards:
        part = summed[start : start + shard.shape[0]]
        parts.append(part.astype(jnp.float32))
        start += shard.shape[0]
    return parts


def forward(dec_rows, enc_rows, self_ok, cross_ok, get_self, get_cross):
    gain_a, wq_a, wk_a, wv_a, wo_a = get_self()
    dec_float = dec_rows.astype(jnp.float32)
    normed_a = rms_forward(dec_float, gain_a.astype(jnp.float32)).astype(jnp.bfloat16)
    query_a = (project(normed_a, wq_a) * HD ** (-0.5)).astype(jnp.bfloat16)
    keys_a = project(normed_a, wk_a).astype(jnp.bfloat16)
    values_a = project(normed_a, wv_a).astype(jnp.bfloat16)
    mix_a = attend_forward(query_a, keys_a, values_a, self_ok)
    after_self = dec_float + project(mix_a, wo_a)
    gain_c, wq_c, wk_c, wv_c, wo_c = get_cross()
    normed_c = rms_forward(after_self, gain_c.astype(jnp.float32)).astype(jnp.bfloat16)
    query_c = (project(normed_c, wq_c) * HD ** (-0.5)).astype(jnp.bfloat16)
    keys_c = project(enc_rows, wk_c).astype(jnp.bfloat16)
    values_c = project(enc_rows, wv_c).astype(jnp.bfloat16)
    mix_c = attend_forward(query_c, keys_c, values_c, cross_ok)
    after_cross = after_self + project(mix_c, wo_c)
    return (
        (normed_a, query_a, keys_a, values_a, mix_a, normed_c, query_c, mix_c),
        (keys_c, values_c),
        (after_self, after_cross),
    )


def backward(dec_rows, enc_rows, self_ok, cross_ok, grad_rows, kept, get_self, get_cross, get_ffn):
    (normed_a, query_a, keys_a, values_a, mix_a, normed_c, query_c, mix_c) = kept[0]
    keys_c, values_c = kept[1]
    after_self, after_cross = kept[2]
    dec_float = dec_rows.astype(jnp.float32)
    gain_f, gate_w, up_w, down_w = get_ffn()
    normed_f = rms_forward(after_cross, gain_f.astype(jnp.float32)).astype(jnp.bfloat16)
    gate_pre = project(normed_f, gate_w)
    up_pre = project(normed_f, up_w)
    hidden_low = (jax.nn.gelu(gate_pre, approximate=True) * up_pre).astype(jnp.bfloat16)
    dec_result = (after_cross + project(hidden_low, down_w)).astype(jnp.bfloat16)
    grad_res = grad_rows.astype(jnp.float32)
    grad_branch = grad_res.astype(jnp.bfloat16)
    grad_down = weight_grad(hidden_low, grad_branch)
    grad_hidden = input_grad(grad_branch, down_w)
    _, gelu_pull = jax.vjp(
        lambda gate_in, up_in: jax.nn.gelu(gate_in, approximate=True) * up_in, gate_pre, up_pre
    )
    grad_gate_pre, grad_up_pre = gelu_pull(grad_hidden)
    grad_gate_low = grad_gate_pre.astype(jnp.bfloat16)
    grad_up_low = grad_up_pre.astype(jnp.bfloat16)
    grad_gate = weight_grad(normed_f, grad_gate_low)
    grad_up = weight_grad(normed_f, grad_up_low)
    grad_normed = input_grad(grad_gate_low, gate_w) + input_grad(grad_up_low, up_w)
    grad_input, grad_gain_f = rms_backward(after_cross, gain_f, grad_normed)
    grad_res = grad_res + grad_input
    gain_c, wq_c, wk_c, wv_c, wo_c = get_cross()
    grad_branch = grad_res.astype(jnp.bfloat16)
    grad_wo_c = weight_grad(mix_c, grad_branch)
    grad_mix = input_grad(grad_branch, wo_c).astype(jnp.bfloat16)
    grad_query, grad_keys, grad_values = attend_backward(
        query_c, keys_c, values_c, cross_ok, grad_mix
    )
    grad_wq_c = weight_grad(normed_c, grad_query)
    grad_wk_c = weight_grad(enc_rows, grad_keys)
    grad_wv_c = weight_grad(enc_rows, grad_values)
    grad_enc_rows = input_grad(grad_keys, wk_c) + input_grad(grad_values, wv_c)
    grad_normed = input_grad(grad_query, wq_c)
    grad_input, grad_gain_c = rms_backward(after_self, gain_c, grad_normed)
    grad_res = grad_res + grad_input
    gain_a, wq_a, wk_a, wv_a, wo_a = get_self()
    grad_branch = grad_res.astype(jnp.bfloat16)
    grad_wo_a = weight_grad(mix_a, grad_branch)
    grad_mix = input_grad(grad_branch, wo_a).astype(jnp.bfloat16)
    grad_query, grad_keys, grad_values = attend_backward(
        query_a, keys_a, values_a, self_ok, grad_mix
    )
    grad_wq_a = weight_grad(normed_a, grad_query)
    grad_wk_a = weight_grad(normed_a, grad_keys)
    grad_wv_a = weight_grad(normed_a, grad_values)
    grad_normed = (
        input_grad(grad_query, wq_a) + input_grad(grad_keys, wk_a) + input_grad(grad_values, wv_a)
    )
    grad_input, grad_gain_a = rms_backward(dec_float, gain_a, grad_normed)
    grad_dec_rows = grad_res + grad_input
    full_grads = (
        grad_gain_a,
        grad_wq_a,
        grad_wk_a,
        grad_wv_a,
        grad_wo_a,
        grad_gain_c,
        grad_wq_c,
        grad_wk_c,
        grad_wv_c,
        grad_wo_c,
        grad_gain_f,
        grad_gate,
        grad_up,
        grad_down,
    )
    return (dec_result, grad_dec_rows, grad_enc_rows, full_grads)


def dot_nn(left, right):
    return lax.dot_general(left, right, (((1,), (0,)), ((), ())), preferred_element_type=jnp.float32)


def dot_nt(left, right):
    return lax.dot_general(left, right, (((1,), (1,)), ((), ())), preferred_element_type=jnp.float32)


def dot_tn(left, right):
    return lax.dot_general(left, right, (((0,), (0,)), ((), ())), preferred_element_type=jnp.float32)


def flip(index, step):
    return index + step - 2 * step * ((index // step) % 2)


class Place:
    def __init__(self):
        self.dp = lax.axis_index("dp")
        self.fs = lax.axis_index("fsdp")
        self.core = self.fs % 2
        self.x = (self.fs // 2) % 2
        self.y = (self.fs // 4) % 2
        self.inner = (self.dp * (3 - self.dp)) // 2

    def to_core(self):
        return (self.dp, flip(self.fs, 1))

    def to_x(self):
        return (self.dp, flip(self.fs, 2))

    def to_y(self):
        return (self.dp, flip(self.fs, 4))

    def to_pair(self):
        return (flip(self.dp, 1), self.fs)

    def to_middle(self):
        return (3 - self.dp, self.fs)


def remote(source, target, send_sem, recv_sem, device):
    return pltpu.make_async_remote_copy(
        src_ref=source,
        dst_ref=target,
        send_sem=send_sem,
        recv_sem=recv_sem,
        device_id=device,
        device_id_type=pl.DeviceIdType.MESH,
    )


def greet(devices):
    barrier = pltpu.get_barrier_semaphore()
    for device in devices:
        pl.semaphore_signal(
            barrier, inc=1, device_id=device, device_id_type=pl.DeviceIdType.MESH
        )


LINK_BYTES_PER_US = 45000.0
WINDOW = 8
QUARTERS = 4
SQUARE_RING = 2
PLANE_WINDOW_US = 2.5
WORK_SCALE = 1.3
GATHER_SLACK, REST_SLACK, WHOLE_SLACK = 0.0, 3.0, 3.0
CORE_SLACK, PLANE_SLACK, COLUMN_SLACK = 0.0, 0.0, 0.0
PAIRED = (("wide", 0), ("wide", 1), ("wide", 2), ("wide", 3))
LAST_PARTS = 3
HALF = jnp.bfloat16
FULL = jnp.float32


class Events:
    def __init__(self):
        self.now = 0.0
        self.heap = []
        self.count = 0
        self.free = {}
        self.plane_load = 0.0
        self.plane_queue = []

    def enter_plane(self, unit=None):
        if unit is not None:
            self.plane_queue.append(unit)
        while self.plane_queue and self.plane_load < PLANE_WINDOW_US:
            unit = self.plane_queue.pop(0)
            self.plane_load += unit.half_us
            unit.cross_plane()

    def leave_plane(self, unit):
        self.plane_load -= unit.half_us
        self.enter_plane()

    def post(self, ready, slack, action):
        self.count += 1
        self.heap.append((ready, ready + slack, self.count, action))

    def sent(self, links, micros, delay):
        ends = []
        for link in links:
            start = max(self.now, self.free.get(link, 0.0))
            self.free[link] = start + micros
            ends.append(start + micros + delay)
        return max(ends)

    def run(self, event):
        self.heap.remove(event)
        self.now = max(self.now, event[0]) + 0.2
        event[3]()

    def step(self):
        self.run(min(self.heap, key=lambda event: (event[1], event[2])))

    def until(self, holds):
        while not holds():
            self.step()

    def work(self, micros, action):
        while self.heap:
            event = min(self.heap, key=lambda event: (event[1], event[2]))
            if event[1] > self.now:
                break
            self.run(event)
        action()
        self.now += WORK_SCALE * micros

    def drain(self):
        while self.heap:
            self.step()


class Chunk:
    def __init__(self, events, place, shard, whole, part, micros, sems, stages, ready):
        self.events = events
        self.place = place
        self.shard = shard
        self.whole = whole
        self.start, self.rows, self.cols = part
        self.micros = micros
        self.send_sems, self.recv_sems, self.stage_sems, self.own_sems = sems
        self.stages = stages
        self.ready = ready
        self.following = None
        fs = place.fs
        even = 1 - place.dp % 2
        self.first = even * flip(fs, 2) + (1 - even) * flip(fs, 4)
        self.second = even * flip(fs, 4) + (1 - even) * flip(fs, 2)
        self.cross = flip(flip(fs, 2), 4)
        self.to = [
            (place.dp, self.first),
            (place.dp, self.second),
            place.to_pair(),
            place.to_core(),
        ]

    def own(self):
        return self.shard.at[pl.ds(self.start, self.rows), self.cols]

    def block(self, owner):
        return self.whole.at[pl.ds(owner * self.shard.shape[0] + self.start, self.rows), self.cols]

    def copy(self, flow, owner, own=False):
        return remote(
            self.own() if own else self.block(owner),
            self.block(owner),
            self.send_sems.at[flow],
            self.recv_sems.at[flow],
            self.to[min(flow, 3)],
        )

    def piece(self, ref, index):
        rows = self.rows // len(self.stages)
        return ref.at[pl.ds(index * rows, rows)] if len(self.stages) > 1 else ref

    def stage(self):
        return [
            pltpu.make_async_copy(self.piece(self.own(), index), held, self.stage_sems.at[index])
            for index, held in enumerate(self.stages)
        ]

    def keep(self):
        block = self.block(self.place.fs)
        return [
            pltpu.make_async_copy(held, self.piece(block, index), self.own_sems.at[index])
            for index, held in enumerate(self.stages)
        ]

    def begin(self):
        self.copy(0, self.place.fs, own=True).start()
        self.copy(3, self.place.fs, own=True).start()
        self.events.post(
            self.events.sent(["gather first"], self.micros, 2.5), GATHER_SLACK, self.relay_first
        )

    def relay_first(self):
        self.copy(0, self.first).wait_recv()
        self.copy(1, self.first).start()
        self.copy(2, self.first).start()
        self.copy(4, self.first).start()
        if self.following is not None:
            self.following.begin()
        self.events.post(
            self.events.sent(["gather second"], self.micros, 2.5), REST_SLACK, self.relay_rest
        )

    def relay_rest(self):
        self.copy(1, self.cross).wait_recv()
        self.copy(5, self.cross).start()
        self.copy(2, self.second).wait_recv()
        self.copy(6, self.second).start()
        self.events.post(self.events.now + 1.5, WHOLE_SLACK, self.finish)

    def finish(self):
        for flow, owner in ((3, self.place.fs), (4, self.first), (5, self.cross), (6, self.second)):
            self.copy(flow, flip(owner, 1)).wait_recv()
        self.ready()

    def drain(self):
        fs = self.place.fs
        owners = (fs, self.first, self.first, fs, self.first, self.cross, self.second)
        for flow in range(7):
            self.copy(flow, owners[flow], own=flow in (0, 3)).wait_send()


class Reduction:
    plane_flows = (1, 2, 3, 4)

    def __init__(self, events, place, buffers, sems, rows, cols, itemsize, finish):
        self.events = events
        self.place = place
        self.outgoing, self.first, self.along_x, self.along_y = buffers[0:4]
        self.second, self.far, self.final = buffers[4:7]
        self.send_sems, self.recv_sems = sems
        self.half_us = rows * cols * itemsize / LINK_BYTES_PER_US
        self.finish = finish
        self.merged = False

    def flows(self):
        at = self.place
        return (
            (self.outgoing.at[1 - at.core], self.first, at.to_core()),
            (self.first.at[:, 1 - at.x, 0], self.along_x, at.to_x()),
            (self.first.at[1 - at.y, :, 1], self.along_y, at.to_y()),
            (self.along_x.at[1 - at.y], self.second.at[0], at.to_y()),
            (self.along_y.at[1 - at.x], self.second.at[1], at.to_x()),
            (self.second, self.final, at.to_pair()),
            (self.second, self.far, at.to_middle()),
            (self.final, self.final, at.to_pair()),
        )

    def copy(self, flow):
        source, target, device = self.flows()[flow]
        return remote(source, target, self.send_sems.at[flow], self.recv_sems.at[flow], device)

    def begin(self):
        self.copy(0).start()
        self.events.post(self.events.sent(["core"], self.half_us * 0.8, 1.0), CORE_SLACK, self.merge_cores)

    def merge_cores(self):
        at = self.place
        self.copy(0).wait_recv()

        def add(index, carry):
            y, x, half = index // 4, (index // 2) % 2, index % 2
            self.first[y, x, half] = self.first[y, x, half] + self.outgoing[at.core, y, x, half]
            return carry

        lax.fori_loop(0, 8, add, 0)
        self.copy(0).wait_send()
        self.merged = True
        self.events.enter_plane(self)

    def cross_plane(self):
        self.copy(1).start()
        self.copy(2).start()
        self.events.post(self.events.sent(["first", "second"], 2 * self.half_us, 2.5), PLANE_SLACK, self.merge_first)

    def merge_first(self):
        at = self.place
        self.copy(1).wait_recv()
        self.copy(2).wait_recv()
        for index in range(2):
            self.along_x[index] = self.along_x[index] + self.first[index, at.x, 0]
            self.along_y[index] = self.along_y[index] + self.first[at.y, index, 1]
        self.copy(3).start()
        self.copy(4).start()
        self.events.post(self.events.sent(["first", "second"], self.half_us, 2.5), PLANE_SLACK, self.merge_second)
        self.events.leave_plane(self)

    def merge_second(self):
        at = self.place
        self.copy(3).wait_recv()
        self.copy(4).wait_recv()
        self.second[0] = self.second[0] + self.along_x[at.y]
        self.second[1] = self.second[1] + self.along_y[at.x]
        self.enter_column()

    def enter_column(self):
        at = self.place

        @pl.when(at.inner == 0)
        def _():
            self.copy(5).start()

        self.events.post(self.events.sent(["z"], 2 * self.half_us, 2.5), COLUMN_SLACK, self.merge_near)

    def merge_near(self):
        @pl.when(self.place.inner == 1)
        def _():
            self.copy(5).wait_recv()
            for half in range(2):
                self.second[half] = self.second[half] + self.final[half]
            self.copy(6).start()

        self.events.post(self.events.sent(["z middle"], 2 * self.half_us, 2.5), COLUMN_SLACK, self.merge_far)

    def merge_far(self):
        @pl.when(self.place.inner == 1)
        def _():
            self.copy(6).wait_recv()
            for half in range(2):
                self.final[half] = self.second[half] + self.far[half]
            self.copy(7).start()

        self.events.post(self.events.sent(["z back"], 2 * self.half_us, 2.5), COLUMN_SLACK, self.complete)

    def complete(self):
        @pl.when(self.place.inner == 0)
        def _():
            self.copy(7).wait_recv()

        self.finish(self.final)

    def drain(self):
        for flow in self.plane_flows:
            self.copy(flow).wait_send()

        @pl.when(self.place.inner == 0)
        def _():
            self.copy(5).wait_send()

        @pl.when(self.place.inner == 1)
        def _():
            self.copy(6).wait_send()
            self.copy(7).wait_send()


class PairReduction(Reduction):
    plane_flows = (1, 2, 3)

    def chips(self):
        at = self.place
        odd = at.dp % 2
        even = 1 - odd
        first = (even * at.y + odd * (1 - at.y), even * (1 - at.x) + odd * at.x)
        second = (1 - first[0], 1 - first[1])
        return first, second, (1 - at.y, 1 - at.x)

    def flows(self):
        at = self.place
        even = 1 - at.dp % 2
        first, second, opposite = self.chips()
        to_first = (at.dp, even * flip(at.fs, 2) + (1 - even) * flip(at.fs, 4))
        to_second = (at.dp, even * flip(at.fs, 4) + (1 - even) * flip(at.fs, 2))
        base = super().flows()
        return (
            base[0],
            (self.first.at[opposite[0], opposite[1]], self.along_x, to_second),
            (self.first.at[second[0], second[1]], self.along_y, at.to_pair()),
            (self.along_x, self.second, to_first),
            None,
            *base[5:],
        )

    def cross_plane(self):
        self.copy(1).start()
        self.copy(2).start()
        self.events.post(self.events.sent(["second", "z"], 2 * self.half_us, 2.5), PLANE_SLACK, self.merge_first)

    def merge_first(self):
        self.copy(1).wait_recv()
        self.copy(2).wait_recv()
        first = self.chips()[0]
        for half in range(2):
            self.along_x[half] = (
                self.along_x[half] + self.along_y[half] + self.first[first[0], first[1], half]
            )
        self.copy(3).start()
        self.events.post(self.events.sent(["first"], 2 * self.half_us, 2.5), PLANE_SLACK, self.merge_second)
        self.events.leave_plane(self)

    def merge_second(self):
        at = self.place
        self.copy(3).wait_recv()
        for half in range(2):
            self.second[half] = self.second[half] + self.first[at.y, at.x, half]
        self.enter_column()


def norm_rows(source, gain, target, rows, step):
    def body(index, carry):
        block = pl.ds(pl.multiple_of(index * step, step), step)
        values = source[block, :].astype(FULL)
        scale = lax.rsqrt(jnp.mean(values * values, axis=-1, keepdims=True) + EPSILON)
        target[block, :] = (values * scale * gain).astype(target.dtype)
        return carry

    lax.fori_loop(0, rows // step, body, 0)


def norm_back(source, gain, grad_norm, residual, low, rows, step):
    def body(index, total):
        block = pl.ds(pl.multiple_of(index * step, step), step)
        values = source[block, :].astype(FULL)
        scale = lax.rsqrt(jnp.mean(values * values, axis=-1, keepdims=True) + EPSILON)
        unit = values * scale
        grad = grad_norm[block, :]
        scaled = grad * gain
        change = scale * (scaled - unit * jnp.mean(scaled * unit, axis=-1, keepdims=True))
        updated = residual[block, :] + change
        residual[block, :] = updated
        low[block, :] = updated.astype(low.dtype)
        product = grad * unit
        for start in range(0, step, 8):
            total = total + product[start : start + 8]
        return total

    total = lax.fori_loop(0, rows // step, body, jnp.zeros((8, MODEL), FULL))
    return jnp.sum(total, axis=0, keepdims=True)


def make_masks(seg_dec, seg_enc, mask_self, mask_cross):
    rows, length = seg_dec.shape
    query = lax.broadcasted_iota(jnp.int32, (length, length), 0)
    key = lax.broadcasted_iota(jnp.int32, (length, length), 1)
    for row in range(rows):
        along = seg_dec[row : row + 1, :].astype(FULL)
        down = jnp.sum(jnp.where(query == key, along, 0.0), axis=1, keepdims=True)
        mask_self[row] = jnp.where((down == along) & (key <= query), 1.0, 0.0)
        enc = seg_enc[row : row + 1, :].astype(FULL)
        mask_cross[row] = jnp.where(down == enc, 1.0, 0.0)


class Heads:
    def __init__(self, queries, keys, values, mask, len_q, len_k, width):
        self.queries, self.keys, self.values, self.mask = queries, keys, values, mask
        self.len_q, self.len_k, self.width = len_q, len_k, width
        self.pairs = MODEL // (2 * HD)

    def lower(self, shape):
        return lax.broadcasted_iota(jnp.int32, shape, 1) < HD

    def stack(self, both):
        lower = self.lower((1, 2 * HD)).astype(FULL)
        upper = 1.0 - lower
        return jnp.concatenate([both * lower.astype(HALF), both * upper.astype(HALF)], axis=0)

    def join(self, stacked):
        top, bottom = stacked[: self.len_q], stacked[self.len_q :]
        return jnp.where(self.lower(top.shape), top, bottom)

    def places(self, step):
        found = []
        for near in range(self.width):
            index = step * self.width + near
            row, pair = index // self.pairs, index % self.pairs
            cols = pl.ds(pl.multiple_of(pair * 2 * HD, 2 * HD), 2 * HD)
            at_q = pl.ds(pl.multiple_of(row * self.len_q, 16), self.len_q)
            at_k = pl.ds(pl.multiple_of(row * self.len_k, 16), self.len_k)
            found.append((row, at_q, at_k, cols))
        return found

    def probs(self, rows, queries, keys):
        scores = [dot_nt(query, key) for query, key in zip(queries, keys)]
        split = (2, self.len_q, self.len_k)
        scores = [
            jnp.where(self.mask[row][None] > 0.0, score.reshape(split), MASKED)
            for row, score in zip(rows, scores)
        ]
        scores = [score.reshape(2 * self.len_q, self.len_k) for score in scores]
        powers = [jnp.exp(score - jnp.max(score, axis=-1, keepdims=True)) for score in scores]
        return [power * (1.0 / jnp.sum(power, axis=-1, keepdims=True)) for power in powers]

    def forward(self, target, first, last):
        def body(step, carry):
            places = self.places(step)
            rows = [place[0] for place in places]
            queries = [self.stack(self.queries[at_q, cols]) for _, at_q, _, cols in places]
            keys = [self.keys[at_k, cols] for _, _, at_k, cols in places]
            values = [self.values[at_k, cols] for _, _, at_k, cols in places]
            probs = self.probs(rows, queries, keys)
            mixed = [dot_nn(prob.astype(HALF), value) for prob, value in zip(probs, values)]
            for (_, at_q, _, cols), mix in zip(places, mixed):
                target[at_q, cols] = self.join(mix).astype(HALF)
            return carry

        lax.fori_loop(first // self.width, last // self.width, body, 0)

    def backward(self, grads, first, last):
        def body(step, carry):
            places = self.places(step)
            rows = [place[0] for place in places]
            queries = [self.stack(self.queries[at_q, cols]) for _, at_q, _, cols in places]
            keys = [self.keys[at_k, cols] for _, _, at_k, cols in places]
            values = [self.values[at_k, cols] for _, _, at_k, cols in places]
            grad = [self.stack(grads[at_q, cols]) for _, at_q, _, cols in places]
            each = range(self.width)
            grad_p = [dot_nt(grad[i], values[i]) for i in each]
            probs = self.probs(rows, queries, keys)
            grad_v = [dot_tn(probs[i].astype(HALF), grad[i]) for i in each]
            inner = [jnp.sum(probs[i] * grad_p[i], axis=-1, keepdims=True) for i in each]
            grad_s = [(probs[i] * (grad_p[i] - inner[i])).astype(HALF) for i in each]
            grad_q = [self.join(dot_nn(grad_s[i], keys[i])) * HD ** (-0.5) for i in each]
            grad_k = [dot_tn(grad_s[i], queries[i]) for i in each]
            for i, (_, at_q, at_k, cols) in enumerate(places):
                self.queries[at_q, cols] = grad_q[i].astype(HALF)
                self.keys[at_k, cols] = grad_k[i].astype(HALF)
                self.values[at_k, cols] = grad_v[i].astype(HALF)
            return carry

        lax.fori_loop(first // self.width, last // self.width, body, 0)


GELU_SCALE = (2.0 / math.pi) ** 0.5


def gelu_rows(gate_pre, up_pre, grad_hidden, hidden, grad_gate, grad_up, rows, step):
    def body(index, carry):
        block = pl.ds(pl.multiple_of(index * step, step), step)
        gate, up, grad = gate_pre[block, :], up_pre[block, :], grad_hidden[block, :]
        square = gate * gate
        bend = jnp.tanh(GELU_SCALE * gate * (1.0 + 0.044715 * square))
        rise = 0.5 * (1.0 + bend)
        value = gate * rise
        slope = rise + 0.5 * gate * (1.0 - bend * bend) * GELU_SCALE * (1.0 + 3 * 0.044715 * square)
        hidden[block, :] = (value * up).astype(HALF)
        grad_gate[block, :] = (grad * up * slope).astype(HALF)
        grad_up[block, :] = (grad * value).astype(HALF)
        return carry

    lax.fori_loop(0, rows // step, body, 0)


WQ_A, WK_A, WV_A, WO_A, WK_C, WV_C, WQ_C, WO_C, GATE, UP, DOWN, GAINS = range(12)
GATHER_ORDER = (WK_C, WQ_A, WK_A, WV_A, WO_A, WV_C, WQ_C, WO_C)
SLOTS = {WK_C: 1, WQ_A: 0, WK_A: 3, WV_A: 2, WO_A: 4, WV_C: 2, WQ_C: 3, WO_C: 0}
SLOTS_BACK = {WQ_A: 0, WK_A: 3, WV_A: 4}


def layer_kernel(dims, *refs):
    rows, len_q, len_k, count = dims
    tokens = rows * len_q
    shards, gain_shards = refs[0:11], refs[11:14]
    dec_hbm, enc_hbm, grad_hbm, seg_dec, seg_enc = refs[14:19]
    whole = refs[19:30]
    dec_out, grad_dec_out, grad_enc_out, gate_out, up_out, down_out, square_out, gain_out = refs[30:38]
    (gate_w, up_w, down_w, square_w, small, large, floats, enc, grad_low) = refs[38:47]
    (gain_tile, gains, mask_self, mask_cross, gate_pre, up_pre, grad_hidden) = refs[47:54]
    (hidden, grad_gate, grad_up, grad_norm, result, grad_mix, gain_grads) = refs[54:61]
    residual = result
    dec = grad_mix
    wide_bufs, tall_bufs, square_bufs, gain_bufs = refs[61:68], refs[68:75], refs[75:82], refs[82:89]
    last_bufs = refs[89:96]
    gather_send, gather_recv, stage_sems, own_sems, send_sems, recv_sems = refs[96:102]
    load_sems, weight_sems, store_sems = refs[102:105]

    place = Place()
    events = Events()
    loads = {}
    stores = []
    ff_part = whole[DOWN].shape[0] // QUARTERS
    pairs_all = rows * (MODEL // (2 * HD))

    def load(name, source, target, sem):
        loads[name] = pltpu.make_async_copy(source, target, sem)
        loads[name].start()

    def store(source, target):
        stores.append(pltpu.make_async_copy(source, target, store_sems.at[len(stores)]))
        stores[-1].start()

    neighbours = [
        place.to_core(), place.to_x(), place.to_y(), place.to_pair(), place.to_middle()
    ]
    greet(neighbours)
    load("dec", dec_hbm, dec, load_sems.at[0])
    load("enc", enc_hbm, enc, load_sems.at[1])
    load("grad", grad_hbm, grad_low, load_sems.at[2])
    gain_tile[...] = jnp.zeros(gain_tile.shape, FULL)
    for which, shard in enumerate(gain_shards):
        gain_tile[which : which + 1, 0 : shard.shape[1]] = shard[...].astype(FULL)

    gathered = {}
    slot_free = {slot: True for slot in range(5)}
    waiting = []

    def try_loads():
        for entry in list(waiting):
            ready, slot, start = entry
            if ready() and slot_free[slot]:
                slot_free[slot] = False
                start()
                waiting.remove(entry)

    def want(name, ready, slot, start):
        slot_free.setdefault(slot, True)
        waiting.append((ready, slot, start))
        try_loads()

    def release(slot):
        slot_free[slot] = True
        try_loads()

    def want_square(which, slot, name):
        want(
            name,
            lambda: gathered.get(which, False),
            slot,
            lambda: load(name, whole[which], square_w.at[slot], weight_sems.at[slot]),
        )

    def want_quarter(quarter):
        slot = quarter % 2
        part = pl.ds(quarter * ff_part, ff_part)

        def start():
            load(("gate", quarter), whole[GATE].at[:, part], gate_w.at[slot], weight_sems.at[5 + slot])
            load(("up", quarter), whole[UP].at[:, part], up_w.at[slot], weight_sems.at[7 + slot])
            load(("down", quarter), whole[DOWN].at[part], down_w.at[slot], weight_sems.at[9 + slot])

        want(
            ("quarter", quarter),
            lambda: gathered.get(DOWN, False) and gathered.get((UP, quarter), False),
            ("ffn", slot),
            start,
        )

    for which in GATHER_ORDER:
        want_square(which, SLOTS[which], ("square", which))
    for quarter in range(QUARTERS):
        want_quarter(quarter)

    def need(name):
        events.until(lambda: name in loads)
        loads[name].wait()

    chunks = []

    def add_chunk(shard, target, start, height, cols, name, stages):
        index = len(chunks)
        width = cols.size if cols is not None else shard.shape[1]
        itemsize = jnp.dtype(shard.dtype).itemsize

        def ready():
            if name is not None:
                gathered[name] = True
                try_loads()

        chunks.append(
            Chunk(
                events,
                place,
                shard,
                target,
                (start, height, slice(None) if cols is None else cols),
                height * width * itemsize / LINK_BYTES_PER_US,
                (
                    gather_send.at[index],
                    gather_recv.at[index],
                    stage_sems.at[index],
                    own_sems.at[index],
                ),
                stages,
                ready,
            )
        )

    for index, which in enumerate(GATHER_ORDER):
        if index == 1:
            add_chunk(gain_tile, gains, 0, 8, None, GAINS, [gain_bufs[0].at[0, 0, 0, 0, 0]])
        held = square_bufs[0].at[0, index // 4, (index // 2) % 2, index % 2]
        add_chunk(
            shards[which],
            whole[which],
            0,
            shards[which].shape[0],
            None,
            which,
            [held.at[0], held.at[1]],
        )
    down_rows = shards[DOWN].shape[0]
    for part in range(4):
        piece = down_rows // 4
        add_chunk(
            shards[DOWN],
            whole[DOWN],
            part * piece,
            piece,
            None,
            DOWN if part == 3 else None,
            [tall_bufs[0].at[0, 0, 0, part // 2, part % 2]],
        )
    for quarter in range(QUARTERS):
        for which in (GATE, UP):
            add_chunk(
                shards[which],
                whole[which],
                0,
                shards[which].shape[0],
                pl.ds(quarter * ff_part, ff_part),
                (which, quarter),
                [wide_bufs[0].at[0, 0, quarter // 2, quarter % 2, which - GATE]],
            )
    for index, chunk in enumerate(chunks):
        if index + WINDOW < len(chunks):
            chunk.following = chunks[index + WINDOW]
    for chunk in chunks:
        for copy in chunk.stage():
            copy.start()
    pl.semaphore_wait(pltpu.get_barrier_semaphore(), len(neighbours))
    for chunk in chunks[:WINDOW]:
        chunk.begin()
    for chunk in chunks:
        for staged, kept in zip(chunk.stage(), chunk.keep()):
            staged.wait()
            kept.start()

    def gain_row(which):
        width = MODEL // count
        return jnp.concatenate(
            [gains[8 * owner + which : 8 * owner + which + 1, 0:width] for owner in range(count)],
            axis=1,
        )

    def masks():
        make_masks(seg_dec, seg_enc, mask_self, mask_cross)
        gain_grads[...] = jnp.zeros(gain_grads.shape, FULL)
        loads["dec"].wait()
        for chunk in chunks:
            for kept in chunk.keep():
                kept.wait()

    def project(acts, which, target, scale=None, free=True):
        name = ("square", which)
        need(name)

        def run():
            value = dot_nn(acts[...], square_w[SLOTS[which]])
            if scale is not None:
                value = value * scale
            target[...] = value.astype(target.dtype)
            if free:
                release(SLOTS[which])

        events.work(0.6 * acts.shape[0] / tokens, run)

    def residual_add(before, acts, which, after, free):
        need(("square", which))

        def run():
            after[...] = before[...].astype(FULL) + dot_nn(acts[...], square_w[SLOTS[which]])

        events.work(0.8, run)

    def norm(source, which, target):
        events.work(
            0.4, lambda: norm_rows(source, gain_row(which), target, tokens, len_q)
        )

    def attend(heads, target, parts, micros):
        for part in range(parts):
            bounds = (part * pairs_all // parts, (part + 1) * pairs_all // parts)
            events.work(micros / parts, functools.partial(heads.forward, target, *bounds))

    self_heads = Heads(small.at[1], small.at[2], small.at[3], mask_self, len_q, len_q, 3)
    cross_heads = Heads(small.at[6], large.at[0], large.at[1], mask_cross, len_q, len_k, 2)
    root = HD ** (-0.5)

    events.work(0.5, masks)
    loads["enc"].wait()
    project(enc, WK_C, large.at[0], free=False)
    events.until(lambda: GAINS in gathered)
    norm(dec, 0, small.at[0])
    project(small.at[0], WQ_A, small.at[1], scale=root)
    project(small.at[0], WK_A, small.at[2])
    project(small.at[0], WV_A, small.at[3])
    attend(self_heads, small.at[4], 4, 3.0)
    residual_add(dec, small.at[4], WO_A, floats.at[0], False)
    norm(floats.at[0], 1, small.at[5])
    project(enc, WV_C, large.at[1], free=False)
    project(small.at[5], WQ_C, small.at[6], scale=root, free=False)
    attend(cross_heads, small.at[7], 6, 5.4)
    residual_add(floats.at[0], small.at[7], WO_C, floats.at[1], False)
    norm(floats.at[1], 2, small.at[8])
    loads["grad"].wait()

    units = []

    def unit_of(buffers, index, slot, finish, paired=False):
        number = len(units)
        final = buffers[6]
        unit = (PairReduction if paired else Reduction)(
            events,
            place,
            (buffers[0].at[slot], *(buffer.at[index] for buffer in buffers[1:7])),
            (send_sems.at[number], recv_sems.at[number]),
            final.shape[-2],
            final.shape[-1],
            jnp.dtype(final.dtype).itemsize,
            finish,
        )
        units.append(unit)
        return unit

    def claim(earlier):
        events.until(lambda: earlier.merged)

    wide_units = []

    def ffn_forward(quarter):
        slot = quarter % 2
        gate_pre[...] = dot_nn(small[8], gate_w[slot])
        up_pre[...] = dot_nn(small[8], up_w[slot])
        grad_hidden[...] = dot_nt(grad_low[...], down_w[slot])

    def ffn_gelu():
        gelu_rows(gate_pre, up_pre, grad_hidden, hidden, grad_gate, grad_up, tokens, len_q)

    def ffn_wide(quarter):
        def finish(final):
            part = pl.ds(quarter * ff_part, ff_part)
            store(final.at[0], gate_out.at[:, part])
            store(final.at[1], up_out.at[:, part])

        unit = unit_of(wide_bufs, quarter, 0, finish, ("wide", quarter) in PAIRED)
        wide_units.append(unit)
        height = MODEL // count
        for half, grads in enumerate((grad_gate, grad_up)):
            value = dot_tn(small[8], grads[...]).astype(HALF)
            for owner in range(count):
                unit.outgoing[owner % 2, owner // 4, (owner // 2) % 2, half] = value[
                    owner * height : (owner + 1) * height
                ]
        unit.begin()

    def ffn_tall(quarter):
        value = dot_tn(hidden[...], grad_low[...]).astype(HALF)
        owners = count // QUARTERS
        height = ff_part // owners
        piece = height // 4
        for near in range(owners):
            owner = quarter * owners + near
            for part in range(4):
                start = near * height + part * piece
                tall_bufs[0][part // 2, owner % 2, owner // 4, (owner // 2) % 2, part % 2] = value[
                    start : start + piece
                ]

    def ffn_rest(quarter):
        slot = quarter % 2
        change = dot_nt(grad_gate[...], gate_w[slot]) + dot_nt(grad_up[...], up_w[slot])
        output = dot_nn(hidden[...], down_w[slot])
        if quarter == 0:
            grad_norm[...] = change
            result[...] = floats[1] + output
        else:
            grad_norm[...] += change
            result[...] += output
        release(("ffn", slot))

    for quarter in range(QUARTERS):
        for kind in ("gate", "up", "down"):
            need((kind, quarter))
        events.work(1.1, functools.partial(ffn_forward, quarter))
        events.work(0.2, ffn_gelu)
        if quarter >= 1:
            claim(wide_units[quarter - 1])
        events.work(1.1, functools.partial(ffn_wide, quarter))
        events.work(0.8, functools.partial(ffn_tall, quarter))
        events.work(1.2, functools.partial(ffn_rest, quarter))

    def start_tall():
        for part in range(2):

            def finish(final, part=part):
                piece = final.shape[1]
                for half in range(2):
                    store(final.at[half], down_out.at[pl.ds((2 * part + half) * piece, piece)])

            unit_of(tall_bufs, part, part, finish).begin()

    def ffn_norm():
        small[8] = result[...].astype(HALF)
        store(small.at[8], dec_out)
        residual[...] = grad_low[...].astype(FULL)
        gain_grads[2:3, :] = norm_back(
            floats.at[1], gain_row(2), grad_norm, residual, grad_low, tokens, len_q
        )

    events.work(0.1, start_tall)
    events.work(1.0, ffn_norm)

    square_units = []

    def square_grad(which, acts, grads):
        index = len(square_units)
        height = MODEL // count

        def finish(final):
            piece = final.shape[1]
            for half in range(2):
                store(final.at[half], square_out.at[which, pl.ds(half * piece, piece)])

        if index >= SQUARE_RING:
            claim(square_units[index - SQUARE_RING])
        unit = unit_of(
            square_bufs, index, index % SQUARE_RING, finish, ("square", index) in PAIRED
        )
        square_units.append(unit)

        def compute():
            value = dot_tn(acts[...], grads[...]).astype(HALF)
            piece = height // 2
            for owner in range(count):
                for half in range(2):
                    start = owner * height + half * piece
                    unit.outgoing[owner % 2, owner // 4, (owner // 2) % 2, half] = value[
                        start : start + piece
                    ]
            unit.begin()

        events.work(0.9 if acts.shape[0] == tokens else 1.5, compute)

    last_units = []

    def last_grad(which, acts, grads):
        index = len(last_units)
        height = MODEL // count
        piece = height // 2
        width = MODEL // LAST_PARTS
        parts = []
        for part in range(LAST_PARTS):
            cols = pl.ds(part * width, width)

            def finish(final, cols=cols):
                for half in range(2):
                    store(final.at[half], square_out.at[which, pl.ds(half * piece, piece), cols])

            if index:
                claim(last_units[index - LAST_PARTS + part])
            parts.append(unit_of(last_bufs, index + part, part, finish))
        last_units.extend(parts)

        def compute():
            value = dot_tn(acts[...], grads[...]).astype(HALF)
            for part, unit in enumerate(parts):
                for owner in range(count):
                    for half in range(2):
                        start = owner * height + half * piece
                        unit.outgoing[owner % 2, owner // 4, (owner // 2) % 2, half] = value[
                            start : start + piece, part * width : (part + 1) * width
                        ]
                unit.begin()

        events.work(1.0, compute)

    def mix_grad(which):
        def run():
            grad_mix[...] = dot_nt(grad_low[...], square_w[SLOTS[which]]).astype(HALF)
            release(SLOTS[which])

        events.work(0.8, run)

    def attend_back(heads, parts, micros):
        for part in range(parts):
            bounds = (part * pairs_all // parts, (part + 1) * pairs_all // parts)
            events.work(micros / parts, functools.partial(heads.backward, grad_mix, *bounds))

    square_grad(WO_C, small.at[7], grad_low)
    mix_grad(WO_C)
    want_square(WQ_A, SLOTS_BACK[WQ_A], ("back", WQ_A))
    attend_back(cross_heads, 6, 10.0)
    square_grad(WK_C, enc, large.at[0])
    square_grad(WV_C, enc, large.at[1])
    square_grad(WQ_C, small.at[5], small.at[6])

    def cross_back():
        grad_norm[...] = dot_nt(small[6], square_w[SLOTS[WQ_C]])
        release(SLOTS[WQ_C])

    events.work(0.7, cross_back)

    def cross_norm():
        gain_grads[1:2, :] = norm_back(
            floats.at[0], gain_row(1), grad_norm, residual, grad_low, tokens, len_q
        )

    events.work(0.7, cross_norm)
    want_square(WK_A, SLOTS_BACK[WK_A], ("back", WK_A))

    square_grad(WO_A, small.at[4], grad_low)
    mix_grad(WO_A)
    want_square(WV_A, SLOTS_BACK[WV_A], ("back", WV_A))
    attend_back(self_heads, 4, 6.0)
    load("dec again", dec_hbm, dec, load_sems.at[0])
    last_grad(WQ_A, small.at[0], small.at[1])
    last_grad(WK_A, small.at[0], small.at[2])
    last_grad(WV_A, small.at[0], small.at[3])

    def self_back(index, which):
        part = dot_nt(small[1 + index], square_w[SLOTS_BACK[which]])
        if index == 0:
            grad_norm[...] = part
        else:
            grad_norm[...] += part

    for index, which in enumerate((WQ_A, WK_A, WV_A)):
        need(("back", which))
        events.work(0.7, functools.partial(self_back, index, which))

    def self_norm():
        loads["dec again"].wait()
        gain_grads[0:1, :] = norm_back(
            dec, gain_row(0), grad_norm, residual, grad_low, tokens, len_q
        )
        store(grad_low, grad_dec_out)
        width = MODEL // count
        unit = unit_of(gain_bufs, 0, 0, lambda final: store(final, gain_out))
        unit.outgoing[...] = jnp.zeros(unit.outgoing.shape, FULL)
        for owner in range(count):
            unit.outgoing[owner % 2, owner // 4, (owner // 2) % 2, 0, :, 0:width] = gain_grads[
                :, owner * width : (owner + 1) * width
            ]
        unit.begin()

    events.work(0.8, self_norm)

    def enc_grad(part):
        block = pl.ds(part * (enc.shape[0] // 4), enc.shape[0] // 4)
        value = dot_nt(large[0, block], square_w[SLOTS[WK_C]])
        value = value + dot_nt(large[1, block], square_w[SLOTS[WV_C]])
        enc[block, :] = value.astype(HALF)
        store(enc.at[block], grad_enc_out.at[block])

    for part in range(4):
        events.work(0.8, functools.partial(enc_grad, part))
    events.drain()
    for chunk in chunks:
        chunk.drain()
    for unit in units:
        unit.drain()
    for copy in stores:
        copy.wait()


def layer_call(shards, gain_shards, dec, enc, grad, seg_dec, seg_enc):
    rows, len_q = seg_dec.shape
    len_k = seg_enc.shape[1]
    count = lax.axis_size("fsdp")
    tokens, enc_tokens = rows * len_q, rows * len_k
    hidden_units = shards[DOWN].shape[0] * count
    ff_part = hidden_units // QUARTERS
    height = MODEL // count
    down_height = hidden_units // count
    in_any = pl.BlockSpec(memory_space=pl.ANY)
    in_vmem = pl.BlockSpec(memory_space=pltpu.VMEM)

    def buffers(number, ring, height, width, kind):
        return [
            pltpu.VMEM((ring, 2, 2, 2, 2, height, width), kind),
            pltpu.VMEM((number, 2, 2, 2, height, width), kind),
            *[pltpu.VMEM((number, 2, height, width), kind)] * 5,
        ]

    n_chunks = 1 + 8 + 4 + 2 * QUARTERS
    n_units = QUARTERS + 2 + 5 + 3 * LAST_PARTS + 1
    wholes = [
        jax.ShapeDtypeStruct((shard.shape[0] * count, shard.shape[1]), shard.dtype)
        for shard in shards
    ]
    results = pl.pallas_call(
        functools.partial(layer_kernel, (rows, len_q, len_k, count)),
        out_shape=wholes
        + [
            jax.ShapeDtypeStruct((tokens, MODEL), HALF),
            jax.ShapeDtypeStruct((tokens, MODEL), HALF),
            jax.ShapeDtypeStruct((enc_tokens, MODEL), HALF),
            jax.ShapeDtypeStruct((height, hidden_units), HALF),
            jax.ShapeDtypeStruct((height, hidden_units), HALF),
            jax.ShapeDtypeStruct((down_height, MODEL), HALF),
            jax.ShapeDtypeStruct((8, height, MODEL), HALF),
            jax.ShapeDtypeStruct((2, 8, 128), FULL),
        ],
        in_specs=[in_any] * 11 + [in_vmem] * 3 + [in_any] * 3 + [in_vmem] * 2,
        out_specs=[in_any] * 19,
        scratch_shapes=[
            pltpu.VMEM((2, MODEL, ff_part), HALF),
            pltpu.VMEM((2, MODEL, ff_part), HALF),
            pltpu.VMEM((2, ff_part, MODEL), HALF),
            pltpu.VMEM((5, MODEL, MODEL), HALF),
            pltpu.VMEM((9, tokens, MODEL), HALF),
            pltpu.VMEM((2, enc_tokens, MODEL), HALF),
            pltpu.VMEM((2, tokens, MODEL), FULL),
            pltpu.VMEM((enc_tokens, MODEL), HALF),
            pltpu.VMEM((tokens, MODEL), HALF),
            pltpu.VMEM((8, 128), FULL),
            pltpu.VMEM((8 * count, 128), FULL),
            pltpu.VMEM((rows, len_q, len_q), FULL),
            pltpu.VMEM((rows, len_q, len_k), FULL),
            *[pltpu.VMEM((tokens, ff_part), FULL)] * 3,
            *[pltpu.VMEM((tokens, ff_part), HALF)] * 3,
            pltpu.VMEM((tokens, MODEL), FULL),
            pltpu.VMEM((tokens, MODEL), FULL),
            pltpu.VMEM((tokens, MODEL), HALF),
            pltpu.VMEM((8, MODEL), FULL),
            *buffers(QUARTERS, 1, height, ff_part, HALF),
            *buffers(2, 2, down_height // 4, MODEL, HALF),
            *buffers(5, SQUARE_RING, height // 2, MODEL, HALF),
            *buffers(1, 1, 8, 128, FULL),
            *buffers(3 * LAST_PARTS, LAST_PARTS, height // 2, MODEL // LAST_PARTS, HALF),
            pltpu.SemaphoreType.DMA((n_chunks, 7)),
            pltpu.SemaphoreType.DMA((n_chunks, 7)),
            pltpu.SemaphoreType.DMA((n_chunks, 2)),
            pltpu.SemaphoreType.DMA((n_chunks, 2)),
            pltpu.SemaphoreType.DMA((n_units, 8)),
            pltpu.SemaphoreType.DMA((n_units, 8)),
            pltpu.SemaphoreType.DMA((3,)),
            pltpu.SemaphoreType.DMA((11,)),
            pltpu.SemaphoreType.DMA((48,)),
        ],
        compiler_params=pltpu.CompilerParams(
            collective_id=0,
            has_side_effects=True,
            vmem_limit_bytes=63 * 1024 * 1024 + 512 * 1024,
        ),
        name="layer",
    )(*shards, *gain_shards, dec, enc, grad, seg_dec, seg_enc)
    return results[11:]


def finish_kernel(plan, *refs):
    n_in, n_out = 7, 14
    sources, gain_grads = refs[0:n_in], refs[n_in]
    targets = refs[n_in + 1 : n_in + 1 + n_out]
    gain_targets = refs[n_in + 1 + n_out : n_in + 4 + n_out]
    taken, made = refs[n_in + 4 + n_out : n_in + 6 + n_out]
    in_sems, out_sems = refs[n_in + 6 + n_out :]
    reads, writes = [], []
    for index, (source, source_at, target, target_at, _, _) in enumerate(plan):
        reads.append(
            pltpu.make_async_copy(
                sources[source].at[source_at], taken[index], in_sems.at[index]
            )
        )
        writes.append(
            pltpu.make_async_copy(made[index], targets[target].at[target_at], out_sems.at[index])
        )
    for copy in reads:
        copy.start()
    for index, target in enumerate(gain_targets):
        target[...] = gain_grads[0, index : index + 1, 0 : target.shape[1]]
    for index in range(len(plan)):
        reads[index].wait()
        made[index][...] = taken[index][...].astype(made[index].dtype)
        writes[index].start()
    for copy in writes:
        copy.wait()


def finish_call(results):
    everything = slice(None)
    plan = []

    def add(source, source_at, target, target_at, shape):
        plan.append((source, source_at, target, target_at, *shape))

    enc_rows = results[2].shape[0]
    for part in range(4):
        block = pl.ds(part * enc_rows // 4, enc_rows // 4)
        add(2, (block, everything), 2, (block, everything), (enc_rows // 4, MODEL))
    for index in (3, 4, 5, 1):
        add(index, (everything, everything), index, (everything, everything), results[index].shape)
    for index in range(8):
        add(6, (index, everything, everything), 6 + index, (everything, everything), results[6].shape[1:])
    add(0, (everything, everything), 0, (everything, everything), results[0].shape)
    shapes = [jax.ShapeDtypeStruct(results[0].shape, HALF)]
    shapes += [jax.ShapeDtypeStruct(results[index].shape, FULL) for index in range(1, 6)]
    shapes += [jax.ShapeDtypeStruct(results[6].shape[1:], FULL)] * 8
    gain = results[6].shape[1]
    in_any = pl.BlockSpec(memory_space=pl.ANY)
    in_vmem = pl.BlockSpec(memory_space=pltpu.VMEM)
    return pl.pallas_call(
        functools.partial(finish_kernel, plan),
        out_shape=shapes + [jax.ShapeDtypeStruct((1, gain), FULL)] * 3,
        in_specs=[in_any] * 7 + [in_vmem],
        out_specs=[in_any] * 14 + [in_vmem] * 3,
        scratch_shapes=[
            [pltpu.VMEM(entry[4:6], HALF) for entry in plan],
            [pltpu.VMEM(entry[4:6], HALF if entry[2] == 0 else FULL) for entry in plan],
            pltpu.SemaphoreType.DMA((len(plan),)),
            pltpu.SemaphoreType.DMA((len(plan),)),
        ],
        compiler_params=pltpu.CompilerParams(vmem_limit_bytes=63 * 1024 * 1024),
        name="finish",
    )(*results)


def body(
    dec_in,
    enc_out,
    seg_dec,
    seg_enc,
    out_grad,
    gain_self,
    wq_self,
    wk_self,
    wv_self,
    wo_self,
    gain_cross,
    wq_cross,
    wk_cross,
    wv_cross,
    wo_cross,
    gain_ffn,
    w_gate,
    w_up,
    w_down,
):
    narrow = (wq_self, wk_self, wv_self, wo_self, wq_cross, wk_cross, wv_cross, wo_cross, w_down)
    position = jnp.arange(seg_dec.shape[1])
    causal = position[:, None] >= position[None, :]
    self_ok = (seg_dec[:, :, None] == seg_dec[:, None, :]) & causal[None]
    cross_ok = seg_dec[:, :, None] == seg_enc[:, None, :]
    if lax.axis_size("fsdp") == 8 and lax.axis_size("dp") == 4:
        back = layer_call(
            (wq_self, wk_self, wv_self, wo_self)
            + (wk_cross, wv_cross, wq_cross, wo_cross, w_gate, w_up, w_down),
            tuple(gain.reshape(1, -1) for gain in (gain_self, gain_cross, gain_ffn)),
            dec_in.reshape(-1, MODEL),
            enc_out.reshape(-1, MODEL),
            out_grad.reshape(-1, MODEL),
            seg_dec,
            seg_enc,
        )
        final = finish_call(back)
        squares = final[6:14]
        gain_grads = [grad.reshape(-1) for grad in final[14:17]]
        return (
            final[0].reshape(dec_in.shape),
            final[1].reshape(dec_in.shape),
            final[2].reshape(enc_out.shape),
            gain_grads[0],
            squares[WQ_A],
            squares[WK_A],
            squares[WV_A],
            squares[WO_A],
            gain_grads[1],
            squares[WQ_C],
            squares[WK_C],
            squares[WV_C],
            squares[WO_C],
            gain_grads[2],
            final[3],
            final[4],
            final[5],
        )
    gain_a, gain_c, gain_f = gather_group((gain_self, gain_cross, gain_ffn))
    full = gather_group(narrow)
    gate_full, up_full = gather_group((w_gate, w_up))
    get_self = lambda: (gain_a, *full[0:4])
    get_cross = lambda: (gain_c, *full[4:8])
    get_ffn = lambda: (gain_f, gate_full, up_full, full[8])
    kept = forward(dec_in, enc_out, self_ok, cross_ok, get_self, get_cross)
    result_rows, grad_rows_dec, grad_rows_enc, grads = backward(
        dec_in, enc_out, self_ok, cross_ok, out_grad, kept, get_self, get_cross, get_ffn
    )
    gains = reduce_group((grads[0], grads[5], grads[10]), (gain_self, gain_cross, gain_ffn))
    wide = reduce_group(grads[11:13], (w_gate, w_up))
    thin = reduce_group(grads[1:5] + grads[6:10] + grads[13:14], narrow)
    return (
        (result_rows, grad_rows_dec, grad_rows_enc, gains[0])
        + tuple(thin[0:4])
        + (gains[1],)
        + tuple(thin[4:8])
        + (gains[2], *wide, thin[8])
    )


def solution(mesh):
    placed = (
        P(("dp", "fsdp"), None, None),
        P(("dp", "fsdp"), None, None),
        P(("dp", "fsdp"), None),
        P(("dp", "fsdp"), None),
        P(("dp", "fsdp"), None, None),
        P("fsdp"),
        P("fsdp", None),
        P("fsdp", None),
        P("fsdp", None),
        P("fsdp", None),
        P("fsdp"),
        P("fsdp", None),
        P("fsdp", None),
        P("fsdp", None),
        P("fsdp", None),
        P("fsdp"),
        P("fsdp", None),
        P("fsdp", None),
        P("fsdp", None),
    )
    return jax.shard_map(
        body,
        mesh=mesh,
        in_specs=placed,
        out_specs=(
            P(("dp", "fsdp"), None, None),
            P(("dp", "fsdp"), None, None),
            P(("dp", "fsdp"), None, None),
            P("fsdp"),
            P("fsdp", None),
            P("fsdp", None),
            P("fsdp", None),
            P("fsdp", None),
            P("fsdp"),
            P("fsdp", None),
            P("fsdp", None),
            P("fsdp", None),
            P("fsdp", None),
            P("fsdp"),
            P("fsdp", None),
            P("fsdp", None),
            P("fsdp", None),
        ),
        check_vma=False,
    )
```

```python
import functools
import math

import jax
import jax.numpy as jnp
from jax import lax
from jax.experimental import pallas as pl
from jax.experimental.pallas import tpu as pltpu
from jax.sharding import PartitionSpec as P

HD = 64
MODEL = 768


EPSILON = 1e-06
MASKED = -1000000000.0


def rms_forward(values_in, gain_vec):
    return (
        values_in
        * lax.rsqrt(jnp.mean(values_in * values_in, axis=-1, keepdims=True) + EPSILON)
        * gain_vec
    )


def rms_backward(values_in, gain_low, grad_out):
    _, pullback = jax.vjp(rms_forward, values_in, gain_low.astype(jnp.float32))
    return pullback(grad_out)


def project(acts, weight):
    return jnp.einsum("rld,dn->rln", acts, weight, preferred_element_type=jnp.float32)


def weight_grad(acts, grad_out):
    return jnp.einsum("rld,rln->dn", acts, grad_out, preferred_element_type=jnp.float32)


def input_grad(grad_out, weight):
    return jnp.einsum("rln,dn->rld", grad_out, weight, preferred_element_type=jnp.float32)


def split_heads(tensor):
    return tensor.reshape(tensor.shape[0], tensor.shape[1], -1, HD)


def merge_heads(tensor):
    return tensor.reshape(tensor.shape[0], tensor.shape[1], -1)


def attention_probs(queries, keys_all, allowed):
    scores = jnp.einsum(
        "rqhd,rkhd->rhqk",
        split_heads(queries),
        split_heads(keys_all),
        preferred_element_type=jnp.float32,
    )
    scores = jnp.where(allowed[:, None], scores, MASKED)
    return jax.nn.softmax(scores, axis=-1)


def attend_forward(queries, keys_all, values, allowed):
    probs = attention_probs(queries, keys_all, allowed).astype(jnp.bfloat16)
    mixture = jnp.einsum(
        "rhqk,rkhd->rqhd", probs, split_heads(values), preferred_element_type=jnp.float32
    )
    return merge_heads(mixture).astype(jnp.bfloat16)


def attend_backward(queries, keys_all, values, allowed, grad_mix):
    weights_full = attention_probs(queries, keys_all, allowed)
    grad_heads = split_heads(grad_mix)
    grad_values = jnp.einsum(
        "rhqk,rqhd->rkhd",
        weights_full.astype(jnp.bfloat16),
        grad_heads,
        preferred_element_type=jnp.float32,
    )
    grad_weights = jnp.einsum(
        "rqhd,rkhd->rhqk", grad_heads, split_heads(values), preferred_element_type=jnp.float32
    )
    grad_scores = (
        weights_full * (grad_weights - jnp.sum(weights_full * grad_weights, axis=-1, keepdims=True))
    ).astype(jnp.bfloat16)
    grad_queries = jnp.einsum(
        "rhqk,rkhd->rqhd", grad_scores, split_heads(keys_all), preferred_element_type=jnp.float32
    ) * HD ** (-0.5)
    grad_keys = jnp.einsum(
        "rhqk,rqhd->rkhd", grad_scores, split_heads(queries), preferred_element_type=jnp.float32
    )
    return (
        merge_heads(grad_queries).astype(jnp.bfloat16),
        merge_heads(grad_keys).astype(jnp.bfloat16),
        merge_heads(grad_values).astype(jnp.bfloat16),
    )


def gather_group(shards):
    joined = jnp.concatenate(shards, axis=0)
    whole = lax.all_gather(joined, "fsdp", axis=0, tiled=False)
    parts = []
    start = 0
    for shard in shards:
        part = whole[:, start : start + shard.shape[0]]
        parts.append(part.reshape((-1,) + shard.shape[1:]))
        start += shard.shape[0]
    return parts


def reduce_group(gradients, shards):
    count = lax.axis_size("fsdp")
    joined = jnp.concatenate(
        [
            gradient.astype(jnp.bfloat16).reshape((count, -1) + gradient.shape[1:])
            for gradient in gradients
        ],
        axis=1,
    )
    owned = lax.psum_scatter(joined, "fsdp", scatter_dimension=0, tiled=False)
    quarter = lax.psum_scatter(owned, "dp", scatter_dimension=0, tiled=True)
    summed = lax.all_gather(quarter, "dp", axis=0, tiled=True)
    parts = []
    start = 0
    for shard in shards:
        part = summed[start : start + shard.shape[0]]
        parts.append(part.astype(jnp.float32))
        start += shard.shape[0]
    return parts


def forward(dec_rows, enc_rows, self_ok, cross_ok, get_self, get_cross):
    gain_a, wq_a, wk_a, wv_a, wo_a = get_self()
    dec_float = dec_rows.astype(jnp.float32)
    normed_a = rms_forward(dec_float, gain_a.astype(jnp.float32)).astype(jnp.bfloat16)
    query_a = (project(normed_a, wq_a) * HD ** (-0.5)).astype(jnp.bfloat16)
    keys_a = project(normed_a, wk_a).astype(jnp.bfloat16)
    values_a = project(normed_a, wv_a).astype(jnp.bfloat16)
    mix_a = attend_forward(query_a, keys_a, values_a, self_ok)
    after_self = dec_float + project(mix_a, wo_a)
    gain_c, wq_c, wk_c, wv_c, wo_c = get_cross()
    normed_c = rms_forward(after_self, gain_c.astype(jnp.float32)).astype(jnp.bfloat16)
    query_c = (project(normed_c, wq_c) * HD ** (-0.5)).astype(jnp.bfloat16)
    keys_c = project(enc_rows, wk_c).astype(jnp.bfloat16)
    values_c = project(enc_rows, wv_c).astype(jnp.bfloat16)
    mix_c = attend_forward(query_c, keys_c, values_c, cross_ok)
    after_cross = after_self + project(mix_c, wo_c)
    return (
        (normed_a, query_a, keys_a, values_a, mix_a, normed_c, query_c, mix_c),
        (keys_c, values_c),
        (after_self, after_cross),
    )


def backward(dec_rows, enc_rows, self_ok, cross_ok, grad_rows, kept, get_self, get_cross, get_ffn):
    (normed_a, query_a, keys_a, values_a, mix_a, normed_c, query_c, mix_c) = kept[0]
    keys_c, values_c = kept[1]
    after_self, after_cross = kept[2]
    dec_float = dec_rows.astype(jnp.float32)
    gain_f, gate_w, up_w, down_w = get_ffn()
    normed_f = rms_forward(after_cross, gain_f.astype(jnp.float32)).astype(jnp.bfloat16)
    gate_pre = project(normed_f, gate_w)
    up_pre = project(normed_f, up_w)
    hidden_low = (jax.nn.gelu(gate_pre, approximate=True) * up_pre).astype(jnp.bfloat16)
    dec_result = (after_cross + project(hidden_low, down_w)).astype(jnp.bfloat16)
    grad_res = grad_rows.astype(jnp.float32)
    grad_branch = grad_res.astype(jnp.bfloat16)
    grad_down = weight_grad(hidden_low, grad_branch)
    grad_hidden = input_grad(grad_branch, down_w)
    _, gelu_pull = jax.vjp(
        lambda gate_in, up_in: jax.nn.gelu(gate_in, approximate=True) * up_in, gate_pre, up_pre
    )
    grad_gate_pre, grad_up_pre = gelu_pull(grad_hidden)
    grad_gate_low = grad_gate_pre.astype(jnp.bfloat16)
    grad_up_low = grad_up_pre.astype(jnp.bfloat16)
    grad_gate = weight_grad(normed_f, grad_gate_low)
    grad_up = weight_grad(normed_f, grad_up_low)
    grad_normed = input_grad(grad_gate_low, gate_w) + input_grad(grad_up_low, up_w)
    grad_input, grad_gain_f = rms_backward(after_cross, gain_f, grad_normed)
    grad_res = grad_res + grad_input
    gain_c, wq_c, wk_c, wv_c, wo_c = get_cross()
    grad_branch = grad_res.astype(jnp.bfloat16)
    grad_wo_c = weight_grad(mix_c, grad_branch)
    grad_mix = input_grad(grad_branch, wo_c).astype(jnp.bfloat16)
    grad_query, grad_keys, grad_values = attend_backward(
        query_c, keys_c, values_c, cross_ok, grad_mix
    )
    grad_wq_c = weight_grad(normed_c, grad_query)
    grad_wk_c = weight_grad(enc_rows, grad_keys)
    grad_wv_c = weight_grad(enc_rows, grad_values)
    grad_enc_rows = input_grad(grad_keys, wk_c) + input_grad(grad_values, wv_c)
    grad_normed = input_grad(grad_query, wq_c)
    grad_input, grad_gain_c = rms_backward(after_self, gain_c, grad_normed)
    grad_res = grad_res + grad_input
    gain_a, wq_a, wk_a, wv_a, wo_a = get_self()
    grad_branch = grad_res.astype(jnp.bfloat16)
    grad_wo_a = weight_grad(mix_a, grad_branch)
    grad_mix = input_grad(grad_branch, wo_a).astype(jnp.bfloat16)
    grad_query, grad_keys, grad_values = attend_backward(
        query_a, keys_a, values_a, self_ok, grad_mix
    )
    grad_wq_a = weight_grad(normed_a, grad_query)
    grad_wk_a = weight_grad(normed_a, grad_keys)
    grad_wv_a = weight_grad(normed_a, grad_values)
    grad_normed = (
        input_grad(grad_query, wq_a) + input_grad(grad_keys, wk_a) + input_grad(grad_values, wv_a)
    )
    grad_input, grad_gain_a = rms_backward(dec_float, gain_a, grad_normed)
    grad_dec_rows = grad_res + grad_input
    full_grads = (
        grad_gain_a,
        grad_wq_a,
        grad_wk_a,
        grad_wv_a,
        grad_wo_a,
        grad_gain_c,
        grad_wq_c,
        grad_wk_c,
        grad_wv_c,
        grad_wo_c,
        grad_gain_f,
        grad_gate,
        grad_up,
        grad_down,
    )
    return (dec_result, grad_dec_rows, grad_enc_rows, full_grads)


def dot_nn(left, right):
    return lax.dot_general(left, right, (((1,), (0,)), ((), ())), preferred_element_type=jnp.float32)


def dot_nt(left, right):
    return lax.dot_general(left, right, (((1,), (1,)), ((), ())), preferred_element_type=jnp.float32)


def dot_tn(left, right):
    return lax.dot_general(left, right, (((0,), (0,)), ((), ())), preferred_element_type=jnp.float32)


def flip(index, step):
    return index + step - 2 * step * ((index // step) % 2)


class Place:
    def __init__(self):
        self.dp = lax.axis_index("dp")
        self.fs = lax.axis_index("fsdp")
        self.core = self.fs % 2
        self.x = (self.fs // 2) % 2
        self.y = (self.fs // 4) % 2
        self.inner = (self.dp * (3 - self.dp)) // 2

    def to_core(self):
        return (self.dp, flip(self.fs, 1))

    def to_x(self):
        return (self.dp, flip(self.fs, 2))

    def to_y(self):
        return (self.dp, flip(self.fs, 4))

    def to_pair(self):
        return (flip(self.dp, 1), self.fs)

    def to_middle(self):
        return (3 - self.dp, self.fs)


def remote(source, target, send_sem, recv_sem, device):
    return pltpu.make_async_remote_copy(
        src_ref=source,
        dst_ref=target,
        send_sem=send_sem,
        recv_sem=recv_sem,
        device_id=device,
        device_id_type=pl.DeviceIdType.MESH,
    )


def greet(devices):
    barrier = pltpu.get_barrier_semaphore()
    for device in devices:
        pl.semaphore_signal(
            barrier, inc=1, device_id=device, device_id_type=pl.DeviceIdType.MESH
        )


LINK_BYTES_PER_US = 44000.0
WINDOW = 8
QUARTERS = 4
SQUARE_RING = 2
PLANE_WINDOW_US = 2.5
WORK_SCALE = 1.2
GATHER_SLACK, REST_SLACK, WHOLE_SLACK = 0.0, 3.0, 3.0
CORE_SLACK, PLANE_SLACK, COLUMN_SLACK = 0.0, 0.0, 0.0
PAIRED = (("wide", 0), ("wide", 1), ("wide", 2), ("wide", 3))
LAST_PARTS = 3
HALF = jnp.bfloat16
FULL = jnp.float32


class Events:
    def __init__(self):
        self.now = 0.0
        self.heap = []
        self.count = 0
        self.free = {}
        self.plane_load = 0.0
        self.plane_queue = []

    def enter_plane(self, unit=None):
        if unit is not None:
            self.plane_queue.append(unit)
        while self.plane_queue and self.plane_load < PLANE_WINDOW_US:
            unit = self.plane_queue.pop(0)
            self.plane_load += unit.half_us
            unit.cross_plane()

    def leave_plane(self, unit):
        self.plane_load -= unit.half_us
        self.enter_plane()

    def post(self, ready, slack, action):
        self.count += 1
        self.heap.append((ready, ready + slack, self.count, action))

    def sent(self, links, micros, delay):
        ends = []
        for link in links:
            start = max(self.now, self.free.get(link, 0.0))
            self.free[link] = start + micros
            ends.append(start + micros + delay)
        return max(ends)

    def run(self, event):
        self.heap.remove(event)
        self.now = max(self.now, event[0]) + 0.2
        event[3]()

    def step(self):
        self.run(min(self.heap, key=lambda event: (event[1], event[2])))

    def until(self, holds):
        while not holds():
            self.step()

    def work(self, micros, action):
        while self.heap:
            event = min(self.heap, key=lambda event: (event[1], event[2]))
            if event[1] > self.now:
                break
            self.run(event)
        action()
        self.now += WORK_SCALE * micros

    def drain(self):
        while self.heap:
            self.step()


class Chunk:
    def __init__(self, events, place, shard, whole, part, micros, sems, stages, ready):
        self.events = events
        self.place = place
        self.shard = shard
        self.whole = whole
        self.start, self.rows, self.cols = part
        self.micros = micros
        self.send_sems, self.recv_sems, self.stage_sems, self.own_sems = sems
        self.stages = stages
        self.ready = ready
        self.following = None
        fs = place.fs
        even = 1 - place.dp % 2
        self.first = even * flip(fs, 2) + (1 - even) * flip(fs, 4)
        self.second = even * flip(fs, 4) + (1 - even) * flip(fs, 2)
        self.cross = flip(flip(fs, 2), 4)
        self.to = [
            (place.dp, self.first),
            (place.dp, self.second),
            place.to_pair(),
            place.to_core(),
        ]

    def own(self):
        return self.shard.at[pl.ds(self.start, self.rows), self.cols]

    def block(self, owner):
        return self.whole.at[pl.ds(owner * self.shard.shape[0] + self.start, self.rows), self.cols]

    def copy(self, flow, owner, own=False):
        return remote(
            self.own() if own else self.block(owner),
            self.block(owner),
            self.send_sems.at[flow],
            self.recv_sems.at[flow],
            self.to[min(flow, 3)],
        )

    def piece(self, ref, index):
        rows = self.rows // len(self.stages)
        return ref.at[pl.ds(index * rows, rows)] if len(self.stages) > 1 else ref

    def stage(self):
        return [
            pltpu.make_async_copy(self.piece(self.own(), index), held, self.stage_sems.at[index])
            for index, held in enumerate(self.stages)
        ]

    def keep(self):
        block = self.block(self.place.fs)
        return [
            pltpu.make_async_copy(held, self.piece(block, index), self.own_sems.at[index])
            for index, held in enumerate(self.stages)
        ]

    def begin(self):
        self.copy(0, self.place.fs, own=True).start()
        self.copy(3, self.place.fs, own=True).start()
        self.events.post(
            self.events.sent(["gather first"], self.micros, 2.5), GATHER_SLACK, self.relay_first
        )

    def relay_first(self):
        self.copy(0, self.first).wait_recv()
        self.copy(1, self.first).start()
        self.copy(2, self.first).start()
        self.copy(4, self.first).start()
        if self.following is not None:
            self.following.begin()
        self.events.post(
            self.events.sent(["gather second"], self.micros, 2.5), REST_SLACK, self.relay_rest
        )

    def relay_rest(self):
        self.copy(1, self.cross).wait_recv()
        self.copy(5, self.cross).start()
        self.copy(2, self.second).wait_recv()
        self.copy(6, self.second).start()
        self.events.post(self.events.now + 1.5, WHOLE_SLACK, self.finish)

    def finish(self):
        for flow, owner in ((3, self.place.fs), (4, self.first), (5, self.cross), (6, self.second)):
            self.copy(flow, flip(owner, 1)).wait_recv()
        self.ready()

    def drain(self):
        fs = self.place.fs
        owners = (fs, self.first, self.first, fs, self.first, self.cross, self.second)
        for flow in range(7):
            self.copy(flow, owners[flow], own=flow in (0, 3)).wait_send()


class Reduction:
    plane_flows = (1, 2, 3, 4)

    def __init__(self, events, place, buffers, sems, rows, cols, itemsize, finish):
        self.events = events
        self.place = place
        self.outgoing, self.first, self.along_x, self.along_y = buffers[0:4]
        self.second, self.far, self.final = buffers[4:7]
        self.send_sems, self.recv_sems = sems
        self.half_us = rows * cols * itemsize / LINK_BYTES_PER_US
        self.finish = finish
        self.merged = False

    def flows(self):
        at = self.place
        return (
            (self.outgoing.at[1 - at.core], self.first, at.to_core()),
            (self.first.at[:, 1 - at.x, 0], self.along_x, at.to_x()),
            (self.first.at[1 - at.y, :, 1], self.along_y, at.to_y()),
            (self.along_x.at[1 - at.y], self.second.at[0], at.to_y()),
            (self.along_y.at[1 - at.x], self.second.at[1], at.to_x()),
            (self.second, self.final, at.to_pair()),
            (self.second, self.far, at.to_middle()),
            (self.final, self.final, at.to_pair()),
        )

    def copy(self, flow):
        source, target, device = self.flows()[flow]
        return remote(source, target, self.send_sems.at[flow], self.recv_sems.at[flow], device)

    def begin(self):
        self.copy(0).start()
        self.events.post(self.events.sent(["core"], self.half_us * 0.8, 1.0), CORE_SLACK, self.merge_cores)

    def merge_cores(self):
        at = self.place
        self.copy(0).wait_recv()

        def add(index, carry):
            y, x, half = index // 4, (index // 2) % 2, index % 2
            self.first[y, x, half] = self.first[y, x, half] + self.outgoing[at.core, y, x, half]
            return carry

        lax.fori_loop(0, 8, add, 0)
        self.copy(0).wait_send()
        self.merged = True
        self.events.enter_plane(self)

    def cross_plane(self):
        self.copy(1).start()
        self.copy(2).start()
        self.events.post(self.events.sent(["first", "second"], 2 * self.half_us, 2.5), PLANE_SLACK, self.merge_first)

    def merge_first(self):
        at = self.place
        self.copy(1).wait_recv()
        self.copy(2).wait_recv()
        for index in range(2):
            self.along_x[index] = self.along_x[index] + self.first[index, at.x, 0]
            self.along_y[index] = self.along_y[index] + self.first[at.y, index, 1]
        self.copy(3).start()
        self.copy(4).start()
        self.events.post(self.events.sent(["first", "second"], self.half_us, 2.5), PLANE_SLACK, self.merge_second)
        self.events.leave_plane(self)

    def merge_second(self):
        at = self.place
        self.copy(3).wait_recv()
        self.copy(4).wait_recv()
        self.second[0] = self.second[0] + self.along_x[at.y]
        self.second[1] = self.second[1] + self.along_y[at.x]
        self.enter_column()

    def enter_column(self):
        at = self.place

        @pl.when(at.inner == 0)
        def _():
            self.copy(5).start()

        self.events.post(self.events.sent(["z"], 2 * self.half_us, 2.5), COLUMN_SLACK, self.merge_near)

    def merge_near(self):
        @pl.when(self.place.inner == 1)
        def _():
            self.copy(5).wait_recv()
            for half in range(2):
                self.second[half] = self.second[half] + self.final[half]
            self.copy(6).start()

        self.events.post(self.events.sent(["z middle"], 2 * self.half_us, 2.5), COLUMN_SLACK, self.merge_far)

    def merge_far(self):
        @pl.when(self.place.inner == 1)
        def _():
            self.copy(6).wait_recv()
            for half in range(2):
                self.final[half] = self.second[half] + self.far[half]
            self.copy(7).start()

        self.events.post(self.events.sent(["z back"], 2 * self.half_us, 2.5), COLUMN_SLACK, self.complete)

    def complete(self):
        @pl.when(self.place.inner == 0)
        def _():
            self.copy(7).wait_recv()

        self.finish(self.final)

    def drain(self):
        for flow in self.plane_flows:
            self.copy(flow).wait_send()

        @pl.when(self.place.inner == 0)
        def _():
            self.copy(5).wait_send()

        @pl.when(self.place.inner == 1)
        def _():
            self.copy(6).wait_send()
            self.copy(7).wait_send()


class PairReduction(Reduction):
    plane_flows = (1, 2, 3)

    def chips(self):
        at = self.place
        odd = at.dp % 2
        even = 1 - odd
        first = (even * at.y + odd * (1 - at.y), even * (1 - at.x) + odd * at.x)
        second = (1 - first[0], 1 - first[1])
        return first, second, (1 - at.y, 1 - at.x)

    def flows(self):
        at = self.place
        even = 1 - at.dp % 2
        first, second, opposite = self.chips()
        to_first = (at.dp, even * flip(at.fs, 2) + (1 - even) * flip(at.fs, 4))
        to_second = (at.dp, even * flip(at.fs, 4) + (1 - even) * flip(at.fs, 2))
        base = super().flows()
        return (
            base[0],
            (self.first.at[opposite[0], opposite[1]], self.along_x, to_second),
            (self.first.at[second[0], second[1]], self.along_y, at.to_pair()),
            (self.along_x, self.second, to_first),
            None,
            *base[5:],
        )

    def cross_plane(self):
        self.copy(1).start()
        self.copy(2).start()
        self.events.post(self.events.sent(["second", "z"], 2 * self.half_us, 2.5), PLANE_SLACK, self.merge_first)

    def merge_first(self):
        self.copy(1).wait_recv()
        self.copy(2).wait_recv()
        first = self.chips()[0]
        for half in range(2):
            self.along_x[half] = (
                self.along_x[half] + self.along_y[half] + self.first[first[0], first[1], half]
            )
        self.copy(3).start()
        self.events.post(self.events.sent(["first"], 2 * self.half_us, 2.5), PLANE_SLACK, self.merge_second)
        self.events.leave_plane(self)

    def merge_second(self):
        at = self.place
        self.copy(3).wait_recv()
        for half in range(2):
            self.second[half] = self.second[half] + self.first[at.y, at.x, half]
        self.enter_column()


def norm_rows(source, gain, target, rows, step):
    def body(index, carry):
        block = pl.ds(pl.multiple_of(index * step, step), step)
        values = source[block, :].astype(FULL)
        scale = lax.rsqrt(jnp.mean(values * values, axis=-1, keepdims=True) + EPSILON)
        target[block, :] = (values * scale * gain).astype(target.dtype)
        return carry

    lax.fori_loop(0, rows // step, body, 0)


def norm_back(source, gain, grad_norm, residual, low, rows, step):
    def body(index, total):
        block = pl.ds(pl.multiple_of(index * step, step), step)
        values = source[block, :].astype(FULL)
        scale = lax.rsqrt(jnp.mean(values * values, axis=-1, keepdims=True) + EPSILON)
        unit = values * scale
        grad = grad_norm[block, :]
        scaled = grad * gain
        change = scale * (scaled - unit * jnp.mean(scaled * unit, axis=-1, keepdims=True))
        updated = residual[block, :] + change
        residual[block, :] = updated
        low[block, :] = updated.astype(low.dtype)
        product = grad * unit
        for start in range(0, step, 8):
            total = total + product[start : start + 8]
        return total

    total = lax.fori_loop(0, rows // step, body, jnp.zeros((8, MODEL), FULL))
    return jnp.sum(total, axis=0, keepdims=True)


def make_masks(seg_dec, seg_enc, mask_self, mask_cross):
    rows, length = seg_dec.shape
    query = lax.broadcasted_iota(jnp.int32, (length, length), 0)
    key = lax.broadcasted_iota(jnp.int32, (length, length), 1)
    for row in range(rows):
        along = seg_dec[row : row + 1, :].astype(FULL)
        down = jnp.sum(jnp.where(query == key, along, 0.0), axis=1, keepdims=True)
        mask_self[row] = jnp.where((down == along) & (key <= query), 1.0, 0.0)
        enc = seg_enc[row : row + 1, :].astype(FULL)
        mask_cross[row] = jnp.where(down == enc, 1.0, 0.0)


class Heads:
    def __init__(self, queries, keys, values, mask, len_q, len_k, width):
        self.queries, self.keys, self.values, self.mask = queries, keys, values, mask
        self.len_q, self.len_k, self.width = len_q, len_k, width
        self.pairs = MODEL // (2 * HD)

    def lower(self, shape):
        return lax.broadcasted_iota(jnp.int32, shape, 1) < HD

    def stack(self, both):
        lower = self.lower((1, 2 * HD)).astype(FULL)
        upper = 1.0 - lower
        return jnp.concatenate([both * lower.astype(HALF), both * upper.astype(HALF)], axis=0)

    def join(self, stacked):
        top, bottom = stacked[: self.len_q], stacked[self.len_q :]
        return jnp.where(self.lower(top.shape), top, bottom)

    def places(self, step):
        found = []
        for near in range(self.width):
            index = step * self.width + near
            row, pair = index // self.pairs, index % self.pairs
            cols = pl.ds(pl.multiple_of(pair * 2 * HD, 2 * HD), 2 * HD)
            at_q = pl.ds(pl.multiple_of(row * self.len_q, 16), self.len_q)
            at_k = pl.ds(pl.multiple_of(row * self.len_k, 16), self.len_k)
            found.append((row, at_q, at_k, cols))
        return found

    def probs(self, rows, queries, keys):
        scores = [dot_nt(query, key) for query, key in zip(queries, keys)]
        split = (2, self.len_q, self.len_k)
        scores = [
            jnp.where(self.mask[row][None] > 0.0, score.reshape(split), MASKED)
            for row, score in zip(rows, scores)
        ]
        scores = [score.reshape(2 * self.len_q, self.len_k) for score in scores]
        powers = [jnp.exp(score - jnp.max(score, axis=-1, keepdims=True)) for score in scores]
        return [power * (1.0 / jnp.sum(power, axis=-1, keepdims=True)) for power in powers]

    def forward(self, target, first, last):
        def body(step, carry):
            places = self.places(step)
            rows = [place[0] for place in places]
            queries = [self.stack(self.queries[at_q, cols]) for _, at_q, _, cols in places]
            keys = [self.keys[at_k, cols] for _, _, at_k, cols in places]
            values = [self.values[at_k, cols] for _, _, at_k, cols in places]
            probs = self.probs(rows, queries, keys)
            mixed = [dot_nn(prob.astype(HALF), value) for prob, value in zip(probs, values)]
            for (_, at_q, _, cols), mix in zip(places, mixed):
                target[at_q, cols] = self.join(mix).astype(HALF)
            return carry

        lax.fori_loop(first // self.width, last // self.width, body, 0)

    def backward(self, grads, first, last):
        def body(step, carry):
            places = self.places(step)
            rows = [place[0] for place in places]
            queries = [self.stack(self.queries[at_q, cols]) for _, at_q, _, cols in places]
            keys = [self.keys[at_k, cols] for _, _, at_k, cols in places]
            values = [self.values[at_k, cols] for _, _, at_k, cols in places]
            grad = [self.stack(grads[at_q, cols]) for _, at_q, _, cols in places]
            each = range(self.width)
            grad_p = [dot_nt(grad[i], values[i]) for i in each]
            probs = self.probs(rows, queries, keys)
            grad_v = [dot_tn(probs[i].astype(HALF), grad[i]) for i in each]
            inner = [jnp.sum(probs[i] * grad_p[i], axis=-1, keepdims=True) for i in each]
            grad_s = [(probs[i] * (grad_p[i] - inner[i])).astype(HALF) for i in each]
            grad_q = [self.join(dot_nn(grad_s[i], keys[i])) * HD ** (-0.5) for i in each]
            grad_k = [dot_tn(grad_s[i], queries[i]) for i in each]
            for i, (_, at_q, at_k, cols) in enumerate(places):
                self.queries[at_q, cols] = grad_q[i].astype(HALF)
                self.keys[at_k, cols] = grad_k[i].astype(HALF)
                self.values[at_k, cols] = grad_v[i].astype(HALF)
            return carry

        lax.fori_loop(first // self.width, last // self.width, body, 0)


GELU_SCALE = (2.0 / math.pi) ** 0.5


def gelu_rows(gate_pre, up_pre, grad_hidden, hidden, grad_gate, grad_up, rows, step):
    def body(index, carry):
        block = pl.ds(pl.multiple_of(index * step, step), step)
        gate, up, grad = gate_pre[block, :], up_pre[block, :], grad_hidden[block, :]
        square = gate * gate
        bend = jnp.tanh(GELU_SCALE * gate * (1.0 + 0.044715 * square))
        rise = 0.5 * (1.0 + bend)
        value = gate * rise
        slope = rise + 0.5 * gate * (1.0 - bend * bend) * GELU_SCALE * (1.0 + 3 * 0.044715 * square)
        hidden[block, :] = (value * up).astype(HALF)
        grad_gate[block, :] = (grad * up * slope).astype(HALF)
        grad_up[block, :] = (grad * value).astype(HALF)
        return carry

    lax.fori_loop(0, rows // step, body, 0)


WQ_A, WK_A, WV_A, WO_A, WK_C, WV_C, WQ_C, WO_C, GATE, UP, DOWN, GAINS = range(12)
GATHER_ORDER = (WK_C, WQ_A, WK_A, WV_A, WO_A, WV_C, WQ_C, WO_C)
SLOTS = {WK_C: 1, WQ_A: 0, WK_A: 3, WV_A: 2, WO_A: 4, WV_C: 2, WQ_C: 3, WO_C: 0}
SLOTS_BACK = {WQ_A: 0, WK_A: 3, WV_A: 4}


def layer_kernel(dims, *refs):
    rows, len_q, len_k, count = dims
    tokens = rows * len_q
    shards, gain_shards = refs[0:11], refs[11:14]
    dec_hbm, enc_hbm, grad_hbm, seg_dec, seg_enc = refs[14:19]
    whole = refs[19:30]
    dec_out, grad_dec_out, grad_enc_out, gate_out, up_out, down_out, square_out, gain_out = refs[30:38]
    (gate_w, up_w, down_w, square_w, small, large, floats, enc, grad_low) = refs[38:47]
    (gain_tile, gains, mask_self, mask_cross, gate_pre, up_pre, grad_hidden) = refs[47:54]
    (hidden, grad_gate, grad_up, grad_norm, result, grad_mix, gain_grads) = refs[54:61]
    residual = result
    dec = grad_mix
    wide_bufs, tall_bufs, square_bufs, gain_bufs = refs[61:68], refs[68:75], refs[75:82], refs[82:89]
    last_bufs = refs[89:96]
    gather_send, gather_recv, stage_sems, own_sems, send_sems, recv_sems = refs[96:102]
    load_sems, weight_sems, store_sems = refs[102:105]

    place = Place()
    events = Events()
    loads = {}
    stores = []
    ff_part = whole[DOWN].shape[0] // QUARTERS
    pairs_all = rows * (MODEL // (2 * HD))

    def load(name, source, target, sem):
        loads[name] = pltpu.make_async_copy(source, target, sem)
        loads[name].start()

    def store(source, target):
        stores.append(pltpu.make_async_copy(source, target, store_sems.at[len(stores)]))
        stores[-1].start()

    neighbours = [
        place.to_core(), place.to_x(), place.to_y(), place.to_pair(), place.to_middle()
    ]
    greet(neighbours)
    load("dec", dec_hbm, dec, load_sems.at[0])
    load("enc", enc_hbm, enc, load_sems.at[1])
    load("grad", grad_hbm, grad_low, load_sems.at[2])
    gain_tile[...] = jnp.zeros(gain_tile.shape, FULL)
    for which, shard in enumerate(gain_shards):
        gain_tile[which : which + 1, 0 : shard.shape[1]] = shard[...].astype(FULL)

    gathered = {}
    slot_free = {slot: True for slot in range(5)}
    waiting = []

    def try_loads():
        for entry in list(waiting):
            ready, slot, start = entry
            if ready() and slot_free[slot]:
                slot_free[slot] = False
                start()
                waiting.remove(entry)

    def want(name, ready, slot, start):
        slot_free.setdefault(slot, True)
        waiting.append((ready, slot, start))
        try_loads()

    def release(slot):
        slot_free[slot] = True
        try_loads()

    def want_square(which, slot, name):
        want(
            name,
            lambda: gathered.get(which, False),
            slot,
            lambda: load(name, whole[which], square_w.at[slot], weight_sems.at[slot]),
        )

    def want_quarter(quarter):
        slot = quarter % 2
        part = pl.ds(quarter * ff_part, ff_part)

        def start():
            load(("gate", quarter), whole[GATE].at[:, part], gate_w.at[slot], weight_sems.at[5 + slot])
            load(("up", quarter), whole[UP].at[:, part], up_w.at[slot], weight_sems.at[7 + slot])
            load(("down", quarter), whole[DOWN].at[part], down_w.at[slot], weight_sems.at[9 + slot])

        want(
            ("quarter", quarter),
            lambda: gathered.get(DOWN, False) and gathered.get((UP, quarter), False),
            ("ffn", slot),
            start,
        )

    for which in GATHER_ORDER:
        want_square(which, SLOTS[which], ("square", which))
    for quarter in range(QUARTERS):
        want_quarter(quarter)

    def need(name):
        events.until(lambda: name in loads)
        loads[name].wait()

    chunks = []

    def add_chunk(shard, target, start, height, cols, name, stages):
        index = len(chunks)
        width = cols.size if cols is not None else shard.shape[1]
        itemsize = jnp.dtype(shard.dtype).itemsize

        def ready():
            if name is not None:
                gathered[name] = True
                try_loads()

        chunks.append(
            Chunk(
                events,
                place,
                shard,
                target,
                (start, height, slice(None) if cols is None else cols),
                height * width * itemsize / LINK_BYTES_PER_US,
                (
                    gather_send.at[index],
                    gather_recv.at[index],
                    stage_sems.at[index],
                    own_sems.at[index],
                ),
                stages,
                ready,
            )
        )

    for index, which in enumerate(GATHER_ORDER):
        if index == 1:
            add_chunk(gain_tile, gains, 0, 8, None, GAINS, [gain_bufs[0].at[0, 0, 0, 0, 0]])
        held = square_bufs[0].at[0, index // 4, (index // 2) % 2, index % 2]
        add_chunk(
            shards[which],
            whole[which],
            0,
            shards[which].shape[0],
            None,
            which,
            [held.at[0], held.at[1]],
        )
    down_rows = shards[DOWN].shape[0]
    for part in range(4):
        piece = down_rows // 4
        add_chunk(
            shards[DOWN],
            whole[DOWN],
            part * piece,
            piece,
            None,
            DOWN if part == 3 else None,
            [tall_bufs[0].at[0, 0, 0, part // 2, part % 2]],
        )
    for quarter in range(QUARTERS):
        for which in (GATE, UP):
            add_chunk(
                shards[which],
                whole[which],
                0,
                shards[which].shape[0],
                pl.ds(quarter * ff_part, ff_part),
                (which, quarter),
                [wide_bufs[0].at[0, 0, quarter // 2, quarter % 2, which - GATE]],
            )
    for index, chunk in enumerate(chunks):
        if index + WINDOW < len(chunks):
            chunk.following = chunks[index + WINDOW]
    for chunk in chunks:
        for copy in chunk.stage():
            copy.start()
    pl.semaphore_wait(pltpu.get_barrier_semaphore(), len(neighbours))
    for chunk in chunks[:WINDOW]:
        chunk.begin()
    for chunk in chunks:
        for staged, kept in zip(chunk.stage(), chunk.keep()):
            staged.wait()
            kept.start()

    def gain_row(which):
        width = MODEL // count
        return jnp.concatenate(
            [gains[8 * owner + which : 8 * owner + which + 1, 0:width] for owner in range(count)],
            axis=1,
        )

    def masks():
        make_masks(seg_dec, seg_enc, mask_self, mask_cross)
        gain_grads[...] = jnp.zeros(gain_grads.shape, FULL)
        loads["dec"].wait()
        for chunk in chunks:
            for kept in chunk.keep():
                kept.wait()

    def project(acts, which, target, scale=None, free=True):
        name = ("square", which)
        need(name)

        def run():
            value = dot_nn(acts[...], square_w[SLOTS[which]])
            if scale is not None:
                value = value * scale
            target[...] = value.astype(target.dtype)
            if free:
                release(SLOTS[which])

        events.work(0.6 * acts.shape[0] / tokens, run)

    def residual_add(before, acts, which, after, free):
        need(("square", which))

        def run():
            after[...] = before[...].astype(FULL) + dot_nn(acts[...], square_w[SLOTS[which]])

        events.work(0.8, run)

    def norm(source, which, target):
        events.work(
            0.4, lambda: norm_rows(source, gain_row(which), target, tokens, len_q)
        )

    def attend(heads, target, parts, micros):
        for part in range(parts):
            bounds = (part * pairs_all // parts, (part + 1) * pairs_all // parts)
            events.work(micros / parts, functools.partial(heads.forward, target, *bounds))

    self_heads = Heads(small.at[1], small.at[2], small.at[3], mask_self, len_q, len_q, 3)
    cross_heads = Heads(small.at[6], large.at[0], large.at[1], mask_cross, len_q, len_k, 2)
    root = HD ** (-0.5)

    events.work(0.5, masks)
    loads["enc"].wait()
    project(enc, WK_C, large.at[0], free=False)
    events.until(lambda: GAINS in gathered)
    norm(dec, 0, small.at[0])
    project(small.at[0], WQ_A, small.at[1], scale=root)
    project(small.at[0], WK_A, small.at[2])
    project(small.at[0], WV_A, small.at[3])
    attend(self_heads, small.at[4], 4, 3.0)
    residual_add(dec, small.at[4], WO_A, floats.at[0], False)
    norm(floats.at[0], 1, small.at[5])
    project(enc, WV_C, large.at[1], free=False)
    project(small.at[5], WQ_C, small.at[6], scale=root, free=False)
    attend(cross_heads, small.at[7], 6, 5.4)
    residual_add(floats.at[0], small.at[7], WO_C, floats.at[1], False)
    norm(floats.at[1], 2, small.at[8])
    loads["grad"].wait()

    units = []

    def unit_of(buffers, index, slot, finish, paired=False):
        number = len(units)
        final = buffers[6]
        unit = (PairReduction if paired else Reduction)(
            events,
            place,
            (buffers[0].at[slot], *(buffer.at[index] for buffer in buffers[1:7])),
            (send_sems.at[number], recv_sems.at[number]),
            final.shape[-2],
            final.shape[-1],
            jnp.dtype(final.dtype).itemsize,
            finish,
        )
        units.append(unit)
        return unit

    def claim(earlier):
        events.until(lambda: earlier.merged)

    wide_units = []

    def ffn_forward(quarter):
        slot = quarter % 2
        gate_pre[...] = dot_nn(small[8], gate_w[slot])
        up_pre[...] = dot_nn(small[8], up_w[slot])
        grad_hidden[...] = dot_nt(grad_low[...], down_w[slot])

    def ffn_gelu():
        gelu_rows(gate_pre, up_pre, grad_hidden, hidden, grad_gate, grad_up, tokens, len_q)

    def ffn_wide(quarter):
        def finish(final):
            part = pl.ds(quarter * ff_part, ff_part)
            store(final.at[0], gate_out.at[:, part])
            store(final.at[1], up_out.at[:, part])

        unit = unit_of(wide_bufs, quarter, 0, finish, ("wide", quarter) in PAIRED)
        wide_units.append(unit)
        height = MODEL // count
        for half, grads in enumerate((grad_gate, grad_up)):
            value = dot_tn(small[8], grads[...]).astype(HALF)
            for owner in range(count):
                unit.outgoing[owner % 2, owner // 4, (owner // 2) % 2, half] = value[
                    owner * height : (owner + 1) * height
                ]
        unit.begin()

    def ffn_tall(quarter):
        value = dot_tn(hidden[...], grad_low[...]).astype(HALF)
        owners = count // QUARTERS
        height = ff_part // owners
        piece = height // 4
        for near in range(owners):
            owner = quarter * owners + near
            for part in range(4):
                start = near * height + part * piece
                tall_bufs[0][part // 2, owner % 2, owner // 4, (owner // 2) % 2, part % 2] = value[
                    start : start + piece
                ]

    def ffn_rest(quarter):
        slot = quarter % 2
        change = dot_nt(grad_gate[...], gate_w[slot]) + dot_nt(grad_up[...], up_w[slot])
        output = dot_nn(hidden[...], down_w[slot])
        if quarter == 0:
            grad_norm[...] = change
            result[...] = floats[1] + output
        else:
            grad_norm[...] += change
            result[...] += output
        release(("ffn", slot))

    for quarter in range(QUARTERS):
        for kind in ("gate", "up", "down"):
            need((kind, quarter))
        events.work(1.1, functools.partial(ffn_forward, quarter))
        events.work(0.2, ffn_gelu)
        if quarter >= 1:
            claim(wide_units[quarter - 1])
        events.work(1.1, functools.partial(ffn_wide, quarter))
        events.work(0.8, functools.partial(ffn_tall, quarter))
        events.work(1.2, functools.partial(ffn_rest, quarter))

    def start_tall():
        for part in range(2):

            def finish(final, part=part):
                piece = final.shape[1]
                for half in range(2):
                    store(final.at[half], down_out.at[pl.ds((2 * part + half) * piece, piece)])

            unit_of(tall_bufs, part, part, finish).begin()

    def ffn_norm():
        small[8] = result[...].astype(HALF)
        store(small.at[8], dec_out)
        residual[...] = grad_low[...].astype(FULL)
        gain_grads[2:3, :] = norm_back(
            floats.at[1], gain_row(2), grad_norm, residual, grad_low, tokens, len_q
        )

    events.work(0.1, start_tall)
    events.work(1.0, ffn_norm)

    square_units = []

    def square_grad(which, acts, grads):
        index = len(square_units)
        height = MODEL // count

        def finish(final):
            piece = final.shape[1]
            for half in range(2):
                store(final.at[half], square_out.at[which, pl.ds(half * piece, piece)])

        if index >= SQUARE_RING:
            claim(square_units[index - SQUARE_RING])
        unit = unit_of(
            square_bufs, index, index % SQUARE_RING, finish, ("square", index) in PAIRED
        )
        square_units.append(unit)

        def compute():
            value = dot_tn(acts[...], grads[...]).astype(HALF)
            piece = height // 2
            for owner in range(count):
                for half in range(2):
                    start = owner * height + half * piece
                    unit.outgoing[owner % 2, owner // 4, (owner // 2) % 2, half] = value[
                        start : start + piece
                    ]
            unit.begin()

        events.work(0.9 if acts.shape[0] == tokens else 1.5, compute)

    last_units = []

    def last_grad(which, acts, grads):
        index = len(last_units)
        height = MODEL // count
        piece = height // 2
        width = MODEL // LAST_PARTS
        parts = []
        for part in range(LAST_PARTS):
            cols = pl.ds(part * width, width)

            def finish(final, cols=cols):
                for half in range(2):
                    store(final.at[half], square_out.at[which, pl.ds(half * piece, piece), cols])

            if index:
                claim(last_units[index - LAST_PARTS + part])
            parts.append(unit_of(last_bufs, index + part, part, finish))
        last_units.extend(parts)

        def compute():
            value = dot_tn(acts[...], grads[...]).astype(HALF)
            for part, unit in enumerate(parts):
                for owner in range(count):
                    for half in range(2):
                        start = owner * height + half * piece
                        unit.outgoing[owner % 2, owner // 4, (owner // 2) % 2, half] = value[
                            start : start + piece, part * width : (part + 1) * width
                        ]
                unit.begin()

        events.work(1.0, compute)

    def mix_grad(which):
        def run():
            grad_mix[...] = dot_nt(grad_low[...], square_w[SLOTS[which]]).astype(HALF)
            release(SLOTS[which])

        events.work(0.8, run)

    def attend_back(heads, parts, micros):
        for part in range(parts):
            bounds = (part * pairs_all // parts, (part + 1) * pairs_all // parts)
            events.work(micros / parts, functools.partial(heads.backward, grad_mix, *bounds))

    square_grad(WO_C, small.at[7], grad_low)
    mix_grad(WO_C)
    want_square(WQ_A, SLOTS_BACK[WQ_A], ("back", WQ_A))
    attend_back(cross_heads, 6, 10.0)
    square_grad(WK_C, enc, large.at[0])
    square_grad(WV_C, enc, large.at[1])
    square_grad(WQ_C, small.at[5], small.at[6])

    def cross_back():
        grad_norm[...] = dot_nt(small[6], square_w[SLOTS[WQ_C]])
        release(SLOTS[WQ_C])

    events.work(0.7, cross_back)

    def cross_norm():
        gain_grads[1:2, :] = norm_back(
            floats.at[0], gain_row(1), grad_norm, residual, grad_low, tokens, len_q
        )

    events.work(0.7, cross_norm)
    want_square(WK_A, SLOTS_BACK[WK_A], ("back", WK_A))

    square_grad(WO_A, small.at[4], grad_low)
    mix_grad(WO_A)
    want_square(WV_A, SLOTS_BACK[WV_A], ("back", WV_A))
    attend_back(self_heads, 4, 6.0)
    load("dec again", dec_hbm, dec, load_sems.at[0])
    last_grad(WQ_A, small.at[0], small.at[1])
    last_grad(WK_A, small.at[0], small.at[2])
    last_grad(WV_A, small.at[0], small.at[3])

    def self_back(index, which):
        part = dot_nt(small[1 + index], square_w[SLOTS_BACK[which]])
        if index == 0:
            grad_norm[...] = part
        else:
            grad_norm[...] += part

    for index, which in enumerate((WQ_A, WK_A, WV_A)):
        need(("back", which))
        events.work(0.7, functools.partial(self_back, index, which))

    def self_norm():
        loads["dec again"].wait()
        gain_grads[0:1, :] = norm_back(
            dec, gain_row(0), grad_norm, residual, grad_low, tokens, len_q
        )
        store(grad_low, grad_dec_out)
        width = MODEL // count
        unit = unit_of(gain_bufs, 0, 0, lambda final: store(final, gain_out))
        unit.outgoing[...] = jnp.zeros(unit.outgoing.shape, FULL)
        for owner in range(count):
            unit.outgoing[owner % 2, owner // 4, (owner // 2) % 2, 0, :, 0:width] = gain_grads[
                :, owner * width : (owner + 1) * width
            ]
        unit.begin()

    events.work(0.8, self_norm)

    def enc_grad(part):
        block = pl.ds(part * (enc.shape[0] // 4), enc.shape[0] // 4)
        value = dot_nt(large[0, block], square_w[SLOTS[WK_C]])
        value = value + dot_nt(large[1, block], square_w[SLOTS[WV_C]])
        enc[block, :] = value.astype(HALF)
        store(enc.at[block], grad_enc_out.at[block])

    for part in range(4):
        events.work(0.8, functools.partial(enc_grad, part))
    events.drain()
    for chunk in chunks:
        chunk.drain()
    for unit in units:
        unit.drain()
    for copy in stores:
        copy.wait()


def layer_call(shards, gain_shards, dec, enc, grad, seg_dec, seg_enc):
    rows, len_q = seg_dec.shape
    len_k = seg_enc.shape[1]
    count = lax.axis_size("fsdp")
    tokens, enc_tokens = rows * len_q, rows * len_k
    hidden_units = shards[DOWN].shape[0] * count
    ff_part = hidden_units // QUARTERS
    height = MODEL // count
    down_height = hidden_units // count
    in_any = pl.BlockSpec(memory_space=pl.ANY)
    in_vmem = pl.BlockSpec(memory_space=pltpu.VMEM)

    def buffers(number, ring, height, width, kind):
        return [
            pltpu.VMEM((ring, 2, 2, 2, 2, height, width), kind),
            pltpu.VMEM((number, 2, 2, 2, height, width), kind),
            *[pltpu.VMEM((number, 2, height, width), kind)] * 5,
        ]

    n_chunks = 1 + 8 + 4 + 2 * QUARTERS
    n_units = QUARTERS + 2 + 5 + 3 * LAST_PARTS + 1
    wholes = [
        jax.ShapeDtypeStruct((shard.shape[0] * count, shard.shape[1]), shard.dtype)
        for shard in shards
    ]
    results = pl.pallas_call(
        functools.partial(layer_kernel, (rows, len_q, len_k, count)),
        out_shape=wholes
        + [
            jax.ShapeDtypeStruct((tokens, MODEL), HALF),
            jax.ShapeDtypeStruct((tokens, MODEL), HALF),
            jax.ShapeDtypeStruct((enc_tokens, MODEL), HALF),
            jax.ShapeDtypeStruct((height, hidden_units), HALF),
            jax.ShapeDtypeStruct((height, hidden_units), HALF),
            jax.ShapeDtypeStruct((down_height, MODEL), HALF),
            jax.ShapeDtypeStruct((8, height, MODEL), HALF),
            jax.ShapeDtypeStruct((2, 8, 128), FULL),
        ],
        in_specs=[in_any] * 11 + [in_vmem] * 3 + [in_any] * 3 + [in_vmem] * 2,
        out_specs=[in_any] * 19,
        scratch_shapes=[
            pltpu.VMEM((2, MODEL, ff_part), HALF),
            pltpu.VMEM((2, MODEL, ff_part), HALF),
            pltpu.VMEM((2, ff_part, MODEL), HALF),
            pltpu.VMEM((5, MODEL, MODEL), HALF),
            pltpu.VMEM((9, tokens, MODEL), HALF),
            pltpu.VMEM((2, enc_tokens, MODEL), HALF),
            pltpu.VMEM((2, tokens, MODEL), FULL),
            pltpu.VMEM((enc_tokens, MODEL), HALF),
            pltpu.VMEM((tokens, MODEL), HALF),
            pltpu.VMEM((8, 128), FULL),
            pltpu.VMEM((8 * count, 128), FULL),
            pltpu.VMEM((rows, len_q, len_q), FULL),
            pltpu.VMEM((rows, len_q, len_k), FULL),
            *[pltpu.VMEM((tokens, ff_part), FULL)] * 3,
            *[pltpu.VMEM((tokens, ff_part), HALF)] * 3,
            pltpu.VMEM((tokens, MODEL), FULL),
            pltpu.VMEM((tokens, MODEL), FULL),
            pltpu.VMEM((tokens, MODEL), HALF),
            pltpu.VMEM((8, MODEL), FULL),
            *buffers(QUARTERS, 1, height, ff_part, HALF),
            *buffers(2, 2, down_height // 4, MODEL, HALF),
            *buffers(5, SQUARE_RING, height // 2, MODEL, HALF),
            *buffers(1, 1, 8, 128, FULL),
            *buffers(3 * LAST_PARTS, LAST_PARTS, height // 2, MODEL // LAST_PARTS, HALF),
            pltpu.SemaphoreType.DMA((n_chunks, 7)),
            pltpu.SemaphoreType.DMA((n_chunks, 7)),
            pltpu.SemaphoreType.DMA((n_chunks, 2)),
            pltpu.SemaphoreType.DMA((n_chunks, 2)),
            pltpu.SemaphoreType.DMA((n_units, 8)),
            pltpu.SemaphoreType.DMA((n_units, 8)),
            pltpu.SemaphoreType.DMA((3,)),
            pltpu.SemaphoreType.DMA((11,)),
            pltpu.SemaphoreType.DMA((48,)),
        ],
        compiler_params=pltpu.CompilerParams(
            collective_id=0,
            has_side_effects=True,
            vmem_limit_bytes=63 * 1024 * 1024 + 512 * 1024,
        ),
        name="layer",
    )(*shards, *gain_shards, dec, enc, grad, seg_dec, seg_enc)
    return results[11:]


def finish_kernel(plan, *refs):
    n_in, n_out = 7, 14
    sources, gain_grads = refs[0:n_in], refs[n_in]
    targets = refs[n_in + 1 : n_in + 1 + n_out]
    gain_targets = refs[n_in + 1 + n_out : n_in + 4 + n_out]
    taken, made = refs[n_in + 4 + n_out : n_in + 6 + n_out]
    in_sems, out_sems = refs[n_in + 6 + n_out :]
    reads, writes = [], []
    for index, (source, source_at, target, target_at, _, _) in enumerate(plan):
        reads.append(
            pltpu.make_async_copy(
                sources[source].at[source_at], taken[index], in_sems.at[index]
            )
        )
        writes.append(
            pltpu.make_async_copy(made[index], targets[target].at[target_at], out_sems.at[index])
        )
    for copy in reads:
        copy.start()
    for index, target in enumerate(gain_targets):
        target[...] = gain_grads[0, index : index + 1, 0 : target.shape[1]]
    for index in range(len(plan)):
        reads[index].wait()
        made[index][...] = taken[index][...].astype(made[index].dtype)
        writes[index].start()
    for copy in writes:
        copy.wait()


def finish_call(results):
    everything = slice(None)
    plan = []

    def add(source, source_at, target, target_at, shape):
        plan.append((source, source_at, target, target_at, *shape))

    enc_rows = results[2].shape[0]
    for part in range(4):
        block = pl.ds(part * enc_rows // 4, enc_rows // 4)
        add(2, (block, everything), 2, (block, everything), (enc_rows // 4, MODEL))
    for index in (3, 4, 5, 1):
        add(index, (everything, everything), index, (everything, everything), results[index].shape)
    for index in range(8):
        add(6, (index, everything, everything), 6 + index, (everything, everything), results[6].shape[1:])
    add(0, (everything, everything), 0, (everything, everything), results[0].shape)
    shapes = [jax.ShapeDtypeStruct(results[0].shape, HALF)]
    shapes += [jax.ShapeDtypeStruct(results[index].shape, FULL) for index in range(1, 6)]
    shapes += [jax.ShapeDtypeStruct(results[6].shape[1:], FULL)] * 8
    gain = results[6].shape[1]
    in_any = pl.BlockSpec(memory_space=pl.ANY)
    in_vmem = pl.BlockSpec(memory_space=pltpu.VMEM)
    return pl.pallas_call(
        functools.partial(finish_kernel, plan),
        out_shape=shapes + [jax.ShapeDtypeStruct((1, gain), FULL)] * 3,
        in_specs=[in_any] * 7 + [in_vmem],
        out_specs=[in_any] * 14 + [in_vmem] * 3,
        scratch_shapes=[
            [pltpu.VMEM(entry[4:6], HALF) for entry in plan],
            [pltpu.VMEM(entry[4:6], HALF if entry[2] == 0 else FULL) for entry in plan],
            pltpu.SemaphoreType.DMA((len(plan),)),
            pltpu.SemaphoreType.DMA((len(plan),)),
        ],
        compiler_params=pltpu.CompilerParams(vmem_limit_bytes=63 * 1024 * 1024),
        name="finish",
    )(*results)


def body(
    dec_in,
    enc_out,
    seg_dec,
    seg_enc,
    out_grad,
    gain_self,
    wq_self,
    wk_self,
    wv_self,
    wo_self,
    gain_cross,
    wq_cross,
    wk_cross,
    wv_cross,
    wo_cross,
    gain_ffn,
    w_gate,
    w_up,
    w_down,
):
    narrow = (wq_self, wk_self, wv_self, wo_self, wq_cross, wk_cross, wv_cross, wo_cross, w_down)
    position = jnp.arange(seg_dec.shape[1])
    causal = position[:, None] >= position[None, :]
    self_ok = (seg_dec[:, :, None] == seg_dec[:, None, :]) & causal[None]
    cross_ok = seg_dec[:, :, None] == seg_enc[:, None, :]
    if lax.axis_size("fsdp") == 8 and lax.axis_size("dp") == 4:
        back = layer_call(
            (wq_self, wk_self, wv_self, wo_self)
            + (wk_cross, wv_cross, wq_cross, wo_cross, w_gate, w_up, w_down),
            tuple(gain.reshape(1, -1) for gain in (gain_self, gain_cross, gain_ffn)),
            dec_in.reshape(-1, MODEL),
            enc_out.reshape(-1, MODEL),
            out_grad.reshape(-1, MODEL),
            seg_dec,
            seg_enc,
        )
        final = finish_call(back)
        squares = final[6:14]
        gain_grads = [grad.reshape(-1) for grad in final[14:17]]
        return (
            final[0].reshape(dec_in.shape),
            final[1].reshape(dec_in.shape),
            final[2].reshape(enc_out.shape),
            gain_grads[0],
            squares[WQ_A],
            squares[WK_A],
            squares[WV_A],
            squares[WO_A],
            gain_grads[1],
            squares[WQ_C],
            squares[WK_C],
            squares[WV_C],
            squares[WO_C],
            gain_grads[2],
            final[3],
            final[4],
            final[5],
        )
    gain_a, gain_c, gain_f = gather_group((gain_self, gain_cross, gain_ffn))
    full = gather_group(narrow)
    gate_full, up_full = gather_group((w_gate, w_up))
    get_self = lambda: (gain_a, *full[0:4])
    get_cross = lambda: (gain_c, *full[4:8])
    get_ffn = lambda: (gain_f, gate_full, up_full, full[8])
    kept = forward(dec_in, enc_out, self_ok, cross_ok, get_self, get_cross)
    result_rows, grad_rows_dec, grad_rows_enc, grads = backward(
        dec_in, enc_out, self_ok, cross_ok, out_grad, kept, get_self, get_cross, get_ffn
    )
    gains = reduce_group((grads[0], grads[5], grads[10]), (gain_self, gain_cross, gain_ffn))
    wide = reduce_group(grads[11:13], (w_gate, w_up))
    thin = reduce_group(grads[1:5] + grads[6:10] + grads[13:14], narrow)
    return (
        (result_rows, grad_rows_dec, grad_rows_enc, gains[0])
        + tuple(thin[0:4])
        + (gains[1],)
        + tuple(thin[4:8])
        + (gains[2], *wide, thin[8])
    )


def solution(mesh):
    placed = (
        P(("dp", "fsdp"), None, None),
        P(("dp", "fsdp"), None, None),
        P(("dp", "fsdp"), None),
        P(("dp", "fsdp"), None),
        P(("dp", "fsdp"), None, None),
        P("fsdp"),
        P("fsdp", None),
        P("fsdp", None),
        P("fsdp", None),
        P("fsdp", None),
        P("fsdp"),
        P("fsdp", None),
        P("fsdp", None),
        P("fsdp", None),
        P("fsdp", None),
        P("fsdp"),
        P("fsdp", None),
        P("fsdp", None),
        P("fsdp", None),
    )
    return jax.shard_map(
        body,
        mesh=mesh,
        in_specs=placed,
        out_specs=(
            P(("dp", "fsdp"), None, None),
            P(("dp", "fsdp"), None, None),
            P(("dp", "fsdp"), None, None),
            P("fsdp"),
            P("fsdp", None),
            P("fsdp", None),
            P("fsdp", None),
            P("fsdp", None),
            P("fsdp"),
            P("fsdp", None),
            P("fsdp", None),
            P("fsdp", None),
            P("fsdp", None),
            P("fsdp"),
            P("fsdp", None),
            P("fsdp", None),
            P("fsdp", None),
        ),
        check_vma=False,
    )
```
